32 devices in a mesh: dp: 4 (over y, x), ctx: 8 (over z, core).
Axes of the slice: x: 2, y: 2, z: 4, core: 2. Of those that a mesh axis runs over, the one named last changes fastest.
Arguments:
- stream: bfloat16 [16, 4096, 1600], P('dp', 'ctx'), may hold values from -16 to 16
- segments: int32 [16, 4096], P('dp'), may hold values from 0 to 3, never falling along the last dimension, each value on 1 to 2000 neighbouring positions
- cotangent: bfloat16 [16, 4096, 1600], P('dp', 'ctx'), may hold values from -6 to 6
- gain_zero: bfloat16 [1600], P('dp'), may hold values from 0.099609375 to 1.8984375
- shift_zero: bfloat16 [1600], P('dp'), may hold values from -2.390625 to 2.390625
- weight_in: bfloat16 [1600, 800], P('dp'), may hold values from -0.21875 to 0.21875
- bias_in: bfloat16 [800], P('dp'), may hold values from -3 to 3
- gain_one: bfloat16 [800], P('dp'), may hold values from 0.099609375 to 1.8984375
- shift_one: bfloat16 [800], P('dp'), may hold values from -2.390625 to 2.390625
- weight_conv: bfloat16 [3, 800, 800], P(None, 'dp'), may hold values from -0.15625 to 0.15625
- bias_conv: bfloat16 [800], P('dp'), may hold values from -3 to 3
- gain_two: bfloat16 [800], P('dp'), may hold values from 0.099609375 to 1.8984375
- shift_two: bfloat16 [800], P('dp'), may hold values from -2.390625 to 2.390625
- weight_out: bfloat16 [800, 1600], P('dp'), may hold values from -0.3125 to 0.3125
- bias_out: bfloat16 [1600], P('dp'), may hold values from -3 to 3
Outputs:
- output: bfloat16 [16, 4096, 1600], P('dp', 'ctx')
- grad_stream: bfloat16 [16, 4096, 1600], P('dp', 'ctx')
- grad_gain_zero: float32 [1600], P('dp')
- grad_shift_zero: float32 [1600], P('dp')
- grad_weight_in: float32 [1600, 800], P('dp')
- grad_bias_in: float32 [800], P('dp')
- grad_gain_one: float32 [800], P('dp')
- grad_shift_one: float32 [800], P('dp')
- grad_weight_conv: float32 [3, 800, 800], P(None, 'dp')
- grad_bias_conv: float32 [800], P('dp')
- grad_gain_two: float32 [800], P('dp')
- grad_shift_two: float32 [800], P('dp')
- grad_weight_out: float32 [800, 1600], P('dp')
- grad_bias_out: float32 [1600], P('dp')
- rms_in: float32 [], replicated
- rms_out: float32 [], replicated
- rms_hidden_one: float32 [], replicated
- rms_hidden_two: float32 [], replicated
- rms_branch: float32 [], replicated
The draws below stay inside these ranges and needn't reach their ends.
All inputs are finite; a program needn't handle non-finite values.
Results may differ from the reference program's by a relative error of at most 0.0066.
Values may be sent and summed in bfloat16 or wider, within the bound.
No kernel may reach another device: no remote copies, remote signals or barrier semaphores. Data moves between devices by JAX's collectives and lax.ppermute only.
A program may use at most 256 MiB of HBM per device.

```python
import math
import jax
import jax.numpy as jnp
import numpy as np
from jax import lax

D = 800
WIDE = 1600
SEQS = 16
LENGTH = 4096
SEGS = 4
DOC_MOST = 2000


def draw_stream(key, part):
    seq_ids = jnp.arange(SEQS, dtype=jnp.float32)[:, None]
    positions = jnp.arange(LENGTH, dtype=jnp.float32)[None, :]
    place_share = (seq_ids * LENGTH + positions) / (SEQS * LENGTH)
    noise_part = jax.random.truncated_normal(key, -4.0, 4.0, (SEQS, LENGTH, WIDE), jnp.float32)
    row_scale = jnp.exp(jnp.log(3.0) * place_share)
    return (noise_part * row_scale[:, :, None]).astype(jnp.bfloat16)


def levels(rng, dims, split, smallest, largest):
    level = 1.0
    for position, shards_of in split:
        heights = jax.random.uniform(jax.random.fold_in(jax.random.fold_in(rng, 6), position), (shards_of,), jnp.float32, smallest / len(split), largest / len(split))
        level = level * jnp.repeat(jnp.exp(heights), dims[position] // shards_of).reshape((-1,) + (1,) * (len(dims) - 1 - position))
    return level


def profile(count, total, bound, slope):
    loads = [(1 << 20) // math.isqrt(standing ** slope) + 1 for standing in range(2, count + 1)]
    rest, holding = total - bound - (count - 1), [1] * (count - 1)
    while rest > 0:
        free = [i for i in range(count - 1) if holding[i] < bound]
        whole, left = sum([loads[i] for i in free]), rest
        for i in free:
            addition = min(bound - holding[i], max(1, left * loads[i] // whole), rest)
            holding[i] = holding[i] + addition
            rest = rest - addition
    return np.array([bound] + holding)


def ragged_sizes(key, amount, total, bound, slope):
    if amount == 2:
        one = jax.random.randint(key, (), max(1, total - bound), min(bound, total - 1) + 1)
        return jnp.stack([one, total - one])
    tallies = jnp.asarray(profile(amount, total, bound, slope), jnp.int32)
    pairs = (amount - 1) // 2
    giver, sink = tallies[1:1 + 2 * pairs:2], tallies[2:2 + 2 * pairs:2]
    slack = jnp.minimum(giver - 1, bound - sink)
    passed = jax.random.randint(jax.random.fold_in(key, 1), (pairs,), 0, 1 << 20) % (slack + 1)
    tallies = tallies.at[1:1 + 2 * pairs:2].set(giver - passed).at[2:2 + 2 * pairs:2].set(sink + passed)
    return tallies[jax.random.permutation(jax.random.fold_in(key, 2), amount)]


def gaussian(key, shape, deviation, most, cuts=(), held_as=jnp.bfloat16):
    level = levels(key, shape, cuts, -0.22, 0.18) if cuts else 1.0
    entries = jax.random.normal(key, shape, jnp.float32) * deviation * level
    return jnp.minimum(jnp.maximum(entries, -most), most).astype(held_as)


def setup_inputs(seed: int = 0) -> dict:
    key_list = jax.random.split(jax.random.key(seed), 16)
    return {
        "stream": draw_stream(jax.random.fold_in(key_list[15], 71), 0),
        "segments": jax.vmap(lambda own: jnp.searchsorted(jnp.cumsum(ragged_sizes(own, SEGS, LENGTH, DOC_MOST, 0)), jnp.arange(LENGTH), side="right"))(jax.random.split(key_list[1], SEQS)).reshape((SEQS, LENGTH)).astype(jnp.int32),
        "cotangent": gaussian(key_list[2], (SEQS, LENGTH, WIDE), 1.0, 6.0, ((0, 4), (1, 8))),
        "gain_zero": jnp.clip(1.0 + 0.18 * jax.random.normal(key_list[3], (WIDE,), jnp.float32), 0.099609375, 1.8984375).astype(jnp.bfloat16),
        "shift_zero": gaussian(key_list[4], (WIDE,), 0.4, 2.390625, ((0, 4),)),
        "weight_in": gaussian(key_list[5], (WIDE, D), (WIDE // 2) ** -0.5, 0.21875, ((0, 4),)),
        "bias_in": gaussian(key_list[6], (D,), 0.5, 3.0, ((0, 4),)),
        "gain_one": jnp.clip(1.0 + 0.18 * jax.random.normal(key_list[7], (D,), jnp.float32), 0.099609375, 1.8984375).astype(jnp.bfloat16),
        "shift_one": gaussian(key_list[8], (D,), 0.4, 2.390625, ((0, 4),)),
        "weight_conv": gaussian(key_list[9], (3, D, D), (2 * D) ** -0.5, 0.15625, ((1, 4),)),
        "bias_conv": gaussian(key_list[10], (D,), 0.5, 3.0, ((0, 4),)),
        "gain_two": jnp.clip(1.0 + 0.18 * jax.random.normal(key_list[11], (D,), jnp.float32), 0.099609375, 1.8984375).astype(jnp.bfloat16),
        "shift_two": gaussian(key_list[12], (D,), 0.4, 2.390625, ((0, 4),)),
        "weight_out": gaussian(key_list[13], (D, WIDE), (D // 2) ** -0.5, 0.3125, ((0, 4),)),
        "bias_out": gaussian(key_list[14], (WIDE,), 0.5, 3.0, ((0, 4),)),
    }


@jax.custom_vjp
def low(v):
    return lax.optimization_barrier(v.astype(jnp.bfloat16)).astype(jnp.float32)

@jax.custom_vjp
def low_back(v):
    return v

def low_keep(v):
    return (low(v), None)

def low_pass(kept, grad):
    return (grad,)

def back_keep(v):
    return (v, None)

def back_low(kept, grad):
    return (low(grad),)
low.defvjp(low_keep, low_pass)
low_back.defvjp(back_keep, back_low)

def smooth_act(values):
    return values * jax.nn.sigmoid(values)

def layer_norm(values, gain_vec, shift_vec):
    average = lax.optimization_barrier(jnp.mean(values, axis=-1, keepdims=True))
    centred = values - average
    variance = lax.optimization_barrier(jnp.mean(centred * centred, axis=-1, keepdims=True))
    return centred * lax.rsqrt(variance + 1e-05) * gain_vec + shift_vec

def wide_dot(left, right):
    return jnp.einsum('gld,de->gle', left, right, precision=lax.Precision.HIGHEST)

def conv_stack(activations, seg_ids):
    length = activations.shape[1]
    padded = jnp.pad(activations, ((0, 0), (4, 0), (0, 0)))
    seg_pad = jnp.pad(seg_ids, ((0, 0), (4, 0)), constant_values=-1)
    pieces = []
    for offset in range(3):
        first_row = 4 - 2 * offset
        matching = (seg_pad[:, first_row:first_row + length] == seg_ids).astype(activations.dtype)
        pieces.append(padded[:, first_row:first_row + length] * matching[:, :, None])
    return jnp.concatenate(pieces, axis=-1)

def branch(params, stream_f, seg_ids):
    gain_zero, shift_zero, weight_in, bias_in, gain_one, shift_one, weight_conv, bias_conv, gain_two, shift_two, weight_out, bias_out = params
    conv_width = weight_conv.shape[1]
    first_act = low(smooth_act(layer_norm(stream_f, gain_zero, shift_zero)))
    hidden_one = low_back(wide_dot(first_act, weight_in) + bias_in)
    second_act = low(smooth_act(layer_norm(hidden_one, gain_one, shift_one)))
    stacked = conv_stack(second_act, seg_ids)
    hidden_two = low_back(wide_dot(stacked, weight_conv.reshape(3 * conv_width, conv_width)) + bias_conv)
    third_act = low(smooth_act(layer_norm(hidden_two, gain_two, shift_two)))
    branch_out = wide_dot(third_act, weight_out) + bias_out
    squares = (jnp.sum(hidden_one * hidden_one), jnp.sum(hidden_two * hidden_two), jnp.sum(branch_out * branch_out))
    return (stream_f + branch_out, squares)

def reference(stream, segments, cotangent, gain_zero, shift_zero, weight_in, bias_in, gain_one, shift_one, weight_conv, bias_conv, gain_two, shift_two, weight_out, bias_out):
    params = tuple((entry.astype(jnp.float32) for entry in (gain_zero, shift_zero, weight_in, bias_in, gain_one, shift_one, weight_conv, bias_conv, gain_two, shift_two, weight_out, bias_out)))
    seq_count, length, wide_dim = stream.shape
    inner_dim = weight_conv.shape[1]
    group_size = math.gcd(seq_count, max(1, 4096 // length))
    group_count = seq_count // group_size

    def grouped(array):
        return array.reshape((group_count, group_size) + array.shape[1:])
    zero_grads = tuple((jnp.zeros(entry.shape, jnp.float32) for entry in params))
    zero_sum = jnp.zeros((), jnp.float32)
    start_carry = (zero_sum, zero_sum, zero_sum, zero_sum, zero_sum, zero_grads)

    def one_group(carry, inputs):
        stream_g, seg_g, cot_g = inputs
        stream_f = stream_g.astype(jnp.float32)

        def wrapped(params_in, stream_in):
            return branch(params_in, stream_in, seg_g)
        result, pullback, squares = jax.vjp(wrapped, params, stream_f, has_aux=True)
        grad_params, grad_in = pullback(cot_g.astype(jnp.float32))
        new_carry = (carry[0] + jnp.sum(stream_f * stream_f), carry[1] + jnp.sum(result * result), carry[2] + squares[0], carry[3] + squares[1], carry[4] + squares[2], jax.tree.map(jnp.add, carry[5], grad_params))
        return (new_carry, (result.astype(jnp.bfloat16), grad_in.astype(jnp.bfloat16)))
    final, (outputs, grads_in) = lax.scan(one_group, start_carry, (grouped(stream), grouped(segments), grouped(cotangent)))
    total = float(seq_count * length * wide_dim)
    total_inner = float(seq_count * length * inner_dim)
    rms_in = jnp.sqrt(final[0] / total)
    rms_out = jnp.sqrt(final[1] / total)
    rms_hidden_one = jnp.sqrt(final[2] / total_inner)
    rms_hidden_two = jnp.sqrt(final[3] / total_inner)
    rms_branch = jnp.sqrt(final[4] / total)
    grads = final[5]
    return (outputs.reshape(stream.shape), grads_in.reshape(stream.shape), grads[0], grads[1], grads[2], grads[3], grads[4], grads[5], grads[6], grads[7], grads[8], grads[9], grads[10], grads[11], rms_in, rms_out, rms_hidden_one, rms_hidden_two, rms_branch)
```

```python
import jax
import jax.numpy as jnp
from jax import lax
from jax.experimental import pallas as pl
from jax.experimental.pallas import tpu as pltpu
from jax.sharding import PartitionSpec as P

F32 = jnp.float32
BF = jnp.bfloat16
EPS = 1e-05
ROWS = 16
NN = (((1,), (0,)), ((), ()))
NT = (((1,), (1,)), ((), ()))
MIB = 1024 * 1024


def by_core(value, even_mask, odd_mask):
    n_dp, n_ctx = lax.axis_size("dp"), lax.axis_size("ctx")
    masks = (even_mask, odd_mask)
    pairs = [
        (d * n_ctx + t, (d ^ masks[t % 2]) * n_ctx + t) for d in range(n_dp) for t in range(n_ctx)
    ]
    return lax.ppermute(value, ("dp", "ctx"), pairs)


def swap(value, axis, mask):
    return lax.ppermute(value, axis, [(i, i ^ mask) for i in range(lax.axis_size(axis))])


def shifted(value, by):
    size = lax.axis_size("ctx")
    return lax.ppermute(value, "ctx", [(i, i + by) for i in range(size) if 0 <= i + by < size])


def half_of(rows):
    off = rows // 2 // 16 * 16
    return off, rows - off


def gather_pieces(shard, row_dim, core):
    off, size = half_of(shard.shape[row_dim])
    own_half = lax.dynamic_slice_in_dim(shard, core * off, size, row_dim)
    first = by_core(own_half, 1, 2)
    second = by_core(jnp.stack([own_half, first]), 2, 1)
    other_first = swap(first, "ctx", 1)
    other_second = swap(second, "ctx", 1)
    return shard, first, second, other_first, other_second


def sum_shards(keep, send):
    from_core = swap(send, "ctx", 1).astype(F32)
    one = by_core((keep[2:4] + from_core[2:4]).astype(BF), 1, 2).astype(F32)
    two = by_core((keep[1] + from_core[1] + one[1]).astype(BF), 2, 1).astype(F32)
    part = keep[0] + from_core[0] + one[0] + two
    mask = 2
    while mask < lax.axis_size("ctx"):
        part = part.astype(BF)
        part = part.astype(F32) + swap(part, "ctx", mask).astype(F32)
        mask *= 2
    return part, swap(part, "ctx", 1)


def join_halves(mine, other, rows, row_dim, core):
    off, size = half_of(rows)
    low = jnp.where(core == 0, mine, other)
    high = jnp.where(core == 0, other, mine)
    return jnp.concatenate(
        [low, lax.slice_in_dim(high, size - off, size, axis=row_dim)], axis=row_dim
    )


def sum_all(value):
    value = value + swap(value, "ctx", 1)
    value = value + swap(value, "dp", 1)
    value = value + swap(value, "dp", 2)
    mask = 2
    while mask < lax.axis_size("ctx"):
        value = value + swap(value, "ctx", mask)
        mask *= 2
    return value


def mm(left, right, dims=NN):
    return lax.dot_general(left, right, dims, preferred_element_type=F32)


def sig(z):
    return 0.5 * jnp.tanh(0.5 * z) + 0.5


def loop(count, body, unroll):
    lax.fori_loop(0, count, lambda i, _: (body(i), 0)[1], 0, unroll=unroll)


def full(shape):
    return pl.BlockSpec(shape, lambda s: (0,) * len(shape), pipeline_mode=pl.Buffered(1))


def seq(shape):
    return pl.BlockSpec((None,) + shape, lambda s: (s,) + (0,) * len(shape))


ANY = pl.BlockSpec(memory_space=pl.ANY)


def sds(shape, dtype):
    return jax.ShapeDtypeStruct(shape, dtype)


def rows_at(i, base=0):
    return pl.ds(pl.multiple_of(i * ROWS + base, ROWS), ROWS)


def lanes(tile, width):
    return jnp.concatenate([tile] * (width // 128), axis=1)


def col(ref, j, r, width):
    return lanes(ref[j, r, :], width)


def fold(v):
    t = v[:, 0:128]
    for j in range(1, v.shape[1] // 128):
        t = t + v[:, j * 128 : (j + 1) * 128]
    return t


def eight(v):
    return v[0:8] + v[8:16]


def spread(vec_ref, out_ref, j, row):
    v = vec_ref[row : row + 1, :]
    out_ref[j] = jnp.broadcast_to(v, (128, v.shape[1])).T


def gathered_row(sums):
    return jnp.sum(sums.T, axis=0, keepdims=True)


def row_stats(count, load, width, length):
    def total(i, a):
        return a + eight(load(i))

    zero = jnp.zeros((8, length), F32)
    a = lax.fori_loop(0, count, total, zero, unroll=5)
    mean = jnp.sum(a, axis=0, keepdims=True) * (1.0 / width)

    def squares(i, a):
        c = load(i) - mean
        return a + eight(c * c)

    a = lax.fori_loop(0, count, squares, zero, unroll=5)
    var = jnp.sum(a, axis=0, keepdims=True) * (1.0 / width)
    return mean, var


def start_load(pieces, dst, sems):
    shard, first, second, other_first, other_second = pieces
    rows = shard.shape[0]
    off, size = half_of(rows)
    me, core = lax.axis_index("dp"), lax.rem(lax.axis_index("ctx"), 2)
    near = jnp.bitwise_xor(me, 1 + core)
    far = jnp.bitwise_xor(me, 2 - core)
    both = jnp.bitwise_xor(me, 3)

    def at(device, half, count):
        return dst.at[pl.ds(pl.multiple_of(device * rows + half * off, 16), count), :]

    batch_one = [
        (shard, at(me, 0, rows)),
        (first, at(near, core, size)),
        (second.at[0], at(far, core, size)),
        (second.at[1], at(both, core, size)),
    ]
    batch_two = [
        (other_first, at(far, 1 - core, size)),
        (other_second.at[0], at(near, 1 - core, size)),
        (other_second.at[1], at(both, 1 - core, size)),
    ]
    copies = [
        pltpu.make_async_copy(src, to, sems.at[i])
        for i, (src, to) in enumerate(batch_one + batch_two)
    ]
    for c in copies[:4]:
        c.start()
    return copies


def finish_load(copies):
    for c in copies[:4]:
        c.wait()
    for c in copies[4:]:
        c.start()
    for c in copies[4:]:
        c.wait()


def assemble(pieces, wide_s):
    shard, first, second, other_first, other_second = pieces
    rows = shard.shape[0]
    off, size = half_of(rows)
    me, core = lax.axis_index("dp"), lax.rem(lax.axis_index("ctx"), 2)
    near = jnp.bitwise_xor(me, 1 + core)
    far = jnp.bitwise_xor(me, 2 - core)
    both = jnp.bitwise_xor(me, 3)

    def put(device, half, piece):
        start = pl.ds(pl.multiple_of(device * rows + half * off, 8), piece.shape[0])
        wide_s[start, :] = piece.astype(F32)

    put(me, 0, shard[...])
    put(near, core, first[...])
    put(far, core, second[0])
    put(both, core, second[1])
    put(far, 1 - core, other_first[...])
    put(near, 1 - core, other_second[0])
    put(both, 1 - core, other_second[1])
    return wide_s[...].astype(BF)


def params(mib):
    return pltpu.CompilerParams(vmem_limit_bytes=mib * MIB)


def split_grad(acc_ref, keep_ref, send_ref, lead):
    me, core = lax.axis_index("dp"), lax.rem(lax.axis_index("ctx"), 2)
    rows = acc_ref.shape[lead] // 4
    off, size = half_of(rows)
    mine = (0, 2 - core, 1 + core, 3)
    theirs = (0, 1 + core, 2 - core, 3)
    for j in range(4):
        a = pl.ds(pl.multiple_of(jnp.bitwise_xor(me, mine[j]) * rows + core * off, 8), size)
        b = pl.ds(pl.multiple_of(jnp.bitwise_xor(me, theirs[j]) * rows + (1 - core) * off, 8), size)
        if lead:
            for k in range(acc_ref.shape[0]):
                keep_ref[j, k] = acc_ref[k, a, :]
                send_ref[j, k] = acc_ref[k, b, :].astype(BF)
        else:
            keep_ref[j] = acc_ref[a, :]
            send_ref[j] = acc_ref[b, :].astype(BF)


def first_body(
    x_ref, p0, p1, p2, p3, p4, vw_ref, vi_ref,
    a0_ref, h1_ref, a1_ref, edge_ref, sq_ref,
    w_s, wt_s, vw_s, vi_s, sems,
):
    s = pl.program_id(0)
    wide, length = x_ref.shape
    inner = h1_ref.shape[0]

    @pl.when(s == 0)
    def _():
        copies = start_load((p0, p1, p2, p3, p4), w_s, sems)
        sq_ref[...] = jnp.zeros_like(sq_ref)
        for j in range(2):
            spread(vw_ref, vw_s, j, j)
        for j in range(3):
            spread(vi_ref, vi_s, j, j)
        finish_load(copies)
        wt_s[...] = w_s[...].T

    mean, var = row_stats(wide // ROWS, lambda i: x_ref[rows_at(i), :].astype(F32), wide, length)
    inv = lax.rsqrt(var + EPS)
    sq_ref[0:1, :] += (var + mean * mean) * float(wide)

    def act0(i):
        r = rows_at(i)
        z = (x_ref[r, :].astype(F32) - mean) * inv * col(vw_s, 0, r, length)
        z = z + col(vw_s, 1, r, length)
        a0_ref[r, :] = (z * sig(z)).astype(BF)

    loop(wide // ROWS, act0, 5)
    h1_ref[...] = mm(wt_s[...], a0_ref[...]) + lanes(vi_s[0], length)
    mean1, var1 = row_stats(inner // ROWS, lambda i: h1_ref[rows_at(i), :], inner, length)
    inv1 = lax.rsqrt(var1 + EPS)
    sq_ref[1:2, :] += (var1 + mean1 * mean1) * float(inner)

    def act1(i):
        r = rows_at(i)
        z = (h1_ref[r, :] - mean1) * inv1 * col(vi_s, 1, r, length) + col(vi_s, 2, r, length)
        a1_ref[r, :] = (z * sig(z)).astype(BF)

    loop(inner // ROWS, act1, 5)
    edge_ref[...] = a1_ref[:, length - 128 :].astype(F32).T[120:128, :].astype(BF)


def first(x, pieces, vw, vi):
    seqs, wide, length = x.shape
    inner = pieces[0].shape[1]
    return pl.pallas_call(
        first_body,
        grid=(seqs,),
        in_specs=[seq((wide, length))] + [ANY] * 5 + [full(vw.shape), full(vi.shape)],
        out_specs=[
            seq((wide, length)),
            seq((inner, length)),
            seq((inner, length)),
            seq((8, inner)),
            full((8, length)),
        ],
        out_shape=[
            sds((seqs, wide, length), BF),
            sds((seqs, inner, length), F32),
            sds((seqs, inner, length), BF),
            sds((seqs, 8, inner), BF),
            sds((8, length), F32),
        ],
        scratch_shapes=[
            pltpu.VMEM((wide, inner), BF),
            pltpu.VMEM((inner, wide), BF),
            pltpu.VMEM((2, wide, 128), F32),
            pltpu.VMEM((3, inner, 128), F32),
            pltpu.SemaphoreType.DMA((7,)),
        ],
        compiler_params=params(40),
        name="norm_and_first_product",
    )(x, *pieces, vw, vi)


def conv_body(
    a1_ref, halo_ref, dy_ref, mk_ref, c0, c1, c2, c3, c4, o0, o1, o2, o3, o4, vi_ref,
    a2_ref, dh2_ref, edge_ref, sums_ref, bo_ref, sq_ref, wc_ref, wot_ref,
    wct_s, wo_s, st_s, h_s, d_s, hl_s, vi_s, sums_s, bo_s, tap_s, out_s,
):
    s = pl.program_id(0)
    inner, length = a1_ref.shape
    wide = dy_ref.shape[0]
    steps = inner // ROWS

    @pl.when(s == 0)
    def _():
        sq_ref[...] = jnp.zeros_like(sq_ref)
        sums_s[...] = jnp.zeros_like(sums_s)
        bo_s[...] = jnp.zeros_like(bo_s)
        for j in range(3):
            spread(vi_ref, vi_s, j, j + 3)
        for k in range(3):
            wc_ref[k] = assemble(
                (c0.at[k], c1.at[k], c2.at[:, k], c3.at[k], c4.at[:, k]), tap_s
            )
        wct_s[...] = wc_ref[...].reshape(3 * inner, inner).T
        wo_s[...] = assemble((o0, o1, o2, o3, o4), out_s)
        wot_ref[...] = wo_s[...].T

    hl_s[...] = jnp.concatenate(
        [jnp.zeros((120, inner), F32), halo_ref[...].astype(F32)], axis=0
    ).T
    m1 = mk_ref[1:2, :]
    m2 = mk_ref[2:3, :]

    def build(i):
        r = rows_at(i)
        b = a1_ref[r, :]
        v = jnp.concatenate([b.astype(F32), hl_s[r, :]], axis=1)
        st_s[r, :] = b
        st_s[rows_at(i, inner), :] = (pltpu.roll(v, 2, 1)[:, 0:length] * m1).astype(BF)
        st_s[rows_at(i, 2 * inner), :] = (pltpu.roll(v, 4, 1)[:, 0:length] * m2).astype(BF)

    loop(steps, build, 2)
    h_s[...] = mm(wct_s[...], st_s[...]) + lanes(vi_s[0], length)
    d_s[...] = mm(wo_s[...], dy_ref[...])
    mean, var = row_stats(steps, lambda i: h_s[rows_at(i), :], inner, length)
    inv = lax.rsqrt(var + EPS)
    sq_ref[0:1, :] += (var + mean * mean) * float(inner)

    def back(i, acc):
        r = rows_at(i)
        n = (h_s[r, :] - mean) * inv
        g = col(vi_s, 1, r, length)
        z = n * g + col(vi_s, 2, r, length)
        sg = sig(z)
        zs = z * sg
        a2_ref[r, :] = zs.astype(BF)
        e = d_s[r, :] * (sg + zs * (1.0 - sg))
        q = e * g
        d_s[r, :] = q
        h_s[r, :] = n
        sums_s[0, r, :] += fold(e * n)
        sums_s[1, r, :] += fold(e)
        return acc[0] + eight(q), acc[1] + eight(q * n)

    zero = jnp.zeros((8, length), F32)
    qa, qn = lax.fori_loop(0, steps, back, (zero, zero), unroll=2)
    mq = jnp.sum(qa, axis=0, keepdims=True) * (1.0 / inner)
    mqn = jnp.sum(qn, axis=0, keepdims=True) * (1.0 / inner)

    def last(i):
        r = rows_at(i)
        dh = ((d_s[r, :] - mq - h_s[r, :] * mqn) * inv).astype(BF)
        dh2_ref[r, :] = dh
        sums_s[2, r, :] += fold(dh.astype(F32))

    loop(steps, last, 5)

    def bias(i):
        r = rows_at(i)
        bo_s[r, :] += fold(dy_ref[r, :].astype(F32))

    loop(wide // ROWS, bias, 5)
    edge_ref[...] = dh2_ref[:, 0:128].astype(F32).T[0:8, :].astype(BF)

    @pl.when(s == pl.num_programs(0) - 1)
    def _():
        for j in range(3):
            sums_ref[j : j + 1, :] = gathered_row(sums_s[j])
        bo_ref[0:1, :] = gathered_row(bo_s[...])


def conv(a1, halo, dy, mk, pc, po, vi):
    seqs, inner, length = a1.shape
    wide = dy.shape[1]
    return pl.pallas_call(
        conv_body,
        grid=(seqs,),
        in_specs=[seq((inner, length)), seq((8, inner)), seq((wide, length)), seq((8, length))]
        + [full(p.shape) for p in pc + po]
        + [full(vi.shape)],
        out_specs=[
            seq((inner, length)),
            seq((inner, length)),
            seq((8, inner)),
            full((8, inner)),
            full((8, wide)),
            full((8, length)),
            full((3, inner, inner)),
            full((wide, inner)),
        ],
        out_shape=[
            sds((seqs, inner, length), BF),
            sds((seqs, inner, length), BF),
            sds((seqs, 8, inner), BF),
            sds((8, inner), F32),
            sds((8, wide), F32),
            sds((8, length), F32),
            sds((3, inner, inner), BF),
            sds((wide, inner), BF),
        ],
        scratch_shapes=[
            pltpu.VMEM((inner, 3 * inner), BF),
            pltpu.VMEM((inner, wide), BF),
            pltpu.VMEM((3 * inner, length), BF),
            pltpu.VMEM((inner, length), F32),
            pltpu.VMEM((inner, length), F32),
            pltpu.VMEM((inner, 128), F32),
            pltpu.VMEM((3, inner, 128), F32),
            pltpu.VMEM((3, inner, 128), F32),
            pltpu.VMEM((wide, 128), F32),
            pltpu.VMEM((inner, inner), F32),
            pltpu.VMEM((inner, wide), F32),
        ],
        compiler_params=params(56),
        name="conv_and_third_norm",
    )(a1, halo, dy, mk, *pc, *po, vi)


def grad_body(a_ref, b_ref, keep_ref, send_ref, acc_s):
    s = pl.program_id(0)

    @pl.when(s == 0)
    def _():
        acc_s[...] = mm(a_ref[...], b_ref[...], NT)

    @pl.when(s > 0)
    def _():
        acc_s[...] += mm(a_ref[...], b_ref[...], NT)

    @pl.when(s == pl.num_programs(0) - 1)
    def _():
        split_grad(acc_s, keep_ref, send_ref, 0)


def grad(a, b, name):
    seqs, m, length = a.shape
    n = b.shape[1]
    size = half_of(m // 4)[1]
    return pl.pallas_call(
        grad_body,
        grid=(seqs,),
        in_specs=[seq((m, length)), seq((n, length))],
        out_specs=[full((4, size, n)), full((4, size, n))],
        out_shape=[sds((4, size, n), F32), sds((4, size, n), BF)],
        scratch_shapes=[pltpu.VMEM((m, n), F32)],
        compiler_params=params(32),
        name=name,
    )(a, b)


def shift_back(dh2_ref, halo_ref, mk_ref, hl_s, t_s):
    inner, length = dh2_ref.shape
    hl_s[...] = jnp.concatenate(
        [halo_ref[...].astype(F32), jnp.zeros((120, inner), F32)], axis=0
    ).T
    f1 = mk_ref[3:4, :]
    f2 = mk_ref[4:5, :]

    def build(i):
        r = rows_at(i)
        v = jnp.concatenate([dh2_ref[r, :].astype(F32), hl_s[r, :]], axis=1)
        t_s[0, r, :] = (pltpu.roll(v, length + 126, 1)[:, 0:length] * f1).astype(BF)
        t_s[1, r, :] = (pltpu.roll(v, length + 124, 1)[:, 0:length] * f2).astype(BF)

    loop(inner // ROWS, build, 2)


def grad_conv_body(a1_ref, dh2_ref, halo_ref, mk_ref, keep_ref, send_ref, acc_s, t_s, hl_s):
    s = pl.program_id(0)
    shift_back(dh2_ref, halo_ref, mk_ref, hl_s, t_s)

    @pl.when(s == 0)
    def _():
        acc_s[0] = mm(a1_ref[...], dh2_ref[...], NT)
        for k in (1, 2):
            acc_s[k] = mm(a1_ref[...], t_s[k - 1], NT)

    @pl.when(s > 0)
    def _():
        acc_s[0] += mm(a1_ref[...], dh2_ref[...], NT)
        for k in (1, 2):
            acc_s[k] += mm(a1_ref[...], t_s[k - 1], NT)

    @pl.when(s == pl.num_programs(0) - 1)
    def _():
        split_grad(acc_s, keep_ref, send_ref, 1)


def grad_conv(a1, dh2, halo, mk):
    seqs, inner, length = a1.shape
    size = half_of(inner // 4)[1]
    return pl.pallas_call(
        grad_conv_body,
        grid=(seqs,),
        in_specs=[
            seq((inner, length)),
            seq((inner, length)),
            seq((8, inner)),
            seq((8, length)),
        ],
        out_specs=[full((4, 3, size, inner)), full((4, 3, size, inner))],
        out_shape=[sds((4, 3, size, inner), F32), sds((4, 3, size, inner), BF)],
        scratch_shapes=[
            pltpu.VMEM((3, inner, inner), F32),
            pltpu.VMEM((2, inner, length), BF),
            pltpu.VMEM((inner, 128), F32),
        ],
        compiler_params=params(40),
        name="grad_weight_conv",
    )(a1, dh2, halo, mk)


def conv_back_body(
    dh2_ref, halo_ref, h1_ref, mk_ref, wc_ref, vi_ref,
    dh1_ref, sums_ref,
    t_s, d_s, n_s, hl_s, vi_s, sums_s,
):
    s = pl.program_id(0)
    inner, length = dh2_ref.shape
    steps = inner // ROWS

    @pl.when(s == 0)
    def _():
        sums_s[...] = jnp.zeros_like(sums_s)
        for j in range(2):
            spread(vi_ref, vi_s, j, j + 1)

    shift_back(dh2_ref, halo_ref, mk_ref, hl_s, t_s)
    d_s[...] = mm(wc_ref[0], dh2_ref[...]) + mm(wc_ref[1], t_s[0]) + mm(wc_ref[2], t_s[1])
    mean, var = row_stats(steps, lambda i: h1_ref[rows_at(i), :], inner, length)
    inv = lax.rsqrt(var + EPS)

    def back(i, acc):
        r = rows_at(i)
        n = (h1_ref[r, :] - mean) * inv
        g = col(vi_s, 0, r, length)
        z = n * g + col(vi_s, 1, r, length)
        sg = sig(z)
        e = d_s[r, :] * (sg + z * sg * (1.0 - sg))
        q = e * g
        d_s[r, :] = q
        n_s[r, :] = n
        sums_s[0, r, :] += fold(e * n)
        sums_s[1, r, :] += fold(e)
        return acc[0] + eight(q), acc[1] + eight(q * n)

    zero = jnp.zeros((8, length), F32)
    qa, qn = lax.fori_loop(0, steps, back, (zero, zero), unroll=2)
    mq = jnp.sum(qa, axis=0, keepdims=True) * (1.0 / inner)
    mqn = jnp.sum(qn, axis=0, keepdims=True) * (1.0 / inner)

    def last(i):
        r = rows_at(i)
        dh = ((d_s[r, :] - mq - n_s[r, :] * mqn) * inv).astype(BF)
        dh1_ref[r, :] = dh
        sums_s[2, r, :] += fold(dh.astype(F32))

    loop(steps, last, 5)

    @pl.when(s == pl.num_programs(0) - 1)
    def _():
        for j in range(3):
            sums_ref[j : j + 1, :] = gathered_row(sums_s[j])


def conv_back(dh2, halo, h1, mk, wc, vi):
    seqs, inner, length = dh2.shape
    return pl.pallas_call(
        conv_back_body,
        grid=(seqs,),
        in_specs=[
            seq((inner, length)),
            seq((8, inner)),
            seq((inner, length)),
            seq((8, length)),
            full(wc.shape),
            full(vi.shape),
        ],
        out_specs=[seq((inner, length)), full((8, inner))],
        out_shape=[sds((seqs, inner, length), BF), sds((8, inner), F32)],
        scratch_shapes=[
            pltpu.VMEM((2, inner, length), BF),
            pltpu.VMEM((inner, length), F32),
            pltpu.VMEM((inner, length), F32),
            pltpu.VMEM((inner, 128), F32),
            pltpu.VMEM((2, inner, 128), F32),
            pltpu.VMEM((3, inner, 128), F32),
        ],
        compiler_params=params(32),
        name="conv_backward",
    )(dh2, halo, h1, mk, wc, vi)


def stream_body(
    x_ref, dy_ref, dh1_ref, p0, p1, p2, p3, p4, vw_ref,
    gs_ref, sums_ref,
    w_s, d_s, n_s, vw_s, sums_s, sems,
):
    s = pl.program_id(0)
    wide, length = x_ref.shape
    steps = wide // ROWS

    @pl.when(s == 0)
    def _():
        copies = start_load((p0, p1, p2, p3, p4), w_s, sems)
        sums_s[...] = jnp.zeros_like(sums_s)
        for j in range(2):
            spread(vw_ref, vw_s, j, j)
        finish_load(copies)

    d_s[...] = mm(w_s[...], dh1_ref[...])
    mean, var = row_stats(steps, lambda i: x_ref[rows_at(i), :].astype(F32), wide, length)
    inv = lax.rsqrt(var + EPS)

    def back(i, acc):
        r = rows_at(i)
        n = (x_ref[r, :].astype(F32) - mean) * inv
        g = col(vw_s, 0, r, length)
        z = n * g + col(vw_s, 1, r, length)
        sg = sig(z)
        e = d_s[r, :] * (sg + z * sg * (1.0 - sg))
        q = e * g
        d_s[r, :] = q
        n_s[r, :] = n
        sums_s[0, r, :] += fold(e * n)
        sums_s[1, r, :] += fold(e)
        return acc[0] + eight(q), acc[1] + eight(q * n)

    zero = jnp.zeros((8, length), F32)
    qa, qn = lax.fori_loop(0, steps, back, (zero, zero), unroll=2)
    mq = jnp.sum(qa, axis=0, keepdims=True) * (1.0 / wide)
    mqn = jnp.sum(qn, axis=0, keepdims=True) * (1.0 / wide)

    def last(i):
        r = rows_at(i)
        gs = dy_ref[r, :].astype(F32) + (d_s[r, :] - mq - n_s[r, :] * mqn) * inv
        gs_ref[r, :] = gs.astype(BF)

    loop(steps, last, 5)

    @pl.when(s == pl.num_programs(0) - 1)
    def _():
        for j in range(2):
            sums_ref[j : j + 1, :] = gathered_row(sums_s[j])


def stream_back(x, dy, dh1, pieces, vw):
    seqs, wide, length = x.shape
    inner = dh1.shape[1]
    return pl.pallas_call(
        stream_body,
        grid=(seqs,),
        in_specs=[seq((wide, length)), seq((wide, length)), seq((inner, length))]
        + [ANY] * 5
        + [full(vw.shape)],
        out_specs=[seq((wide, length)), full((8, wide))],
        out_shape=[sds((seqs, wide, length), BF), sds((8, wide), F32)],
        scratch_shapes=[
            pltpu.VMEM((wide, inner), BF),
            pltpu.VMEM((wide, length), F32),
            pltpu.VMEM((wide, length), F32),
            pltpu.VMEM((2, wide, 128), F32),
            pltpu.VMEM((2, wide, 128), F32),
            pltpu.SemaphoreType.DMA((7,)),
        ],
        compiler_params=params(40),
        name="grad_stream",
    )(x, dy, dh1, *pieces, vw)


def output_body(x_ref, a2_ref, wt_ref, vw_ref, out_ref, sq_ref, o_s, vw_s):
    s = pl.program_id(0)
    wide, length = x_ref.shape

    @pl.when(s == 0)
    def _():
        sq_ref[...] = jnp.zeros_like(sq_ref)
        spread(vw_ref, vw_s, 0, 2)

    o_s[...] = mm(wt_ref[...], a2_ref[...])

    def close(i, acc):
        r = rows_at(i)
        branch = o_s[r, :] + col(vw_s, 0, r, length)
        result = x_ref[r, :].astype(F32) + branch
        out_ref[r, :] = result.astype(BF)
        return acc[0] + eight(branch * branch), acc[1] + eight(result * result)

    zero = jnp.zeros((8, length), F32)
    b2, r2 = lax.fori_loop(0, wide // ROWS, close, (zero, zero), unroll=5)
    sq_ref[0:1, :] += jnp.sum(b2, axis=0, keepdims=True)
    sq_ref[1:2, :] += jnp.sum(r2, axis=0, keepdims=True)


def output_of(x, a2, wt, vw):
    seqs, wide, length = x.shape
    inner = a2.shape[1]
    return pl.pallas_call(
        output_body,
        grid=(seqs,),
        in_specs=[seq((wide, length)), seq((inner, length)), full(wt.shape), full(vw.shape)],
        out_specs=[seq((wide, length)), full((8, length))],
        out_shape=[sds((seqs, wide, length), BF), sds((8, length), F32)],
        scratch_shapes=[
            pltpu.VMEM((wide, length), F32),
            pltpu.VMEM((1, wide, 128), F32),
        ],
        compiler_params=params(32),
        name="block_output",
    )(x, a2, wt, vw)


def local(
    stream, segments, cotangent, gain_zero, shift_zero, weight_in, bias_in, gain_one, shift_one,
    weight_conv, bias_conv, gain_two, shift_two, weight_out, bias_out,
):
    n_dp, n_ctx = lax.axis_size("dp"), lax.axis_size("ctx")
    assert n_dp == 4 and n_ctx & (n_ctx - 1) == 0
    me, place = lax.axis_index("dp"), lax.axis_index("ctx")
    core = place % 2
    seqs, length, wide = stream.shape
    inner = weight_conv.shape[2]
    part_w, part_i = gain_zero.shape[0], bias_in.shape[0]

    small = jnp.concatenate(
        [gain_zero, shift_zero, bias_out, bias_in, gain_one, shift_one, bias_conv, gain_two, shift_two]
    )
    piece_in = gather_pieces(weight_in, 0, core)
    near = swap(small, "dp", 1)
    pair = jnp.where(me % 2 == 0, jnp.stack([small, near]), jnp.stack([near, small]))
    far = swap(pair, "dp", 2)
    vectors = jnp.where(me < 2, jnp.concatenate([pair, far]), jnp.concatenate([far, pair]))
    vectors = vectors.astype(F32)
    vw = jnp.stack([vectors[:, j * part_w : (j + 1) * part_w].reshape(wide) for j in range(3)])
    base = 3 * part_w
    vi = jnp.stack(
        [vectors[:, base + j * part_i : base + (j + 1) * part_i].reshape(inner) for j in range(6)]
    )
    piece_conv = gather_pieces(weight_conv, 1, core)
    piece_out = gather_pieces(weight_out, 0, core)

    padded = jnp.pad(segments, ((0, 0), (4, 4)), constant_values=-1)
    near_segs = lax.dynamic_slice_in_dim(padded, place * length, length + 8, 1)
    own = near_segs[:, 4 : 4 + length]
    same = [(near_segs[:, 4 + j : 4 + j + length] == own).astype(F32) for j in (0, -2, -4, 2, 4)]
    masks = jnp.stack(same + same[:3], axis=1)

    x = jnp.swapaxes(stream, 1, 2)
    dy = jnp.swapaxes(cotangent, 1, 2)

    act_zero, hidden_one, act_one, edge, sq_one = first(x, piece_in, vw, vi)
    halo = shifted(edge, 1)
    act_two, d_hidden_two, edge_back, sums_two, sum_bo, sq_two, full_conv, full_out_t = conv(
        act_one, halo, dy, masks, piece_conv, piece_out, vi
    )
    halo_back = shifted(edge_back, -1)
    keep_out, send_out = grad(act_two, dy, "grad_weight_out")
    keep_conv, send_conv = grad_conv(act_one, d_hidden_two, halo_back, masks)
    d_hidden_one, sums_one = conv_back(d_hidden_two, halo_back, hidden_one, masks, full_conv, vi)
    keep_in, send_in = grad(act_zero, d_hidden_one, "grad_weight_in")
    grad_x, sums_zero = stream_back(x, dy, d_hidden_one, piece_in, vw)
    output, sq_out = output_of(x, act_two, full_out_t, vw)

    sum_out = sum_shards(keep_out, send_out)
    sum_conv = sum_shards(keep_conv, send_conv)
    sum_in = sum_shards(keep_in, send_in)
    grad_weight_out = join_halves(*sum_out, part_i, 0, core)
    grad_weight_conv = join_halves(*sum_conv, part_i, 1, core)
    grad_weight_in = join_halves(*sum_in, part_w, 0, core)

    def padded_scalars(values):
        return jnp.pad(jnp.stack(values), (0, 128 - len(values)))

    early = sum_all(
        jnp.concatenate(
            [
                sum_bo[0],
                sums_one[0:3].reshape(-1),
                sums_two[0:3].reshape(-1),
                padded_scalars([jnp.sum(sq_one[0]), jnp.sum(sq_one[1]), jnp.sum(sq_two[0])]),
            ]
        )
    )
    late = sum_all(
        jnp.concatenate(
            [
                sums_zero[0:2].reshape(-1),
                padded_scalars([jnp.sum(sq_out[0]), jnp.sum(sq_out[1])]),
            ]
        )
    )

    def part(values, begin, size):
        return lax.dynamic_slice_in_dim(values, begin + me * size, size)

    at = wide
    grad_gain_one = part(early, at, part_i)
    grad_shift_one = part(early, at + inner, part_i)
    grad_bias_in = part(early, at + 2 * inner, part_i)
    grad_gain_two = part(early, at + 3 * inner, part_i)
    grad_shift_two = part(early, at + 4 * inner, part_i)
    grad_bias_conv = part(early, at + 5 * inner, part_i)
    grad_bias_out = part(early, 0, part_w)
    grad_gain_zero = part(late, 0, part_w)
    grad_shift_zero = part(late, wide, part_w)
    count = float(seqs * length * n_dp * n_ctx)
    sq_at = at + 6 * inner
    rms_in = jnp.sqrt(early[sq_at] / (count * wide))
    rms_hidden_one = jnp.sqrt(early[sq_at + 1] / (count * inner))
    rms_hidden_two = jnp.sqrt(early[sq_at + 2] / (count * inner))
    rms_branch = jnp.sqrt(late[2 * wide] / (count * wide))
    rms_out = jnp.sqrt(late[2 * wide + 1] / (count * wide))
    return (
        jnp.swapaxes(output, 1, 2),
        jnp.swapaxes(grad_x, 1, 2),
        grad_gain_zero,
        grad_shift_zero,
        grad_weight_in,
        grad_bias_in,
        grad_gain_one,
        grad_shift_one,
        grad_weight_conv,
        grad_bias_conv,
        grad_gain_two,
        grad_shift_two,
        grad_weight_out,
        grad_bias_out,
        rms_in,
        rms_out,
        rms_hidden_one,
        rms_hidden_two,
        rms_branch,
    )


def solution(mesh):
    placed = (
        P("dp", "ctx", None),
        P("dp", None),
        P("dp", "ctx", None),
        P("dp"),
        P("dp"),
        P("dp", None),
        P("dp"),
        P("dp"),
        P("dp"),
        P(None, "dp", None),
        P("dp"),
        P("dp"),
        P("dp"),
        P("dp", None),
        P("dp"),
    )
    return jax.shard_map(
        local,
        mesh=mesh,
        in_specs=placed,
        out_specs=(
            P("dp", "ctx", None),
            P("dp", "ctx", None),
            P("dp"),
            P("dp"),
            P("dp", None),
            P("dp"),
            P("dp"),
            P("dp"),
            P(None, "dp", None),
            P("dp"),
            P("dp"),
            P("dp"),
            P("dp", None),
            P("dp"),
            P(),
            P(),
            P(),
            P(),
            P(),
        ),
        check_vma=False,
    )
```

```python
import functools

import jax
import jax.numpy as jnp
from jax import lax
from jax.experimental import pallas as pl
from jax.experimental.pallas import tpu as pltpu
from jax.sharding import PartitionSpec as P

F32 = jnp.float32
BF = jnp.bfloat16
EPS = 1e-05
ROWS = 16
NN = (((1,), (0,)), ((), ()))
NT = (((1,), (1,)), ((), ()))
MIB = 1024 * 1024


def by_core(value, even_mask, odd_mask):
    n_dp, n_ctx = lax.axis_size("dp"), lax.axis_size("ctx")
    masks = (even_mask, odd_mask)
    pairs = [
        (d * n_ctx + t, (d ^ masks[t % 2]) * n_ctx + t) for d in range(n_dp) for t in range(n_ctx)
    ]
    return lax.ppermute(value, ("dp", "ctx"), pairs)


def swap(value, axis, mask):
    return lax.ppermute(value, axis, [(i, i ^ mask) for i in range(lax.axis_size(axis))])


def shifted(value, by):
    size = lax.axis_size("ctx")
    return lax.ppermute(value, "ctx", [(i, i + by) for i in range(size) if 0 <= i + by < size])


def half_of(rows):
    off = rows // 2 // 16 * 16
    return off, rows - off


def gated(value, gate):
    return value if gate is None else lax.optimization_barrier((value, gate))[0]


def after(value, *others):
    return lax.optimization_barrier((value, *others))[0]


def gather_halves(half):
    first = by_core(half, 1, 2)
    gate = yield half
    sent = jnp.stack([half, gated(first, gate)])
    second = by_core(sent, 2, 1)
    gate = yield sent
    second = gated(second, gate)
    other_first = swap(first, "ctx", 1)
    other_second = swap(second, "ctx", 1)
    yield second
    yield first, second, other_first, other_second


def sum_shards(keep, send):
    got = swap(send, "ctx", 1)
    gate = yield send
    got = gated(got, gate)
    sent = (keep[2:4].astype(F32) + got[2:4].astype(F32)).astype(BF)
    one = by_core(sent, 1, 2)
    gate = yield sent
    one = gated(one, gate)
    sent = (keep[1].astype(F32) + got[1].astype(F32) + one[1].astype(F32)).astype(BF)
    two = by_core(sent, 2, 1)
    gate = yield sent
    two = gated(two, gate)
    part = keep[0].astype(F32) + got[0].astype(F32) + one[0].astype(F32) + two.astype(F32)
    mask = 2
    while mask < lax.axis_size("ctx"):
        sent = part.astype(BF)
        came = swap(sent, "ctx", mask)
        gate = yield sent
        part = sent.astype(F32) + gated(came, gate).astype(F32)
        mask *= 2
    other = swap(part, "ctx", 1)
    gate = yield part
    yield part, gated(other, gate)


def sum_all(value):
    value = value + swap(value, "ctx", 1)
    value = value + swap(value, "dp", 1)
    value = value + swap(value, "dp", 2)
    mask = 2
    while mask < lax.axis_size("ctx"):
        value = value + swap(value, "ctx", mask)
        mask *= 2
    return value


def finish(stages):
    for value in stages:
        pass
    return value


def join_halves(mine, other, rows, row_dim, core):
    off, size = half_of(rows)
    low = jnp.where(core == 0, mine, other)
    high = jnp.where(core == 0, other, mine)
    return jnp.concatenate(
        [low, lax.slice_in_dim(high, size - off, size, axis=row_dim)], axis=row_dim
    )


def mm(left, right, dims=NN):
    return lax.dot_general(left, right, dims, preferred_element_type=F32)


def silu_of_half(y):
    return y * (1.0 + jnp.tanh(y))


def loop(count, body, unroll):
    lax.fori_loop(0, count, lambda i, _: (body(i), 0)[1], 0, unroll=unroll)


def full(shape):
    return pl.BlockSpec(shape, lambda s: (0,) * len(shape), pipeline_mode=pl.Buffered(1))


def seq(shape):
    return pl.BlockSpec((None,) + shape, lambda s: (s,) + (0,) * len(shape))


ANY = pl.BlockSpec(memory_space=pl.ANY)


def sds(shape, dtype):
    return jax.ShapeDtypeStruct(shape, dtype)


def rows_at(i, base=0):
    return pl.ds(pl.multiple_of(i * ROWS + base, ROWS), ROWS)


def lanes(tile, width):
    return jnp.concatenate([tile] * (width // 128), axis=1)


def col(ref, j, r, width):
    return lanes(ref[j, r, :], width)


def fold(v):
    t = v[:, 0:128]
    for j in range(1, v.shape[1] // 128):
        t = t + v[:, j * 128 : (j + 1) * 128]
    return t


def eight(v):
    return v[0:8] + v[8:16]


def spread(packs, out_ref, j, row, scale=1.0):
    own, near, far = packs
    me, core = lax.axis_index("dp"), lax.rem(lax.axis_index("ctx"), 2)
    part = out_ref.shape[1] // 4
    for mask, ref in ((0, own), (1 + core, near), (2 - core, far.at[0]), (3, far.at[1])):
        start = pl.multiple_of(jnp.bitwise_xor(me, mask) * part, 8)
        v = ref[...].astype(F32)[row : row + 1, 0:part] * scale
        out_ref[j, pl.ds(start, part), :] = jnp.broadcast_to(v, (128, part)).T


def gathered_row(sums):
    return jnp.sum(sums.T, axis=0, keepdims=True)


def row_stats(count, load, width, length):
    def total(i, a):
        return a + eight(load(i))

    zero = jnp.zeros((8, length), F32)
    a = lax.fori_loop(0, count, total, zero, unroll=5)
    mean = jnp.sum(a, axis=0, keepdims=True) * (1.0 / width)

    def squares(i, a):
        c = load(i) - mean
        return a + eight(c * c)

    a = lax.fori_loop(0, count, squares, zero, unroll=5)
    var = jnp.sum(a, axis=0, keepdims=True) * (1.0 / width)
    return mean, var


def start_load(pieces, dst, sems):
    shard, first, second, other_first, other_second = pieces
    rows = shard.shape[0]
    off, size = half_of(rows)
    me, core = lax.axis_index("dp"), lax.rem(lax.axis_index("ctx"), 2)
    near = jnp.bitwise_xor(me, 1 + core)
    far = jnp.bitwise_xor(me, 2 - core)
    both = jnp.bitwise_xor(me, 3)

    def at(device, half, count):
        return dst.at[pl.ds(pl.multiple_of(device * rows + half * off, 16), count), :]

    batch_one = [
        (shard, at(me, 0, rows)),
        (first.at[0:size], at(near, core, size)),
        (second.at[0, 0:size], at(far, core, size)),
        (second.at[1, 0:size], at(both, core, size)),
    ]
    batch_two = [
        (other_first.at[0:size], at(far, 1 - core, size)),
        (other_second.at[0, 0:size], at(near, 1 - core, size)),
        (other_second.at[1, 0:size], at(both, 1 - core, size)),
    ]
    copies = [
        pltpu.make_async_copy(src, to, sems.at[i])
        for i, (src, to) in enumerate(batch_one + batch_two)
    ]
    for c in copies[:4]:
        c.start()
    return copies


def finish_load(copies):
    for c in copies[:4]:
        c.wait()
    for c in copies[4:]:
        c.start()
    for c in copies[4:]:
        c.wait()


def assemble(shard, pieces, k, wide_s):
    first, second, other_first, other_second = pieces
    rows = shard.shape[0]
    off, _ = half_of(rows)
    me, core = lax.axis_index("dp"), lax.rem(lax.axis_index("ctx"), 2)
    near = jnp.bitwise_xor(me, 1 + core)
    far = jnp.bitwise_xor(me, 2 - core)
    both = jnp.bitwise_xor(me, 3)

    def put(device, half, piece):
        start = pl.ds(pl.multiple_of(device * rows + half * off, 8), piece.shape[0])
        wide_s[start, :] = piece.astype(F32)

    put(me, 0, shard)
    put(near, core, first[k])
    put(far, core, second[0, k])
    put(both, core, second[1, k])
    put(far, 1 - core, other_first[k])
    put(near, 1 - core, other_second[0, k])
    put(both, 1 - core, other_second[1, k])
    return wide_s[...].astype(BF)


def params():
    return pltpu.CompilerParams(vmem_limit_bytes=60 * MIB)


def cost(products, entries):
    return pl.CostEstimate(
        flops=2 * products + 40 * entries, bytes_accessed=8 * entries, transcendentals=entries
    )


def split_grad(acc_ref, keep_ref, send_ref, taps):
    me, core = lax.axis_index("dp"), lax.rem(lax.axis_index("ctx"), 2)
    block = acc_ref.shape[0] // taps
    rows = block // 4
    off, size = half_of(rows)
    mine = (0, 2 - core, 1 + core, 3)
    theirs = (0, 1 + core, 2 - core, 3)
    for j in range(4):
        for k in range(taps):
            a = jnp.bitwise_xor(me, mine[j]) * rows + core * off + k * block
            b = jnp.bitwise_xor(me, theirs[j]) * rows + (1 - core) * off + k * block
            at = (j, k) if taps > 1 else (j,)
            keep_ref[at] = acc_ref[pl.ds(pl.multiple_of(a, 8), size), :].astype(BF)
            send_ref[at] = acc_ref[pl.ds(pl.multiple_of(b, 8), size), :].astype(BF)


def prepare_in_body(*refs):
    w_ref, out_ref, rows_s = refs[0], refs[-2], refs[-1]
    off, size = half_of(w_ref.shape[0])
    core = lax.rem(lax.axis_index("ctx"), 2)
    out_ref[0:size, :] = w_ref[pl.ds(pl.multiple_of(core * off, 16), size), :]
    rows_s[...] = jnp.zeros_like(rows_s)
    for j, ref in enumerate(refs[1:-2]):
        n = ref.shape[0]
        rows_s[j : j + 1, 0:n] = ref[...].astype(F32).reshape(1, n)
    out_ref[size:, :] = rows_s[...].astype(BF)


def prepare_in(weight, vectors):
    rows, inner = weight.shape
    size = half_of(rows)[1]
    assert size % 16 == 0 and max(v.shape[0] for v in vectors) <= inner and len(vectors) <= 16
    vmem = pl.BlockSpec(memory_space=pltpu.VMEM)
    return pl.pallas_call(
        prepare_in_body,
        in_specs=[vmem] * (1 + len(vectors)),
        out_specs=vmem,
        out_shape=sds((size + 16, inner), BF),
        scratch_shapes=[pltpu.VMEM((16, inner), F32)],
        compiler_params=params(),
        name="prepare_in",
    )(weight, *vectors)


def prepare_rest_body(wc_ref, wo_ref, out_ref):
    inner = wc_ref.shape[2]
    off, size = half_of(wc_ref.shape[1])
    core = lax.rem(lax.axis_index("ctx"), 2)
    r = pl.ds(pl.multiple_of(core * off, 16), size)
    for k in range(3):
        out_ref[k] = wc_ref[k, r, :]
    half = wo_ref[r, :]
    out_ref[3] = half[:, 0:inner]
    out_ref[4] = half[:, inner:]


def prepare_rest(weight_conv, weight_out):
    inner = weight_conv.shape[2]
    vmem = pl.BlockSpec(memory_space=pltpu.VMEM)
    return pl.pallas_call(
        prepare_rest_body,
        in_specs=[vmem] * 2,
        out_specs=vmem,
        out_shape=sds((5, half_of(weight_conv.shape[1])[1], inner), BF),
        compiler_params=params(),
        name="prepare_rest",
    )(weight_conv, weight_out)


def vec_specs(packs):
    own, first, second = packs
    inner = own.shape[1]
    at = own.shape[0] // 16 - 1
    row = pl.BlockSpec((16, inner), lambda s: (at, 0))
    return [row, row, pl.BlockSpec((2, 16, inner), lambda s: (0, at, 0))]


def stats_body(x_ref, st_ref, sq_ref):
    wide, length = x_ref.shape

    @pl.when(pl.program_id(0) == 0)
    def _():
        sq_ref[...] = jnp.zeros_like(sq_ref)

    mean, var = row_stats(wide // ROWS, lambda i: x_ref[rows_at(i), :].astype(F32), wide, length)
    st_ref[0:1, :] = mean
    st_ref[1:2, :] = lax.rsqrt(var + EPS)
    sq_ref[0:1, :] += (var + mean * mean) * float(wide)


def input_stats(x):
    seqs, wide, length = x.shape
    return pl.pallas_call(
        stats_body,
        grid=(seqs,),
        in_specs=[seq((wide, length))],
        out_specs=[seq((8, length)), full((8, length))],
        out_shape=[sds((seqs, 8, length), F32), sds((8, length), F32)],
        compiler_params=params(),
        cost_estimate=cost(0, x.size // 4),
        name="input_stats",
    )(x)


def act_body(x_ref, st_ref, v0, v1, v2, a0_ref, vw_s):
    wide, length = x_ref.shape

    @pl.when(pl.program_id(0) == 0)
    def _():
        for j in range(2):
            spread((v0, v1, v2), vw_s, j, j, 0.5)

    mean = st_ref[0:1, :]
    inv = st_ref[1:2, :]

    def act0(i):
        r = rows_at(i)
        y = (x_ref[r, :].astype(F32) - mean) * inv * col(vw_s, 0, r, length)
        a0_ref[r, :] = silu_of_half(y + col(vw_s, 1, r, length)).astype(BF)

    loop(wide // ROWS, act0, 5)


def first_act(x, stats, packs):
    seqs, wide, length = x.shape
    return pl.pallas_call(
        act_body,
        grid=(seqs,),
        in_specs=[seq((wide, length)), seq((8, length))] + vec_specs(packs),
        out_specs=seq((wide, length)),
        out_shape=sds((seqs, wide, length), BF),
        scratch_shapes=[pltpu.VMEM((2, wide, 128), F32)],
        compiler_params=params(),
        cost_estimate=cost(0, x.size // 2),
        name="first_act",
    )(x, stats, *packs)


def first_body(
    a0_ref, p0, p1, p2, p3, p4, v0, v1, v2,
    h1_ref, a1_ref, edge_ref, sq_ref,
    w_s, wt_s, vi_s, sems,
):
    s = pl.program_id(0)
    inner, length = h1_ref.shape

    @pl.when(s == 0)
    def _():
        copies = start_load((p0, p1, p2, p3, p4), w_s, sems)
        sq_ref[...] = jnp.zeros_like(sq_ref)
        for j in range(3):
            spread((v0, v1, v2), vi_s, j, j + 3, (1.0, 0.5, 0.5)[j])
        finish_load(copies)
        wt_s[...] = w_s[...].T

    h1_ref[...] = mm(wt_s[...], a0_ref[...]) + lanes(vi_s[0], length)
    mean1, var1 = row_stats(inner // ROWS, lambda i: h1_ref[rows_at(i), :], inner, length)
    inv1 = lax.rsqrt(var1 + EPS)
    sq_ref[0:1, :] += (var1 + mean1 * mean1) * float(inner)

    def act1(i):
        r = rows_at(i)
        y = (h1_ref[r, :] - mean1) * inv1 * col(vi_s, 1, r, length) + col(vi_s, 2, r, length)
        a1_ref[r, :] = silu_of_half(y).astype(BF)

    loop(inner // ROWS, act1, 5)
    edge_ref[...] = a1_ref[:, length - 128 :].astype(F32).T[120:128, :].astype(BF)


def first(a0, pieces, packs):
    seqs, wide, length = a0.shape
    inner = pieces[0].shape[1]
    return pl.pallas_call(
        first_body,
        grid=(seqs,),
        in_specs=[seq((wide, length))] + [ANY] * 5 + vec_specs(packs),
        out_specs=[seq((inner, length)), seq((inner, length)), seq((8, inner)), full((8, length))],
        out_shape=[
            sds((seqs, inner, length), F32),
            sds((seqs, inner, length), BF),
            sds((seqs, 8, inner), BF),
            sds((8, length), F32),
        ],
        scratch_shapes=[
            pltpu.VMEM((wide, inner), BF),
            pltpu.VMEM((inner, wide), BF),
            pltpu.VMEM((3, inner, 128), F32),
            pltpu.SemaphoreType.DMA((7,)),
        ],
        compiler_params=params(),
        cost_estimate=cost(a0.size * inner, a0.size),
        name="first_product",
    )(a0, *pieces, *packs)


def assemble_body(wc_own, wo_own, f, g, of, og, wc_ref, wct_ref, wo_ref, wot_ref, tap_s):
    inner = wc_ref.shape[1]
    pieces = (f, g, of, og)
    for k in range(3):
        wc_ref[k] = assemble(wc_own[k], pieces, k, tap_s)
    wct_ref[...] = wc_ref[...].reshape(3 * inner, inner).T
    for k in range(2):
        wo_ref[k] = assemble(wo_own[:, k * inner : (k + 1) * inner], pieces, 3 + k, tap_s)
        wot_ref[k * inner : (k + 1) * inner, :] = wo_ref[k].T


def assemble_weights(own_conv, own_out, pieces):
    inner = own_conv.shape[2]
    vmem = pl.BlockSpec(memory_space=pltpu.VMEM)
    return pl.pallas_call(
        assemble_body,
        in_specs=[vmem] * 6,
        out_specs=[vmem] * 4,
        out_shape=[
            sds((3, inner, inner), BF),
            sds((inner, 3 * inner), BF),
            sds((2, inner, inner), BF),
            sds((2 * inner, inner), BF),
        ],
        scratch_shapes=[pltpu.VMEM((inner, inner), F32)],
        compiler_params=params(),
        cost_estimate=cost(0, 4 * inner * inner),
        name="assemble_weights",
    )(own_conv, own_out, *pieces)


def conv_body(
    a1_ref, halo_ref, dy_ref, mk_ref, wct_ref, wo_ref, v0, v1, v2,
    a2_ref, dh2_ref, edge_ref, sums_ref, bo_ref, sq_ref, keep_ref, send_ref,
    st_s, h_s, d_s, hl_s, vi_s, sums_s, bo_s, acc_s,
):
    s = pl.program_id(0)
    inner, length = a1_ref.shape
    wide = dy_ref.shape[0]
    steps = inner // ROWS

    @pl.when(s == 0)
    def _():
        sq_ref[...] = jnp.zeros_like(sq_ref)
        sums_s[...] = jnp.zeros_like(sums_s)
        bo_s[...] = jnp.zeros_like(bo_s)
        for j in range(3):
            spread((v0, v1, v2), vi_s, j, j + 6, (1.0, 0.5, 0.5)[j])

    hl_s[...] = jnp.concatenate(
        [jnp.zeros((120, inner), F32), halo_ref[...].astype(F32)], axis=0
    ).T
    m1 = mk_ref[1:2, :]
    m2 = mk_ref[2:3, :]

    def build(i):
        r = rows_at(i)
        b = a1_ref[r, :]
        v = jnp.concatenate([b.astype(F32), hl_s[r, :]], axis=1)
        st_s[r, :] = b
        st_s[rows_at(i, inner), :] = (pltpu.roll(v, 2, 1)[:, 0:length] * m1).astype(BF)
        st_s[rows_at(i, 2 * inner), :] = (pltpu.roll(v, 4, 1)[:, 0:length] * m2).astype(BF)

    loop(steps, build, 10)
    h_s[...] = mm(wct_ref[...], st_s[...]) + lanes(vi_s[0], length)
    d_s[...] = mm(wo_ref[0], dy_ref[0:inner, :]) + mm(wo_ref[1], dy_ref[inner:, :])
    mean, var = row_stats(steps, lambda i: h_s[rows_at(i), :], inner, length)
    inv = lax.rsqrt(var + EPS)
    sq_ref[0:1, :] += (var + mean * mean) * float(inner)

    def back(i, acc):
        r = rows_at(i)
        n = (h_s[r, :] - mean) * inv
        g = col(vi_s, 1, r, length)
        y = n * g + col(vi_s, 2, r, length)
        t = jnp.tanh(y)
        up = 1.0 + t
        a2_ref[r, :] = (y * up).astype(BF)
        e = d_s[r, :] * (up * (1.0 + y * (1.0 - t)))
        q = e * g
        d_s[r, :] = q
        h_s[r, :] = n
        sums_s[0, r, :] += fold(e * n)
        sums_s[1, r, :] += fold(e)
        return acc[0] + eight(q), acc[1] + eight(q * n)

    zero = jnp.zeros((8, length), F32)
    qa, qn = lax.fori_loop(0, steps, back, (zero, zero), unroll=5)
    mq = jnp.sum(qa, axis=0, keepdims=True) * (1.0 / inner)
    mqn = jnp.sum(qn, axis=0, keepdims=True) * (1.0 / inner)

    def last(i):
        r = rows_at(i)
        dh = ((d_s[r, :] - mq - h_s[r, :] * mqn) * inv).astype(BF)
        dh2_ref[r, :] = dh
        sums_s[2, r, :] += fold(dh.astype(F32))

    loop(steps, last, 5)

    def bias(i):
        r = rows_at(i)
        bo_s[r, :] += fold(dy_ref[r, :].astype(F32))

    loop(wide // ROWS, bias, 5)

    @pl.when(s == 0)
    def _():
        acc_s[0 : 3 * inner, :] = mm(st_s[...], dh2_ref[...], NT)
        for k in range(2):
            acc_s[(3 + k) * inner : (4 + k) * inner, :] = mm(
                a2_ref[...], dy_ref[k * inner : (k + 1) * inner, :], NT
            )

    @pl.when(s > 0)
    def _():
        acc_s[0 : 3 * inner, :] += mm(st_s[...], dh2_ref[...], NT)
        for k in range(2):
            acc_s[(3 + k) * inner : (4 + k) * inner, :] += mm(
                a2_ref[...], dy_ref[k * inner : (k + 1) * inner, :], NT
            )

    edge_ref[...] = dh2_ref[:, 0:128].astype(F32).T[0:8, :].astype(BF)

    @pl.when(s == pl.num_programs(0) - 1)
    def _():
        for j in range(3):
            sums_ref[j : j + 1, :] = gathered_row(sums_s[j]) * (0.5, 0.5, 1.0)[j]
        bo_ref[0:1, :] = gathered_row(bo_s[...])
        split_grad(acc_s, keep_ref, send_ref, 5)


def conv(a1, halo, dy, mk, wct, wo, packs):
    seqs, inner, length = a1.shape
    wide = dy.shape[1]
    size = half_of(inner // 4)[1]
    return pl.pallas_call(
        conv_body,
        grid=(seqs,),
        in_specs=[seq((inner, length)), seq((8, inner)), seq((wide, length)), seq((8, length))]
        + [full(p.shape) for p in (wct, wo)]
        + vec_specs(packs),
        out_specs=[
            seq((inner, length)),
            seq((inner, length)),
            seq((8, inner)),
            full((8, inner)),
            full((8, wide)),
            full((8, length)),
            full((4, 5, size, inner)),
            full((4, 5, size, inner)),
        ],
        out_shape=[
            sds((seqs, inner, length), BF),
            sds((seqs, inner, length), BF),
            sds((seqs, 8, inner), BF),
            sds((8, inner), F32),
            sds((8, wide), F32),
            sds((8, length), F32),
            sds((4, 5, size, inner), BF),
            sds((4, 5, size, inner), BF),
        ],
        scratch_shapes=[
            pltpu.VMEM((3 * inner, length), BF),
            pltpu.VMEM((inner, length), F32),
            pltpu.VMEM((inner, length), F32),
            pltpu.VMEM((inner, 128), F32),
            pltpu.VMEM((3, inner, 128), F32),
            pltpu.VMEM((3, inner, 128), F32),
            pltpu.VMEM((wide, 128), F32),
            pltpu.VMEM((5 * inner, inner), F32),
        ],
        compiler_params=params(),
        cost_estimate=cost(a1.size * (6 * inner + 2 * wide), 2 * a1.size),
        name="conv_and_third_norm",
    )(a1, halo, dy, mk, wct, wo, *packs)


def grad_body(a_ref, b_ref, keep_ref, send_ref, acc_s):
    s = pl.program_id(0)

    @pl.when(s == 0)
    def _():
        acc_s[...] = mm(a_ref[...], b_ref[...], NT)

    @pl.when(s > 0)
    def _():
        acc_s[...] += mm(a_ref[...], b_ref[...], NT)

    @pl.when(s == pl.num_programs(0) - 1)
    def _():
        split_grad(acc_s, keep_ref, send_ref, 1)


def grad(a, b, name):
    seqs, m, length = a.shape
    n = b.shape[1]
    size = half_of(m // 4)[1]
    return pl.pallas_call(
        grad_body,
        grid=(seqs,),
        in_specs=[seq((m, length)), seq((n, length))],
        out_specs=[full((4, size, n)), full((4, size, n))],
        out_shape=[sds((4, size, n), BF), sds((4, size, n), BF)],
        scratch_shapes=[pltpu.VMEM((m, n), F32)],
        compiler_params=params(),
        cost_estimate=cost(a.size * n, 0),
        name=name,
    )(a, b)


def shift_back(dh2_ref, halo_ref, mk_ref, hl_s, t_s):
    inner, length = dh2_ref.shape
    hl_s[...] = jnp.concatenate(
        [halo_ref[...].astype(F32), jnp.zeros((120, inner), F32)], axis=0
    ).T
    f1 = mk_ref[3:4, :]
    f2 = mk_ref[4:5, :]

    def build(i):
        r = rows_at(i)
        v = jnp.concatenate([dh2_ref[r, :].astype(F32), hl_s[r, :]], axis=1)
        t_s[0, r, :] = (pltpu.roll(v, length + 126, 1)[:, 0:length] * f1).astype(BF)
        t_s[1, r, :] = (pltpu.roll(v, length + 124, 1)[:, 0:length] * f2).astype(BF)

    loop(inner // ROWS, build, 10)


def conv_back_body(
    dh2_ref, halo_ref, h1_ref, mk_ref, wc_ref, v0, v1, v2, before_ref,
    dh1_ref, sums_ref,
    t_s, d_s, n_s, hl_s, vi_s, sums_s,
):
    s = pl.program_id(0)
    inner, length = dh2_ref.shape
    steps = inner // ROWS

    @pl.when(s == 0)
    def _():
        sums_s[...] = jnp.zeros_like(sums_s)
        for j in range(2):
            spread((v0, v1, v2), vi_s, j, j + 4, 0.5)

    shift_back(dh2_ref, halo_ref, mk_ref, hl_s, t_s)
    d_s[...] = mm(wc_ref[0], dh2_ref[...]) + mm(wc_ref[1], t_s[0]) + mm(wc_ref[2], t_s[1])
    mean, var = row_stats(steps, lambda i: h1_ref[rows_at(i), :], inner, length)
    inv = lax.rsqrt(var + EPS)

    def back(i, acc):
        r = rows_at(i)
        n = (h1_ref[r, :] - mean) * inv
        g = col(vi_s, 0, r, length)
        y = n * g + col(vi_s, 1, r, length)
        t = jnp.tanh(y)
        e = d_s[r, :] * ((1.0 + t) * (1.0 + y * (1.0 - t)))
        q = e * g
        d_s[r, :] = q
        n_s[r, :] = n
        sums_s[0, r, :] += fold(e * n)
        sums_s[1, r, :] += fold(e)
        return acc[0] + eight(q), acc[1] + eight(q * n)

    zero = jnp.zeros((8, length), F32)
    qa, qn = lax.fori_loop(0, steps, back, (zero, zero), unroll=5)
    mq = jnp.sum(qa, axis=0, keepdims=True) * (1.0 / inner)
    mqn = jnp.sum(qn, axis=0, keepdims=True) * (1.0 / inner)

    def last(i):
        r = rows_at(i)
        dh = ((d_s[r, :] - mq - n_s[r, :] * mqn) * inv).astype(BF)
        dh1_ref[r, :] = dh
        sums_s[2, r, :] += fold(dh.astype(F32))

    loop(steps, last, 5)

    @pl.when(s == pl.num_programs(0) - 1)
    def _():
        for j in range(3):
            sums_ref[j : j + 1, :] = gathered_row(sums_s[j]) * (0.5, 0.5, 1.0)[j]


def seq_from(begin, shape):
    return pl.BlockSpec((None,) + shape, lambda s: (s + begin,) + (0,) * len(shape))


def conv_back(dh2, halo, h1, mk, wc, packs, begin, count, before):
    seqs, inner, length = dh2.shape
    return pl.pallas_call(
        conv_back_body,
        grid=(count,),
        in_specs=[
            seq_from(begin, (inner, length)),
            seq_from(begin, (8, inner)),
            seq_from(begin, (inner, length)),
            seq_from(begin, (8, length)),
            full(wc.shape),
        ]
        + vec_specs(packs)
        + [ANY],
        out_specs=[seq_from(begin, (inner, length)), full((8, inner))],
        out_shape=[sds((seqs, inner, length), BF), sds((8, inner), F32)],
        input_output_aliases={8: 0} if begin else {},
        scratch_shapes=[
            pltpu.VMEM((2, inner, length), BF),
            pltpu.VMEM((inner, length), F32),
            pltpu.VMEM((inner, length), F32),
            pltpu.VMEM((inner, 128), F32),
            pltpu.VMEM((2, inner, 128), F32),
            pltpu.VMEM((3, inner, 128), F32),
        ],
        compiler_params=params(),
        cost_estimate=cost(dh2.size * 3 * inner * count // seqs, 2 * dh2.size * count // seqs),
        name="conv_backward",
    )(dh2, halo, h1, mk, wc, *packs, before)


def stream_body(
    x_ref, st_ref, dy_ref, dh1_ref, p0, p1, p2, p3, p4, v0, v1, v2, before_ref,
    gs_ref, sums_ref,
    w_s, d_s, n_s, vw_s, sums_s, sems,
):
    s = pl.program_id(0)
    wide, length = x_ref.shape
    steps = wide // ROWS

    @pl.when(s == 0)
    def _():
        copies = start_load((p0, p1, p2, p3, p4), w_s, sems)
        sums_s[...] = jnp.zeros_like(sums_s)
        for j in range(2):
            spread((v0, v1, v2), vw_s, j, j, 0.5)
        finish_load(copies)

    d_s[...] = mm(w_s[...], dh1_ref[...])
    mean = st_ref[0:1, :]
    inv = st_ref[1:2, :]

    def back(i, acc):
        r = rows_at(i)
        n = (x_ref[r, :].astype(F32) - mean) * inv
        g = col(vw_s, 0, r, length)
        y = n * g + col(vw_s, 1, r, length)
        t = jnp.tanh(y)
        e = d_s[r, :] * ((1.0 + t) * (1.0 + y * (1.0 - t)))
        q = e * g
        d_s[r, :] = q
        n_s[r, :] = n
        sums_s[0, r, :] += fold(e * n)
        sums_s[1, r, :] += fold(e)
        return acc[0] + eight(q), acc[1] + eight(q * n)

    zero = jnp.zeros((8, length), F32)
    qa, qn = lax.fori_loop(0, steps, back, (zero, zero), unroll=5)
    mq = jnp.sum(qa, axis=0, keepdims=True) * (1.0 / wide)
    mqn = jnp.sum(qn, axis=0, keepdims=True) * (1.0 / wide)

    def last(i):
        r = rows_at(i)
        gs = dy_ref[r, :].astype(F32) + (d_s[r, :] - mq - n_s[r, :] * mqn) * inv
        gs_ref[r, :] = gs.astype(BF)

    loop(steps, last, 5)

    @pl.when(s == pl.num_programs(0) - 1)
    def _():
        for j in range(2):
            sums_ref[j : j + 1, :] = gathered_row(sums_s[j]) * 0.5


def stream_back(x, stats, dy, dh1, pieces, packs, begin, count, before):
    seqs, wide, length = x.shape
    inner = dh1.shape[1]
    aliases = {12: 0} if begin else {}
    return pl.pallas_call(
        stream_body,
        grid=(count,),
        in_specs=[
            seq_from(begin, (wide, length)),
            seq_from(begin, (8, length)),
            seq_from(begin, (wide, length)),
            seq_from(begin, (inner, length)),
        ]
        + [ANY] * 5
        + vec_specs(packs)
        + [ANY],
        out_specs=[seq_from(begin, (wide, length)), full((8, wide))],
        out_shape=[sds((seqs, wide, length), BF), sds((8, wide), F32)],
        input_output_aliases=aliases,
        scratch_shapes=[
            pltpu.VMEM((wide, inner), BF),
            pltpu.VMEM((wide, length), F32),
            pltpu.VMEM((wide, length), F32),
            pltpu.VMEM((2, wide, 128), F32),
            pltpu.VMEM((2, wide, 128), F32),
            pltpu.SemaphoreType.DMA((7,)),
        ],
        compiler_params=params(),
        cost_estimate=cost(dh1.size * wide * count // seqs, x.size * count // seqs),
        name="grad_stream",
    )(x, stats, dy, dh1, *pieces, *packs, before)


def output_body(x_ref, a2_ref, wt_ref, v0, v1, v2, before_ref, out_ref, sq_ref, o_s, vw_s):
    s = pl.program_id(0)
    wide, length = x_ref.shape

    @pl.when(s == 0)
    def _():
        sq_ref[...] = jnp.zeros_like(sq_ref)
        spread((v0, v1, v2), vw_s, 0, 2)

    o_s[...] = mm(wt_ref[...], a2_ref[...])

    def close(i, acc):
        r = rows_at(i)
        branch = o_s[r, :] + col(vw_s, 0, r, length)
        result = x_ref[r, :].astype(F32) + branch
        out_ref[r, :] = result.astype(BF)
        return acc[0] + eight(branch * branch), acc[1] + eight(result * result)

    zero = jnp.zeros((8, length), F32)
    b2, r2 = lax.fori_loop(0, wide // ROWS, close, (zero, zero), unroll=5)
    sq_ref[0:1, :] += jnp.sum(b2, axis=0, keepdims=True)
    sq_ref[1:2, :] += jnp.sum(r2, axis=0, keepdims=True)


def output_of(x, a2, wt, packs, begin, count, before):
    seqs, wide, length = x.shape
    inner = a2.shape[1]
    aliases = {6: 0} if begin else {}
    return pl.pallas_call(
        output_body,
        grid=(count,),
        in_specs=[seq_from(begin, (wide, length)), seq_from(begin, (inner, length))]
        + [full(wt.shape)]
        + vec_specs(packs)
        + [ANY],
        out_specs=[seq_from(begin, (wide, length)), full((8, length))],
        out_shape=[sds((seqs, wide, length), BF), sds((8, length), F32)],
        input_output_aliases=aliases,
        scratch_shapes=[
            pltpu.VMEM((wide, length), F32),
            pltpu.VMEM((1, wide, 128), F32),
        ],
        compiler_params=params(),
        cost_estimate=cost(a2.size * wide * count // seqs, x.size * count // (4 * seqs)),
        name="block_output",
    )(x, a2, wt, *packs, before)


def pack_sums_body(bo, two, one_a, one_b, zero_a, zero_b, q_in, q_one, q_two, qo_a, qo_b, out_ref):
    inner = two.shape[1]
    out_ref[...] = jnp.zeros_like(out_ref)
    out_ref[0:2, :] = zero_a[0:2, :] + zero_b[0:2, :]
    out_ref[2:3, :] = bo[0:1, :]
    one = one_a[0:3, :] + one_b[0:3, :]
    out_ref[3:6, 0:inner] = one
    out_ref[3:6, inner : 2 * inner] = two[0:3, :]
    out = qo_a[0:2, :] + qo_b[0:2, :]
    rows = (q_in[0:1, :], out[1:2, :], q_one[0:1, :], q_two[0:1, :], out[0:1, :])
    for j, row in enumerate(rows):
        total = jnp.sum(row, axis=1, keepdims=True)
        out_ref[6:7, j * 128 : (j + 1) * 128] = jnp.broadcast_to(total, (1, 128))


def pack_sums(bo, *rest):
    vmem = pl.BlockSpec(memory_space=pltpu.VMEM)
    return pl.pallas_call(
        pack_sums_body,
        in_specs=[vmem] * (1 + len(rest)),
        out_specs=vmem,
        out_shape=sds((8, bo.shape[1]), F32),
        compiler_params=params(),
        name="pack_sums",
    )(bo, *rest)


def unpack_body(counts, s_ref, *outs):
    me = lax.axis_index("dp")
    wide = s_ref.shape[1]
    inner = wide // 2

    def part(row, begin, size):
        v = s_ref[row : row + 1, begin : begin + size]
        for d in range(1, 4):
            at = begin + d * size
            v = jnp.where(me == d, s_ref[row : row + 1, at : at + size], v)
        return v.reshape(size)

    for j in range(3):
        outs[j][...] = part(j, 0, wide // 4)
    for j in range(6):
        outs[3 + j][...] = part(3 + j % 3, (j // 3) * inner, inner // 4)
    for j, count in enumerate(counts):
        outs[9 + j][...] = jnp.sqrt(s_ref[6:7, j * 128 : (j + 1) * 128] / count)


def unpack_sums(sums, counts):
    wide = sums.shape[1]
    vmem = pl.BlockSpec(memory_space=pltpu.VMEM)
    return pl.pallas_call(
        functools.partial(unpack_body, counts),
        in_specs=[vmem],
        out_specs=[vmem] * 14,
        out_shape=[sds((wide // 4,), F32)] * 3
        + [sds((wide // 8,), F32)] * 6
        + [sds((1, 128), F32)] * 5,
        compiler_params=params(),
        name="unpack_sums",
    )(sums)


def local(
    stream, segments, cotangent, gain_zero, shift_zero, weight_in, bias_in, gain_one, shift_one,
    weight_conv, bias_conv, gain_two, shift_two, weight_out, bias_out,
):
    n_dp, n_ctx = lax.axis_size("dp"), lax.axis_size("ctx")
    assert n_dp == 4 and n_ctx & (n_ctx - 1) == 0
    me, place = lax.axis_index("dp"), lax.axis_index("ctx")
    core = place % 2
    seqs, length, wide = stream.shape
    inner = weight_conv.shape[2]
    part_w, part_i = gain_zero.shape[0], bias_in.shape[0]

    x = jnp.swapaxes(stream, 1, 2)
    dy = jnp.swapaxes(cotangent, 1, 2)

    half_in = prepare_in(
        weight_in,
        [gain_zero, shift_zero, bias_out, bias_in, gain_one, shift_one, bias_conv, gain_two, shift_two],
    )
    part_in = gather_halves(half_in)
    sent = next(part_in)
    rest_half = prepare_rest(after(weight_conv, sent), weight_out)
    stats, sq_in = input_stats(after(x, rest_half))
    part_in.send(sq_in)
    came = part_in.send(None)
    part_rest = gather_halves(after(rest_half, came))
    sent = next(part_rest)
    piece_in = (weight_in, *next(part_in))
    packs = (half_in, *piece_in[1:3])
    act_zero = first_act(x, after(stats, sent), packs)
    sent = part_rest.send(act_zero)

    padded = jnp.pad(segments, ((0, 0), (4, 4)), constant_values=-1)
    near_segs = lax.dynamic_slice_in_dim(padded, place * length, length + 8, 1)
    here = near_segs[:, 4 : 4 + length]
    same = [(near_segs[:, 4 + j : 4 + j + length] == here).astype(F32) for j in (0, -2, -4, 2, 4)]
    masks = jnp.stack(same + same[:3], axis=1)

    hidden_one, act_one, edge, sq_one = first(
        act_zero, piece_in, (after(half_in, sent, masks), *packs[1:])
    )
    halo = shifted(edge, 1)
    part_rest.send(sq_one)
    full_conv, full_conv_t, full_out, full_out_t = assemble_weights(
        weight_conv, weight_out, next(part_rest)
    )
    act_two, d_hidden_two, edge_back, sums_two, sum_bo, sq_two, keep, send = conv(
        act_one, halo, dy, masks, full_conv_t, full_out, packs
    )
    halo_back = shifted(edge_back, -1)
    sum_rest = sum_shards(keep, send)
    own_then = after(half_in, next(sum_rest))
    half = seqs // 2
    d_hidden_one, sums_one = conv_back(
        d_hidden_two, halo_back, hidden_one, masks, full_conv, (own_then, *packs[1:]), 0, half, masks
    )
    own_then = after(own_then, sum_rest.send(sums_one))
    d_hidden_one, more_one = conv_back(
        d_hidden_two, halo_back, hidden_one, masks, full_conv, (own_then, *packs[1:]),
        half, seqs - half, d_hidden_one,
    )
    keep_in, send_in = grad(
        act_zero, after(d_hidden_one, sum_rest.send(more_one)), "grad_weight_in"
    )
    sum_in = sum_shards(keep_in, send_in)
    own_then = after(own_then, next(sum_in), sum_rest.send(send_in))
    grad_x, sums_zero = stream_back(
        x, stats, dy, d_hidden_one, piece_in, (own_then, *packs[1:]), 0, half, stats
    )
    own_then = after(own_then, sum_in.send(sums_zero), sum_rest.send(sums_zero))
    grad_x, more_zero = stream_back(
        x, stats, dy, d_hidden_one, piece_in, (own_then, *packs[1:]), half, seqs - half, grad_x
    )
    own_then = after(own_then, sum_in.send(more_zero))
    output, sq_out = output_of(x, act_two, full_out_t, (own_then, *packs[1:]), 0, half, stats)
    own_then = after(own_then, sum_in.send(sq_out))
    output, more_out = output_of(
        x, act_two, full_out_t, (own_then, *packs[1:]), half, seqs - half, output
    )
    sums = pack_sums(
        sum_bo, sums_two, sums_one, more_one, sums_zero, more_zero,
        sq_in, sq_one, sq_two, sq_out, more_out,
    )
    count = float(seqs * length * n_dp * n_ctx)
    sums = sum_all(sums)
    sum_rest.send(sums)
    sum_in.send(sums)
    totals = unpack_sums(
        sums,
        (count * wide, count * wide, count * inner, count * inner, count * wide),
    )
    grad_gain_zero, grad_shift_zero, grad_bias_out = totals[0:3]
    grad_gain_one, grad_shift_one, grad_bias_in = totals[3:6]
    grad_gain_two, grad_shift_two, grad_bias_conv = totals[6:9]
    rms_in, rms_out, rms_hidden_one, rms_hidden_two, rms_branch = (v[0, 0] for v in totals[9:])
    rest = join_halves(*finish(sum_rest), part_i, 1, core)
    grad_weight_conv = rest[0:3]
    grad_weight_out = jnp.concatenate([rest[3], rest[4]], axis=1)
    grad_weight_in = join_halves(*finish(sum_in), part_w, 0, core)
    return (
        jnp.swapaxes(output, 1, 2),
        jnp.swapaxes(grad_x, 1, 2),
        grad_gain_zero,
        grad_shift_zero,
        grad_weight_in,
        grad_bias_in,
        grad_gain_one,
        grad_shift_one,
        grad_weight_conv,
        grad_bias_conv,
        grad_gain_two,
        grad_shift_two,
        grad_weight_out,
        grad_bias_out,
        rms_in,
        rms_out,
        rms_hidden_one,
        rms_hidden_two,
        rms_branch,
    )


def solution(mesh):
    placed = (
        P("dp", "ctx", None),
        P("dp", None),
        P("dp", "ctx", None),
        P("dp"),
        P("dp"),
        P("dp", None),
        P("dp"),
        P("dp"),
        P("dp"),
        P(None, "dp", None),
        P("dp"),
        P("dp"),
        P("dp"),
        P("dp", None),
        P("dp"),
    )
    return jax.shard_map(
        local,
        mesh=mesh,
        in_specs=placed,
        out_specs=(
            P("dp", "ctx", None),
            P("dp", "ctx", None),
            P("dp"),
            P("dp"),
            P("dp", None),
            P("dp"),
            P("dp"),
            P("dp"),
            P(None, "dp", None),
            P("dp"),
            P("dp"),
            P("dp"),
            P("dp", None),
            P("dp"),
            P(),
            P(),
            P(),
            P(),
            P(),
        ),
        check_vma=False,
    )
```

```python
import functools

import jax
import jax.numpy as jnp
from jax import lax
from jax.experimental import pallas as pl
from jax.experimental.pallas import tpu as pltpu
from jax.sharding import PartitionSpec as P

F32 = jnp.float32
BF = jnp.bfloat16
EPS = 1e-05
ROWS = 16
NN = (((1,), (0,)), ((), ()))
NT = (((1,), (1,)), ((), ()))
MIB = 1024 * 1024


def by_core(value, even_mask, odd_mask):
    n_dp, n_ctx = lax.axis_size("dp"), lax.axis_size("ctx")
    masks = (even_mask, odd_mask)
    pairs = [
        (d * n_ctx + t, (d ^ masks[t % 2]) * n_ctx + t) for d in range(n_dp) for t in range(n_ctx)
    ]
    return lax.ppermute(value, ("dp", "ctx"), pairs)


def swap(value, axis, mask):
    return lax.ppermute(value, axis, [(i, i ^ mask) for i in range(lax.axis_size(axis))])


def shifted(value, by):
    size = lax.axis_size("ctx")
    return lax.ppermute(value, "ctx", [(i, i + by) for i in range(size) if 0 <= i + by < size])


def half_of(rows):
    off = rows // 2 // 16 * 16
    return off, rows - off


def gated(value, gate):
    return value if gate is None else lax.optimization_barrier((value, gate))[0]


def after(value, *others):
    return lax.optimization_barrier((value, *others))[0]


def gather_halves(half):
    first = by_core(half, 1, 2)
    gate = yield half
    sent = jnp.stack([half, gated(first, gate)])
    second = by_core(sent, 2, 1)
    gate = yield sent
    second = gated(second, gate)
    other_first = swap(first, "ctx", 1)
    other_second = swap(second, "ctx", 1)
    yield second
    yield first, second, other_first, other_second


def halved(value, bit):
    rows = value.shape[1]
    off, size = parts_of(rows)
    keep = lax.dynamic_slice_in_dim(value, bit * off, size, 1)
    return keep, lax.dynamic_slice_in_dim(value, (1 - bit) * off, size, 1)


def parts_of(rows):
    off = rows // 2 // 8 * 8
    return off, rows - off


def joined(mine, other, bit, rows):
    off, size = parts_of(rows)
    low = jnp.where(bit == 0, mine, other)
    high = jnp.where(bit == 0, other, mine)
    return jnp.concatenate([low, high[:, size - off :]], axis=1)


def sum_shards(keep, send, halving):
    got = swap(send, "ctx", 1)
    gate = yield send
    got = gated(got, gate)
    sent = (keep[2:4].astype(F32) + got[2:4].astype(F32)).astype(BF)
    one = by_core(sent, 1, 2)
    gate = yield sent
    one = gated(one, gate)
    sent = (keep[1].astype(F32) + got[1].astype(F32) + one[1].astype(F32)).astype(BF)
    two = by_core(sent, 2, 1)
    gate = yield sent
    two = gated(two, gate)
    part = keep[0].astype(F32) + got[0].astype(F32) + one[0].astype(F32) + two.astype(F32)
    place = lax.axis_index("ctx")
    masks = [1 << b for b in range(1, (lax.axis_size("ctx") - 1).bit_length())]
    split = [(mask, (place // mask) % 2) for mask in masks[: 2 if halving else 0]]
    sizes = []
    for mask, bit in split:
        sizes.append(part.shape[1])
        part, sent = halved(part, bit)
        sent = sent.astype(BF)
        came = swap(sent, "ctx", mask)
        gate = yield sent
        part = part + gated(came, gate).astype(F32)
    for mask in masks[len(split) :]:
        sent = part.astype(BF)
        came = swap(sent, "ctx", mask)
        gate = yield sent
        part = sent.astype(F32) + gated(came, gate).astype(F32)
    for mask, bit in split[::-1]:
        sent = part.astype(BF)
        came = swap(sent, "ctx", mask)
        gate = yield sent
        part = joined(sent, gated(came, gate), bit, sizes.pop())
    other = swap(part, "ctx", 1)
    gate = yield part
    yield part, gated(other, gate)


def sum_all(value):
    got = swap(value, "ctx", 1)
    gate = yield value
    value = value + gated(got, gate)
    groups = [("dp", (1, 2, 3)), ("ctx", (2, 4, 6))]
    mask = 8
    while mask < lax.axis_size("ctx"):
        groups.append(("ctx", (mask,)))
        mask *= 2
    for axis, masks in groups:
        got = [value] + [swap(value, axis, m) for m in masks]
        gate = yield value
        if len(got) == 4:
            a, b = got[0] + got[1], got[2] + got[3]
            value = gated(a, gate) + b
        else:
            value = gated(got[0], gate) + got[1]
    yield value


class Stages:
    def __init__(self, stages):
        self.stages, self.value, self.left = stages, next(stages), True

    def step(self, gate):
        try:
            self.value = self.stages.send(gate)
        except StopIteration:
            self.left = False
        return self.value

    def result(self):
        while self.left:
            self.step(None)
        return self.value


def join_halves(mine, other, rows, row_dim, core):
    off, size = half_of(rows)
    low = jnp.where(core == 0, mine, other)
    high = jnp.where(core == 0, other, mine)
    return jnp.concatenate(
        [low, lax.slice_in_dim(high, size - off, size, axis=row_dim)], axis=row_dim
    )


def mm(left, right, dims=NN):
    return lax.dot_general(left, right, dims, preferred_element_type=F32)


def silu_of_half(y):
    return y * (1.0 + jnp.tanh(y))


def loop(count, body, unroll):
    lax.fori_loop(0, count, lambda i, _: (body(i), 0)[1], 0, unroll=unroll)


def full(shape):
    return pl.BlockSpec(shape, lambda s: (0,) * len(shape), pipeline_mode=pl.Buffered(1))


def seq(shape):
    return pl.BlockSpec((None,) + shape, lambda s: (s,) + (0,) * len(shape))


ANY = pl.BlockSpec(memory_space=pl.ANY)


def sds(shape, dtype):
    return jax.ShapeDtypeStruct(shape, dtype)


def rows_at(i, base=0):
    return pl.ds(pl.multiple_of(i * ROWS + base, ROWS), ROWS)


def lanes(tile, width):
    return jnp.concatenate([tile] * (width // 128), axis=1)


def col(ref, j, r, width):
    return lanes(ref[j, r, :], width)


def fold(v):
    t = v[:, 0:128]
    for j in range(1, v.shape[1] // 128):
        t = t + v[:, j * 128 : (j + 1) * 128]
    return t


def eight(v):
    return v[0:8] + v[8:16]


def spread(packs, out_ref, j, row, scale=1.0):
    own, near, far = packs
    me, core = lax.axis_index("dp"), lax.rem(lax.axis_index("ctx"), 2)
    part = out_ref.shape[1] // 4
    for mask, ref in ((0, own), (1 + core, near), (2 - core, far.at[0]), (3, far.at[1])):
        start = pl.multiple_of(jnp.bitwise_xor(me, mask) * part, 8)
        v = ref[...].astype(F32)[row : row + 1, 0:part] * scale
        out_ref[j, pl.ds(start, part), :] = jnp.broadcast_to(v, (128, part)).T


def gathered_row(sums):
    return jnp.sum(sums.T, axis=0, keepdims=True)


def row_stats(count, load, width, length):
    def total(i, a):
        return a + eight(load(i))

    zero = jnp.zeros((8, length), F32)
    a = lax.fori_loop(0, count, total, zero, unroll=5)
    mean = jnp.sum(a, axis=0, keepdims=True) * (1.0 / width)

    def squares(i, a):
        c = load(i) - mean
        return a + eight(c * c)

    a = lax.fori_loop(0, count, squares, zero, unroll=5)
    var = jnp.sum(a, axis=0, keepdims=True) * (1.0 / width)
    return mean, var


def start_load(pieces, dst, sems):
    shard, first, second, other_first, other_second = pieces
    rows = shard.shape[0]
    off, size = half_of(rows)
    me, core = lax.axis_index("dp"), lax.rem(lax.axis_index("ctx"), 2)
    near = jnp.bitwise_xor(me, 1 + core)
    far = jnp.bitwise_xor(me, 2 - core)
    both = jnp.bitwise_xor(me, 3)

    def at(device, half, count):
        return dst.at[pl.ds(pl.multiple_of(device * rows + half * off, 16), count), :]

    batch_one = [
        (shard, at(me, 0, rows)),
        (first.at[0:size], at(near, core, size)),
        (second.at[0, 0:size], at(far, core, size)),
        (second.at[1, 0:size], at(both, core, size)),
    ]
    batch_two = [
        (other_first.at[0:size], at(far, 1 - core, size)),
        (other_second.at[0, 0:size], at(near, 1 - core, size)),
        (other_second.at[1, 0:size], at(both, 1 - core, size)),
    ]
    copies = [
        pltpu.make_async_copy(src, to, sems.at[i])
        for i, (src, to) in enumerate(batch_one + batch_two)
    ]
    for c in copies[:4]:
        c.start()
    return copies


def finish_load(copies):
    for c in copies[:4]:
        c.wait()
    for c in copies[4:]:
        c.start()
    for c in copies[4:]:
        c.wait()


def assemble(shard, pieces, k, wide_s):
    first, second, other_first, other_second = pieces
    rows = shard.shape[0]
    off, _ = half_of(rows)
    me, core = lax.axis_index("dp"), lax.rem(lax.axis_index("ctx"), 2)
    near = jnp.bitwise_xor(me, 1 + core)
    far = jnp.bitwise_xor(me, 2 - core)
    both = jnp.bitwise_xor(me, 3)

    def put(device, half, piece):
        start = pl.ds(pl.multiple_of(device * rows + half * off, 8), piece.shape[0])
        wide_s[start, :] = piece.astype(F32)

    put(me, 0, shard)
    put(near, core, first[k])
    put(far, core, second[0, k])
    put(both, core, second[1, k])
    put(far, 1 - core, other_first[k])
    put(near, 1 - core, other_second[0, k])
    put(both, 1 - core, other_second[1, k])
    return wide_s[...].astype(BF)


def params(mib=60):
    return pltpu.CompilerParams(vmem_limit_bytes=mib * MIB)


def cost(products, entries):
    return pl.CostEstimate(
        flops=40 * products + 800 * entries, bytes_accessed=1, transcendentals=0
    )


def split_grad(acc_ref, keep_ref, send_ref, taps, first_block=None):
    me, core = lax.axis_index("dp"), lax.rem(lax.axis_index("ctx"), 2)
    block = acc_ref.shape[0] // taps
    width = keep_ref.shape[-1]
    rows = block // 4
    off, size = half_of(rows)
    mine = (0, 2 - core, 1 + core, 3)
    theirs = (0, 1 + core, 2 - core, 3)
    for j in range(4):
        for k in range(taps):
            a = jnp.bitwise_xor(me, mine[j]) * rows + core * off + k * block
            b = jnp.bitwise_xor(me, theirs[j]) * rows + (1 - core) * off + k * block
            for ref, begin in ((keep_ref, a), (send_ref, b)):
                v = acc_ref[pl.ds(pl.multiple_of(begin, 8), size), :].astype(BF)
                if taps > 1:
                    ref[j, k] = v
                elif first_block is None:
                    ref[j] = v
                else:
                    for h in range(v.shape[1] // width):
                        ref[j, first_block + h] = v[:, h * width : (h + 1) * width]


def prepare_in_body(*refs):
    w_ref, out_ref, rows_s = refs[0], refs[-2], refs[-1]
    off, size = half_of(w_ref.shape[0])
    core = lax.rem(lax.axis_index("ctx"), 2)
    out_ref[0:size, :] = w_ref[pl.ds(pl.multiple_of(core * off, 16), size), :]
    rows_s[...] = jnp.zeros_like(rows_s)
    for j, ref in enumerate(refs[1:-2]):
        n = ref.shape[0]
        rows_s[j : j + 1, 0:n] = ref[...].astype(F32).reshape(1, n)
    out_ref[size:, :] = rows_s[...].astype(BF)


def prepare_in(weight, vectors):
    rows, inner = weight.shape
    size = half_of(rows)[1]
    assert size % 16 == 0 and max(v.shape[0] for v in vectors) <= inner and len(vectors) <= 16
    vmem = pl.BlockSpec(memory_space=pltpu.VMEM)
    return pl.pallas_call(
        prepare_in_body,
        in_specs=[vmem] * (1 + len(vectors)),
        out_specs=vmem,
        out_shape=sds((size + 16, inner), BF),
        scratch_shapes=[pltpu.VMEM((16, inner), F32)],
        compiler_params=params(),
        name="prepare_in",
    )(weight, *vectors)


def prepare_rest_body(wc_ref, wo_ref, out_ref):
    inner = wc_ref.shape[2]
    off, size = half_of(wc_ref.shape[1])
    core = lax.rem(lax.axis_index("ctx"), 2)
    r = pl.ds(pl.multiple_of(core * off, 16), size)
    for k in range(3):
        out_ref[k] = wc_ref[k, r, :]
    half = wo_ref[r, :]
    out_ref[3] = half[:, 0:inner]
    out_ref[4] = half[:, inner:]


def prepare_rest(weight_conv, weight_out):
    inner = weight_conv.shape[2]
    vmem = pl.BlockSpec(memory_space=pltpu.VMEM)
    return pl.pallas_call(
        prepare_rest_body,
        in_specs=[vmem] * 2,
        out_specs=vmem,
        out_shape=sds((5, half_of(weight_conv.shape[1])[1], inner), BF),
        compiler_params=params(),
        name="prepare_rest",
    )(weight_conv, weight_out)


def vec_specs(packs):
    own, first, second = packs
    inner = own.shape[1]
    at = own.shape[0] // 16 - 1
    row = pl.BlockSpec((16, inner), lambda s: (at, 0))
    return [row, row, pl.BlockSpec((2, 16, inner), lambda s: (0, at, 0))]


def stats_body(x_ref, st_ref, sq_ref):
    wide, length = x_ref.shape

    @pl.when(pl.program_id(0) == 0)
    def _():
        sq_ref[...] = jnp.zeros_like(sq_ref)

    mean, var = row_stats(wide // ROWS, lambda i: x_ref[rows_at(i), :].astype(F32), wide, length)
    st_ref[0:1, :] = mean
    st_ref[1:2, :] = lax.rsqrt(var + EPS)
    sq_ref[0:1, :] += (var + mean * mean) * float(wide)


def input_stats(x):
    seqs, wide, length = x.shape
    return pl.pallas_call(
        stats_body,
        grid=(seqs,),
        in_specs=[seq((wide, length))],
        out_specs=[seq((8, length)), full((8, length))],
        out_shape=[sds((seqs, 8, length), F32), sds((8, length), F32)],
        compiler_params=params(),
        cost_estimate=cost(0, x.size // 4),
        name="input_stats",
    )(x)


def act_body(x_ref, st_ref, v0, v1, v2, a0_ref, vw_s):
    wide, length = x_ref.shape

    @pl.when(pl.program_id(0) == 0)
    def _():
        for j in range(2):
            spread((v0, v1, v2), vw_s, j, j, 0.5)

    mean = st_ref[0:1, :]
    inv = st_ref[1:2, :]

    def act0(i):
        r = rows_at(i)
        y = (x_ref[r, :].astype(F32) - mean) * inv * col(vw_s, 0, r, length)
        a0_ref[r, :] = silu_of_half(y + col(vw_s, 1, r, length)).astype(BF)

    loop(wide // ROWS, act0, 5)


def first_act(x, stats, packs):
    seqs, wide, length = x.shape
    return pl.pallas_call(
        act_body,
        grid=(seqs,),
        in_specs=[seq((wide, length)), seq((8, length))] + vec_specs(packs),
        out_specs=seq((wide, length)),
        out_shape=sds((seqs, wide, length), BF),
        scratch_shapes=[pltpu.VMEM((2, wide, 128), F32)],
        compiler_params=params(),
        cost_estimate=cost(0, x.size // 2),
        name="first_act",
    )(x, stats, *packs)


def first_body(
    a0_ref, p0, p1, p2, p3, p4, v0, v1, v2,
    h1_ref, a1_ref, edge_ref, sq_ref,
    w_s, wt_s, vi_s, sems,
):
    s = pl.program_id(0)
    inner, length = h1_ref.shape

    @pl.when(s == 0)
    def _():
        copies = start_load((p0, p1, p2, p3, p4), w_s, sems)
        sq_ref[...] = jnp.zeros_like(sq_ref)
        for j in range(3):
            spread((v0, v1, v2), vi_s, j, j + 3, (1.0, 0.5, 0.5)[j])
        finish_load(copies)
        wt_s[...] = w_s[...].T

    h1_ref[...] = mm(wt_s[...], a0_ref[...]) + lanes(vi_s[0], length)
    mean1, var1 = row_stats(inner // ROWS, lambda i: h1_ref[rows_at(i), :], inner, length)
    inv1 = lax.rsqrt(var1 + EPS)
    sq_ref[0:1, :] += (var1 + mean1 * mean1) * float(inner)

    def act1(i):
        r = rows_at(i)
        y = (h1_ref[r, :] - mean1) * inv1 * col(vi_s, 1, r, length) + col(vi_s, 2, r, length)
        a1_ref[r, :] = silu_of_half(y).astype(BF)

    loop(inner // ROWS, act1, 5)
    edge_ref[...] = a1_ref[:, length - 128 :].astype(F32).T[120:128, :].astype(BF)


def first(a0, pieces, packs):
    seqs, wide, length = a0.shape
    inner = pieces[0].shape[1]
    return pl.pallas_call(
        first_body,
        grid=(seqs,),
        in_specs=[seq((wide, length))] + [ANY] * 5 + vec_specs(packs),
        out_specs=[seq((inner, length)), seq((inner, length)), seq((8, inner)), full((8, length))],
        out_shape=[
            sds((seqs, inner, length), F32),
            sds((seqs, inner, length), BF),
            sds((seqs, 8, inner), BF),
            sds((8, length), F32),
        ],
        scratch_shapes=[
            pltpu.VMEM((wide, inner), BF),
            pltpu.VMEM((inner, wide), BF),
            pltpu.VMEM((3, inner, 128), F32),
            pltpu.SemaphoreType.DMA((7,)),
        ],
        compiler_params=params(),
        cost_estimate=cost(a0.size * inner, a0.size),
        name="first_product",
    )(a0, *pieces, *packs)


def assemble_body(wc_own, wo_own, f, g, of, og, wc_ref, wct_ref, wo_ref, tap_s):
    inner = wc_ref.shape[1]
    pieces = (f, g, of, og)
    for k in range(3):
        wc_ref[k] = assemble(wc_own[k], pieces, k, tap_s)
    wct_ref[...] = wc_ref[...].reshape(3 * inner, inner).T
    for k in range(2):
        wo_ref[k] = assemble(wo_own[:, k * inner : (k + 1) * inner], pieces, 3 + k, tap_s)


def assemble_weights(own_conv, own_out, pieces):
    inner = own_conv.shape[2]
    vmem = pl.BlockSpec(memory_space=pltpu.VMEM)
    return pl.pallas_call(
        assemble_body,
        in_specs=[vmem] * 6,
        out_specs=[vmem] * 3,
        out_shape=[
            sds((3, inner, inner), BF),
            sds((inner, 3 * inner), BF),
            sds((2, inner, inner), BF),
        ],
        scratch_shapes=[pltpu.VMEM((inner, inner), F32)],
        compiler_params=params(),
        cost_estimate=cost(0, 4 * inner * inner),
        name="assemble_weights",
    )(own_conv, own_out, *pieces)


def transpose_body(w_ref, wt_ref):
    inner = w_ref.shape[1]
    for k in range(2):
        wt_ref[k * inner : (k + 1) * inner, :] = w_ref[k].T


def transposed(w):
    inner = w.shape[1]
    vmem = pl.BlockSpec(memory_space=pltpu.VMEM)
    return pl.pallas_call(
        transpose_body,
        in_specs=[vmem],
        out_specs=vmem,
        out_shape=sds((2 * inner, inner), BF),
        compiler_params=params(),
        name="transpose_out",
    )(w)


def conv_body(
    a1_ref, halo_ref, dy_ref, dyp_ref, mk_ref, wct_ref, wo_ref, v0, v1, v2,
    a2_ref, dh2_ref, edge_ref, sums_ref, bo_ref, sq_ref, keep_ref, send_ref,
    st_s, a2_s, dh_s, h_s, d_s, hl_s, vi_s, sums_s, bo_s, acc_s, out_s, mi_s,
):
    s = pl.program_id(0)
    seqs = pl.num_programs(0) - 1
    inner, length = a1_ref.shape
    wide = dy_ref.shape[0]
    steps = inner // ROWS
    now, then = lax.rem(s, 2), lax.rem(s + 1, 2)

    @pl.when(s == 0)
    def _():
        sq_ref[...] = jnp.zeros_like(sq_ref)
        sums_s[...] = jnp.zeros_like(sums_s)
        bo_s[...] = jnp.zeros_like(bo_s)
        acc_s[...] = jnp.zeros_like(acc_s)
        out_s[...] = jnp.zeros_like(out_s)
        for j in range(3):
            spread((v0, v1, v2), vi_s, j, j + 6, (1.0, 0.5, 0.5)[j])

    @pl.when(s < seqs)
    def _():
        hl_s[...] = jnp.concatenate(
            [jnp.zeros((120, inner), F32), halo_ref[...].astype(F32)], axis=0
        ).T
        m1 = mk_ref[1:2, :]
        m2 = mk_ref[2:3, :]

        def build(i):
            r = rows_at(i)
            b = a1_ref[r, :]
            v = jnp.concatenate([b.astype(F32), hl_s[r, :]], axis=1)
            st_s[now, r, :] = b
            st_s[now, rows_at(i, inner), :] = (pltpu.roll(v, 2, 1)[:, 0:length] * m1).astype(BF)
            st_s[now, rows_at(i, 2 * inner), :] = (pltpu.roll(v, 4, 1)[:, 0:length] * m2).astype(BF)

        loop(steps, build, 10)
        h_s[...] = mm(wct_ref[...], st_s[now]) + lanes(vi_s[0], length)
        d_s[...] = mm(wo_ref[0], dy_ref[0:inner, :]) + mm(wo_ref[1], dy_ref[inner:, :])

        mean, var = row_stats(steps, lambda i: h_s[rows_at(i), :], inner, length)
        mi_s[0:1, :] = mean
        mi_s[1:2, :] = lax.rsqrt(var + EPS)
        sq_ref[0:1, :] += (var + mean * mean) * float(inner)

    mean = mi_s[0:1, :]
    inv = mi_s[1:2, :]
    zero = jnp.zeros((8, length), F32)

    def back(i, acc):
        r = rows_at(i)
        n = (h_s[r, :] - mean) * inv
        g = col(vi_s, 1, r, length)
        y = n * g + col(vi_s, 2, r, length)
        t = jnp.tanh(y)
        up = 1.0 + t
        a2 = (y * up).astype(BF)
        a2_ref[r, :] = a2
        a2_s[now, r, :] = a2
        e = d_s[r, :] * (up * (1.0 + y * (1.0 - t)))
        q = e * g
        d_s[r, :] = q
        h_s[r, :] = n
        sums_s[0, r, :] += fold(e * n)
        sums_s[1, r, :] += fold(e)
        return acc[0] + eight(q), acc[1] + eight(q * n)

    def means(acc):
        return [jnp.sum(a, axis=0, keepdims=True) * (1.0 / inner) for a in acc]

    def last(i, mq, mqn):
        r = rows_at(i)
        dh = ((d_s[r, :] - mq - h_s[r, :] * mqn) * inv).astype(BF)
        dh2_ref[r, :] = dh
        dh_s[now, r, :] = dh
        sums_s[2, r, :] += fold(dh.astype(F32))

    def block(j):
        return pl.ds(pl.multiple_of(j * inner, 16), inner)

    def grad_tap(j):
        acc_s[block(j), :] += mm(st_s[then, block(j), :], dh_s[then], NT)

    def grad_out(k):
        r = pl.ds(pl.multiple_of(k * (inner // 2), 16), inner // 2)
        out_s[r, :] += mm(a2_s[then, r, :], dyp_ref[...], NT)

    def bias(i):
        r = rows_at(i)
        bo_s[r, :] += fold(dyp_ref[r, :].astype(F32))

    @pl.when(s == 0)
    def _():
        acc = lax.fori_loop(0, steps, back, (zero, zero), unroll=5)
        mq, mqn = means(acc)
        loop(steps, lambda i: last(i, mq, mqn), 5)

    @pl.when(jnp.logical_and(s > 0, s < seqs))
    def _():
        each, some = steps // 3, wide // ROWS // 3
        acc = lax.fori_loop(3 * each, steps, back, (zero, zero), unroll=True)
        for i in range(3 * some, wide // ROWS):
            bias(i)

        def tap(j, acc):
            grad_tap(j)
            for c in range(each):
                acc = back(j * each + c, acc)
            for c in range(some):
                bias(j * some + c)
            return acc

        mq, mqn = means(lax.fori_loop(0, 3, tap, acc))

        def out(k):
            grad_out(k)
            for c in range(steps // 2):
                last(k * (steps // 2) + c, mq, mqn)

        loop(2, out, 1)

    @pl.when(s < seqs)
    def _():
        edge_ref[...] = dh2_ref[:, 0:128].astype(F32).T[0:8, :].astype(BF)

    @pl.when(s == seqs)
    def _():
        loop(3, grad_tap, 1)
        loop(2, grad_out, 1)
        loop(wide // ROWS, bias, 5)
        for j in range(3):
            sums_ref[j : j + 1, :] = gathered_row(sums_s[j]) * (0.5, 0.5, 1.0)[j]
        bo_ref[0:1, :] = gathered_row(bo_s[...])
        split_grad(acc_s, keep_ref, send_ref, 3)
        split_grad(out_s, keep_ref, send_ref, 1, 3)


def conv(a1, halo, dy, mk, wct, wo, packs):
    seqs, inner, length = a1.shape
    wide = dy.shape[1]
    assert inner % (2 * ROWS) == 0
    size = half_of(inner // 4)[1]

    this, previous = functools.partial(this_seq, seqs), previous_seq

    return pl.pallas_call(
        conv_body,
        grid=(seqs + 1,),
        in_specs=[
            this((inner, length)),
            this((8, inner)),
            this((wide, length)),
            previous((wide, length)),
            this((8, length)),
        ]
        + [full(p.shape) for p in (wct, wo)]
        + vec_specs(packs),
        out_specs=[
            this((inner, length)),
            this((inner, length)),
            this((8, inner)),
            full((8, inner)),
            full((8, wide)),
            full((8, length)),
            full((4, 5, size, inner)),
            full((4, 5, size, inner)),
        ],
        out_shape=[
            sds((seqs, inner, length), BF),
            sds((seqs, inner, length), BF),
            sds((seqs, 8, inner), BF),
            sds((8, inner), F32),
            sds((8, wide), F32),
            sds((8, length), F32),
            sds((4, 5, size, inner), BF),
            sds((4, 5, size, inner), BF),
        ],
        scratch_shapes=[
            pltpu.VMEM((2, 3 * inner, length), BF),
            pltpu.VMEM((2, inner, length), BF),
            pltpu.VMEM((2, inner, length), BF),
            pltpu.VMEM((inner, length), F32),
            pltpu.VMEM((inner, length), F32),
            pltpu.VMEM((inner, 128), F32),
            pltpu.VMEM((3, inner, 128), F32),
            pltpu.VMEM((3, inner, 128), F32),
            pltpu.VMEM((wide, 128), F32),
            pltpu.VMEM((3 * inner, inner), F32),
            pltpu.VMEM((inner, wide), F32),
            pltpu.VMEM((8, length), F32),
        ],
        compiler_params=params(),
        cost_estimate=cost(a1.size * (6 * inner + 2 * wide), 2 * a1.size),
        name="conv_and_third_norm",
    )(a1, halo, dy, dy, mk, wct, wo, *packs)


def grad_body(a_ref, b_ref, keep_ref, send_ref, acc_s):
    s = pl.program_id(0)

    @pl.when(s == 0)
    def _():
        acc_s[...] = mm(a_ref[...], b_ref[...], NT)

    @pl.when(s > 0)
    def _():
        acc_s[...] += mm(a_ref[...], b_ref[...], NT)

    @pl.when(s == pl.num_programs(0) - 1)
    def _():
        split_grad(acc_s, keep_ref, send_ref, 1)


def grad(a, b, name):
    seqs, m, length = a.shape
    n = b.shape[1]
    size = half_of(m // 4)[1]
    return pl.pallas_call(
        grad_body,
        grid=(seqs,),
        in_specs=[seq((m, length)), seq((n, length))],
        out_specs=[full((4, size, n)), full((4, size, n))],
        out_shape=[sds((4, size, n), BF), sds((4, size, n), BF)],
        scratch_shapes=[pltpu.VMEM((m, n), F32)],
        compiler_params=params(),
        cost_estimate=cost(a.size * n, 0),
        name=name,
    )(a, b)


def shift_back(dh2_ref, halo_ref, mk_ref, hl_s, t_s):
    inner, length = dh2_ref.shape
    hl_s[...] = jnp.concatenate(
        [halo_ref[...].astype(F32), jnp.zeros((120, inner), F32)], axis=0
    ).T
    f1 = mk_ref[3:4, :]
    f2 = mk_ref[4:5, :]

    def build(i):
        r = rows_at(i)
        b = dh2_ref[r, :]
        v = jnp.concatenate([b.astype(F32), hl_s[r, :]], axis=1)
        t_s[0, r, :] = b
        t_s[1, r, :] = (pltpu.roll(v, length + 126, 1)[:, 0:length] * f1).astype(BF)
        t_s[2, r, :] = (pltpu.roll(v, length + 124, 1)[:, 0:length] * f2).astype(BF)

    loop(inner // ROWS, build, 10)


def conv_back_body(
    dh2_ref, halo_ref, h1_ref, mk_ref, wc_ref, v0, v1, v2,
    dh1_ref, sums_ref,
    t_s, d_s, n_s, hl_s, vi_s, sums_s,
):
    s = pl.program_id(0)
    seqs = pl.num_programs(0) - 1
    inner, length = dh2_ref.shape
    steps = inner // ROWS
    now, then = lax.rem(s, 2), lax.rem(s + 1, 2)

    @pl.when(s == 0)
    def _():
        sums_s[...] = jnp.zeros_like(sums_s)
        for j in range(2):
            spread((v0, v1, v2), vi_s, j, j + 4, 0.5)

    @pl.when(s < seqs)
    def _():
        shift_back(dh2_ref, halo_ref, mk_ref, hl_s, t_s)

    def back_of(mean, inv):
        def back(i, acc):
            r = rows_at(i)
            n = (h1_ref[r, :] - mean) * inv
            g = col(vi_s, 0, r, length)
            y = n * g + col(vi_s, 1, r, length)
            t = jnp.tanh(y)
            e = d_s[then, r, :] * ((1.0 + t) * (1.0 + y * (1.0 - t)))
            q = e * g
            d_s[then, r, :] = q
            n_s[r, :] = n
            sums_s[0, r, :] += fold(e * n)
            sums_s[1, r, :] += fold(e)
            return acc[0] + eight(q), acc[1] + eight(q * n)

        return back

    def close(acc, inv):
        mq, mqn = [jnp.sum(a, axis=0, keepdims=True) * (1.0 / inner) for a in acc]

        def last(i):
            r = rows_at(i)
            dh = ((d_s[then, r, :] - mq - n_s[r, :] * mqn) * inv).astype(BF)
            dh1_ref[r, :] = dh
            sums_s[2, r, :] += fold(dh.astype(F32))

        loop(steps, last, 5)

    def stats():
        mean, var = row_stats(steps, lambda i: h1_ref[rows_at(i), :], inner, length)
        return mean, lax.rsqrt(var + EPS)

    zero = jnp.zeros((8, length), F32)

    @pl.when(s == 0)
    def _():
        d_s[now] = mm(wc_ref[0], t_s[0]) + mm(wc_ref[1], t_s[1]) + mm(wc_ref[2], t_s[2])

    @pl.when(jnp.logical_and(s > 0, s < seqs))
    def _():
        mean, inv = stats()
        back = back_of(mean, inv)
        each = steps // 3
        acc = lax.fori_loop(3 * each, steps, back, (zero, zero), unroll=True)
        for k in range(3):
            part = mm(wc_ref[k], t_s[k])
            d_s[now] = part if k == 0 else d_s[now] + part
            for c in range(each):
                acc = back(k * each + c, acc)
        close(acc, inv)

    @pl.when(s == seqs)
    def _():
        mean, inv = stats()
        close(lax.fori_loop(0, steps, back_of(mean, inv), (zero, zero), unroll=5), inv)
        for j in range(3):
            sums_ref[j : j + 1, :] = gathered_row(sums_s[j]) * (0.5, 0.5, 1.0)[j]


def seq_from(begin, shape):
    return pl.BlockSpec((None,) + shape, lambda s: (s + begin,) + (0,) * len(shape))


def this_seq(seqs, shape):
    return pl.BlockSpec((None,) + shape, lambda s: (jnp.minimum(s, seqs - 1),) + (0,) * len(shape))


def previous_seq(shape):
    return pl.BlockSpec((None,) + shape, lambda s: (jnp.maximum(s - 1, 0),) + (0,) * len(shape))


def conv_back(dh2, halo, h1, mk, wc, packs):
    seqs, inner, length = dh2.shape
    return pl.pallas_call(
        conv_back_body,
        grid=(seqs + 1,),
        in_specs=[
            this_seq(seqs, (inner, length)),
            this_seq(seqs, (8, inner)),
            previous_seq((inner, length)),
            this_seq(seqs, (8, length)),
            full(wc.shape),
        ]
        + vec_specs(packs),
        out_specs=[previous_seq((inner, length)), full((8, inner))],
        out_shape=[sds((seqs, inner, length), BF), sds((8, inner), F32)],
        scratch_shapes=[
            pltpu.VMEM((3, inner, length), BF),
            pltpu.VMEM((2, inner, length), F32),
            pltpu.VMEM((inner, length), F32),
            pltpu.VMEM((inner, 128), F32),
            pltpu.VMEM((2, inner, 128), F32),
            pltpu.VMEM((3, inner, 128), F32),
        ],
        compiler_params=params(),
        cost_estimate=cost(dh2.size * 3 * inner, 2 * dh2.size),
        name="conv_backward",
    )(dh2, halo, h1, mk, wc, *packs)


def stream_body(
    x_ref, st_ref, dy_ref, dh1_ref, p0, p1, p2, p3, p4, v0, v1, v2, before_ref,
    gs_ref, sums_ref,
    w_s, d_s, n_s, vw_s, sums_s, sems,
):
    s = pl.program_id(0)
    wide, length = x_ref.shape
    steps = wide // ROWS

    @pl.when(s == 0)
    def _():
        copies = start_load((p0, p1, p2, p3, p4), w_s, sems)
        sums_s[...] = jnp.zeros_like(sums_s)
        for j in range(2):
            spread((v0, v1, v2), vw_s, j, j, 0.5)
        finish_load(copies)

    d_s[...] = mm(w_s[...], dh1_ref[...])
    mean = st_ref[0:1, :]
    inv = st_ref[1:2, :]

    def back(i, acc):
        r = rows_at(i)
        n = (x_ref[r, :].astype(F32) - mean) * inv
        g = col(vw_s, 0, r, length)
        y = n * g + col(vw_s, 1, r, length)
        t = jnp.tanh(y)
        e = d_s[r, :] * ((1.0 + t) * (1.0 + y * (1.0 - t)))
        q = e * g
        d_s[r, :] = q
        n_s[r, :] = n
        sums_s[0, r, :] += fold(e * n)
        sums_s[1, r, :] += fold(e)
        return acc[0] + eight(q), acc[1] + eight(q * n)

    zero = jnp.zeros((8, length), F32)
    qa, qn = lax.fori_loop(0, steps, back, (zero, zero), unroll=5)
    mq = jnp.sum(qa, axis=0, keepdims=True) * (1.0 / wide)
    mqn = jnp.sum(qn, axis=0, keepdims=True) * (1.0 / wide)

    def last(i):
        r = rows_at(i)
        gs = dy_ref[r, :].astype(F32) + (d_s[r, :] - mq - n_s[r, :] * mqn) * inv
        gs_ref[r, :] = gs.astype(BF)

    loop(steps, last, 5)

    @pl.when(s == pl.num_programs(0) - 1)
    def _():
        for j in range(2):
            sums_ref[j : j + 1, :] = gathered_row(sums_s[j]) * 0.5


def stream_back(x, stats, dy, dh1, pieces, packs, begin, count, before):
    seqs, wide, length = x.shape
    inner = dh1.shape[1]
    aliases = {12: 0} if begin else {}
    return pl.pallas_call(
        stream_body,
        grid=(count,),
        in_specs=[
            seq_from(begin, (wide, length)),
            seq_from(begin, (8, length)),
            seq_from(begin, (wide, length)),
            seq_from(begin, (inner, length)),
        ]
        + [ANY] * 5
        + vec_specs(packs)
        + [ANY],
        out_specs=[seq_from(begin, (wide, length)), full((8, wide))],
        out_shape=[sds((seqs, wide, length), BF), sds((8, wide), F32)],
        input_output_aliases=aliases,
        scratch_shapes=[
            pltpu.VMEM((wide, inner), BF),
            pltpu.VMEM((wide, length), F32),
            pltpu.VMEM((wide, length), F32),
            pltpu.VMEM((2, wide, 128), F32),
            pltpu.VMEM((2, wide, 128), F32),
            pltpu.SemaphoreType.DMA((7,)),
        ],
        compiler_params=params(),
        cost_estimate=cost(dh1.size * wide * count // seqs, x.size * count // seqs),
        name="grad_stream",
    )(x, stats, dy, dh1, *pieces, *packs, before)


def output_body(x_ref, a2_ref, wt_ref, v0, v1, v2, before_ref, out_ref, sq_ref, o_s, vw_s):
    s = pl.program_id(0)
    wide, length = x_ref.shape

    @pl.when(s == 0)
    def _():
        sq_ref[...] = jnp.zeros_like(sq_ref)
        spread((v0, v1, v2), vw_s, 0, 2)

    o_s[...] = mm(wt_ref[...], a2_ref[...])

    def close(i, acc):
        r = rows_at(i)
        branch = o_s[r, :] + col(vw_s, 0, r, length)
        result = x_ref[r, :].astype(F32) + branch
        out_ref[r, :] = result.astype(BF)
        return acc[0] + eight(branch * branch), acc[1] + eight(result * result)

    zero = jnp.zeros((8, length), F32)
    b2, r2 = lax.fori_loop(0, wide // ROWS, close, (zero, zero), unroll=5)
    sq_ref[0:1, :] += jnp.sum(b2, axis=0, keepdims=True)
    sq_ref[1:2, :] += jnp.sum(r2, axis=0, keepdims=True)


def output_of(x, a2, wt, packs, begin, count, before):
    seqs, wide, length = x.shape
    inner = a2.shape[1]
    aliases = {6: 0} if begin else {}
    return pl.pallas_call(
        output_body,
        grid=(count,),
        in_specs=[seq_from(begin, (wide, length)), seq_from(begin, (inner, length))]
        + [full(wt.shape)]
        + vec_specs(packs)
        + [ANY],
        out_specs=[seq_from(begin, (wide, length)), full((8, length))],
        out_shape=[sds((seqs, wide, length), BF), sds((8, length), F32)],
        input_output_aliases=aliases,
        scratch_shapes=[
            pltpu.VMEM((wide, length), F32),
            pltpu.VMEM((1, wide, 128), F32),
        ],
        compiler_params=params(),
        cost_estimate=cost(a2.size * wide * count // seqs, x.size * count // (4 * seqs)),
        name="block_output",
    )(x, a2, wt, *packs, before)


def pack_sums_body(n_one, n_zero, n_out, *refs):
    refs, out_ref = list(refs[:-1]), refs[-1]
    bo, two, q_in, q_one, q_two = (refs.pop(0) for _ in range(5))
    one = sum(refs.pop(0)[0:3, :] for _ in range(n_one))
    zero = sum(refs.pop(0)[0:2, :] for _ in range(n_zero))
    out = sum(refs.pop(0)[0:2, :] for _ in range(n_out))
    inner = two.shape[1]
    out_ref[...] = jnp.zeros_like(out_ref)
    out_ref[0:2, :] = zero
    out_ref[2:3, :] = bo[0:1, :]
    out_ref[3:6, 0:inner] = one
    out_ref[3:6, inner : 2 * inner] = two[0:3, :]
    rows = (q_in[0:1, :], out[1:2, :], q_one[0:1, :], q_two[0:1, :], out[0:1, :])
    for j, row in enumerate(rows):
        total = jnp.sum(row, axis=1, keepdims=True)
        out_ref[6:7, j * 128 : (j + 1) * 128] = jnp.broadcast_to(total, (1, 128))


def pack_sums(bo, two, q_in, q_one, q_two, ones, zeros, outs):
    vmem = pl.BlockSpec(memory_space=pltpu.VMEM)
    args = (bo, two, q_in, q_one, q_two, *ones, *zeros, *outs)
    return pl.pallas_call(
        functools.partial(pack_sums_body, len(ones), len(zeros), len(outs)),
        in_specs=[vmem] * len(args),
        out_specs=vmem,
        out_shape=sds((8, bo.shape[1]), F32),
        compiler_params=params(16),
        name="pack_sums",
    )(*args)


def join_rest_body(mine_ref, other_ref, conv_ref, out_ref):
    core = lax.rem(lax.axis_index("ctx"), 2)
    rows, inner = conv_ref.shape[1:]
    off, size = half_of(rows)
    for k in range(5):
        a, b = mine_ref[k], other_ref[k]
        low = jnp.where(core == 0, a, b).astype(F32)
        high = jnp.where(core == 0, b, a).astype(F32)[size - off :]
        if k < 3:
            conv_ref[k, 0:size, :] = low
            conv_ref[k, size:rows, :] = high
        else:
            out_ref[0:size, (k - 3) * inner : (k - 2) * inner] = low
            out_ref[size:rows, (k - 3) * inner : (k - 2) * inner] = high


def join_rest(mine, other, rows):
    inner = mine.shape[2]
    vmem = pl.BlockSpec(memory_space=pltpu.VMEM)
    return pl.pallas_call(
        join_rest_body,
        in_specs=[vmem] * 2,
        out_specs=[vmem] * 2,
        out_shape=[sds((3, rows, inner), F32), sds((rows, 2 * inner), F32)],
        compiler_params=params(32),
        name="join_rest",
    )(mine, other)


def unpack_body(counts, s_ref, *outs):
    me = lax.axis_index("dp")
    wide = s_ref.shape[1]
    inner = wide // 2

    def part(row, begin, size):
        v = s_ref[row : row + 1, begin : begin + size]
        for d in range(1, 4):
            at = begin + d * size
            v = jnp.where(me == d, s_ref[row : row + 1, at : at + size], v)
        return v.reshape(size)

    for j in range(3):
        outs[j][...] = part(j, 0, wide // 4)
    for j in range(6):
        outs[3 + j][...] = part(3 + j % 3, (j // 3) * inner, inner // 4)
    for j, count in enumerate(counts):
        outs[9 + j][...] = jnp.sqrt(s_ref[6:7, j * 128 : (j + 1) * 128] / count)


def unpack_sums(sums, counts):
    wide = sums.shape[1]
    vmem = pl.BlockSpec(memory_space=pltpu.VMEM)
    return pl.pallas_call(
        functools.partial(unpack_body, counts),
        in_specs=[vmem],
        out_specs=[vmem] * 14,
        out_shape=[sds((wide // 4,), F32)] * 3
        + [sds((wide // 8,), F32)] * 6
        + [sds((1, 128), F32)] * 5,
        compiler_params=params(16),
        name="unpack_sums",
    )(sums)


def local(
    stream, segments, cotangent, gain_zero, shift_zero, weight_in, bias_in, gain_one, shift_one,
    weight_conv, bias_conv, gain_two, shift_two, weight_out, bias_out,
):
    n_dp, n_ctx = lax.axis_size("dp"), lax.axis_size("ctx")
    assert n_dp == 4 and n_ctx & (n_ctx - 1) == 0
    me, place = lax.axis_index("dp"), lax.axis_index("ctx")
    core = place % 2
    seqs, length, wide = stream.shape
    inner = weight_conv.shape[2]
    part_w, part_i = gain_zero.shape[0], bias_in.shape[0]

    x = jnp.swapaxes(stream, 1, 2)
    dy = jnp.swapaxes(cotangent, 1, 2)

    half_in = prepare_in(
        weight_in,
        [gain_zero, shift_zero, bias_out, bias_in, gain_one, shift_one, bias_conv, gain_two, shift_two],
    )
    part_in = gather_halves(half_in)
    sent = next(part_in)
    rest_half = prepare_rest(after(weight_conv, sent), weight_out)
    sent = part_in.send(rest_half)
    stats, sq_in = input_stats(after(x, sent))
    came = part_in.send(sq_in)
    part_rest = gather_halves(after(rest_half, came))
    sent = next(part_rest)
    piece_in = (weight_in, *next(part_in))
    packs = (half_in, *piece_in[1:3])
    act_zero = first_act(x, after(stats, sent), packs)
    sent = part_rest.send(act_zero)

    padded = jnp.pad(segments, ((0, 0), (4, 4)), constant_values=-1)
    near_segs = lax.dynamic_slice_in_dim(padded, place * length, length + 8, 1)
    here = near_segs[:, 4 : 4 + length]
    same = [(near_segs[:, 4 + j : 4 + j + length] == here).astype(F32) for j in (0, -2, -4, 2, 4)]
    masks = jnp.stack(same + same[:3], axis=1)

    hidden_one, act_one, edge, sq_one = first(
        act_zero, piece_in, (after(half_in, sent, masks), *packs[1:])
    )
    halo = shifted(edge, 1)
    part_rest.send(sq_one)
    full_conv, full_conv_t, full_out = assemble_weights(
        weight_conv, weight_out, next(part_rest)
    )
    act_two, d_hidden_two, edge_back, sums_two, sum_bo, sq_two, keep, send = conv(
        act_one, halo, dy, masks, full_conv_t, full_out, packs
    )
    halo_back = shifted(edge_back, -1)
    sum_rest = Stages(sum_shards(keep, send, True))
    own = after(half_in, sum_rest.value)
    full_out_t = transposed(after(full_out, edge_back))
    ones, zeros, outs = [], [], []
    output = grad_x = stats

    def run(what, begin, end):
        nonlocal output, grad_x
        vecs = (own, *packs[1:])
        if what == "out":
            output, sums = output_of(x, act_two, full_out_t, vecs, begin, end - begin, output)
            outs.append(sums)
        else:
            grad_x, sums = stream_back(
                x, stats, dy, d_hidden_one, piece_in, vecs, begin, end - begin, grad_x
            )
            zeros.append(sums)
        return sums

    sums = run("out", 0, 1)
    own = after(own, sum_rest.step(sums))
    d_hidden_one, sums = conv_back(
        d_hidden_two, halo_back, hidden_one, masks, full_conv, (own, *packs[1:])
    )
    ones.append(sums)
    own = after(own, sum_rest.step(sums))
    keep_in, send_in = grad(act_zero, after(d_hidden_one, own), "grad_weight_in")
    sum_in = Stages(sum_shards(keep_in, send_in, False))
    own = after(own, sum_in.value, sum_rest.step(send_in))
    sums = run("out", 1, 2)
    own = after(own, sum_in.step(sums))
    sums = run("stream", 0, 1)
    own = after(own, sum_in.step(sums), sum_rest.step(sums))
    sums = run("out", 2, seqs)
    own = after(own, sum_in.step(sums), sum_rest.step(sums))
    sums = run("stream", 1, 2)
    own = after(own, sum_in.step(sums), sum_rest.step(sums))
    sums = run("stream", 2, seqs)
    sum_rest.step(sums)
    sums = pack_sums(after(sum_bo, sum_in.step(sums)), sums_two, sq_in, sq_one, sq_two, ones, zeros, outs)
    count = float(seqs * length * n_dp * n_ctx)
    total = Stages(sum_all(sums))
    grad_weight_conv, grad_weight_out = join_rest(*sum_rest.result(), part_i)
    grad_weight_in = join_halves(*sum_in.result(), part_w, 0, core)
    total.step(None)
    total.step((grad_weight_out, grad_weight_in))
    sums = total.result()
    totals = unpack_sums(
        sums, (count * wide, count * wide, count * inner, count * inner, count * wide)
    )
    grad_gain_zero, grad_shift_zero, grad_bias_out = totals[0:3]
    grad_gain_one, grad_shift_one, grad_bias_in = totals[3:6]
    grad_gain_two, grad_shift_two, grad_bias_conv = totals[6:9]
    rms_in, rms_out, rms_hidden_one, rms_hidden_two, rms_branch = (v[0, 0] for v in totals[9:])
    return (
        jnp.swapaxes(output, 1, 2),
        jnp.swapaxes(grad_x, 1, 2),
        grad_gain_zero,
        grad_shift_zero,
        grad_weight_in,
        grad_bias_in,
        grad_gain_one,
        grad_shift_one,
        grad_weight_conv,
        grad_bias_conv,
        grad_gain_two,
        grad_shift_two,
        grad_weight_out,
        grad_bias_out,
        rms_in,
        rms_out,
        rms_hidden_one,
        rms_hidden_two,
        rms_branch,
    )


def solution(mesh):
    placed = (
        P("dp", "ctx", None),
        P("dp", None),
        P("dp", "ctx", None),
        P("dp"),
        P("dp"),
        P("dp", None),
        P("dp"),
        P("dp"),
        P("dp"),
        P(None, "dp", None),
        P("dp"),
        P("dp"),
        P("dp"),
        P("dp", None),
        P("dp"),
    )
    return jax.shard_map(
        local,
        mesh=mesh,
        in_specs=placed,
        out_specs=(
            P("dp", "ctx", None),
            P("dp", "ctx", None),
            P("dp"),
            P("dp"),
            P("dp", None),
            P("dp"),
            P("dp"),
            P("dp"),
            P(None, "dp", None),
            P("dp"),
            P("dp"),
            P("dp"),
            P("dp", None),
            P("dp"),
            P(),
            P(),
            P(),
            P(),
            P(),
        ),
        check_vma=False,
    )
```

```python
import functools

import jax
import jax.numpy as jnp
from jax import lax
from jax.experimental import pallas as pl
from jax.experimental.pallas import tpu as pltpu
from jax.sharding import PartitionSpec as P

F32 = jnp.float32
BF = jnp.bfloat16
EPS = 1e-05
ROWS = 16
NN = (((1,), (0,)), ((), ()))
NT = (((1,), (1,)), ((), ()))
MIB = 1024 * 1024


def by_core(value, even_mask, odd_mask):
    n_dp, n_ctx = lax.axis_size("dp"), lax.axis_size("ctx")
    masks = (even_mask, odd_mask)
    pairs = [
        (d * n_ctx + t, (d ^ masks[t % 2]) * n_ctx + t) for d in range(n_dp) for t in range(n_ctx)
    ]
    return lax.ppermute(value, ("dp", "ctx"), pairs)


def swap(value, axis, mask):
    return lax.ppermute(value, axis, [(i, i ^ mask) for i in range(lax.axis_size(axis))])


def shifted(value, by):
    size = lax.axis_size("ctx")
    return lax.ppermute(value, "ctx", [(i, i + by) for i in range(size) if 0 <= i + by < size])


def half_of(rows):
    off = rows // 2 // 16 * 16
    return off, rows - off


def gated(value, gate):
    return value if gate is None else lax.optimization_barrier((value, gate))[0]


def after(value, *others):
    return lax.optimization_barrier((value, *others))[0]


def gather_halves(half):
    first = by_core(half, 1, 2)
    gate = yield half
    sent = jnp.stack([half, gated(first, gate)])
    second = by_core(sent, 2, 1)
    gate = yield sent
    second = gated(second, gate)
    other_first = swap(first, "ctx", 1)
    other_second = swap(second, "ctx", 1)
    yield second
    yield first, second, other_first, other_second


def halved(value, bit):
    rows = value.shape[1]
    off, size = parts_of(rows)
    keep = lax.dynamic_slice_in_dim(value, bit * off, size, 1)
    return keep, lax.dynamic_slice_in_dim(value, (1 - bit) * off, size, 1)


def parts_of(rows):
    off = rows // 2 // 8 * 8
    return off, rows - off


def joined(mine, other, bit, rows):
    off, size = parts_of(rows)
    low = jnp.where(bit == 0, mine, other)
    high = jnp.where(bit == 0, other, mine)
    return jnp.concatenate([low, high[:, size - off :]], axis=1)


def sum_shards(keep, send, halving):
    got = swap(send, "ctx", 1)
    gate = yield send
    got = gated(got, gate)
    sent = (keep[2:4].astype(F32) + got[2:4].astype(F32)).astype(BF)
    one = by_core(sent, 1, 2)
    gate = yield sent
    one = gated(one, gate)
    sent = (keep[1].astype(F32) + got[1].astype(F32) + one[1].astype(F32)).astype(BF)
    two = by_core(sent, 2, 1)
    gate = yield sent
    two = gated(two, gate)
    part = keep[0].astype(F32) + got[0].astype(F32) + one[0].astype(F32) + two.astype(F32)
    place = lax.axis_index("ctx")
    masks = [1 << b for b in range(1, (lax.axis_size("ctx") - 1).bit_length())]
    split = [(mask, (place // mask) % 2) for mask in masks[: 2 if halving else 0]]
    sizes = []
    for mask, bit in split:
        sizes.append(part.shape[1])
        part, sent = halved(part, bit)
        sent = sent.astype(BF)
        came = swap(sent, "ctx", mask)
        gate = yield sent
        part = part + gated(came, gate).astype(F32)
    for mask in masks[len(split) :]:
        sent = part.astype(BF)
        came = swap(sent, "ctx", mask)
        gate = yield sent
        part = sent.astype(F32) + gated(came, gate).astype(F32)
    for mask, bit in split[::-1]:
        sent = part.astype(BF)
        came = swap(sent, "ctx", mask)
        gate = yield sent
        part = joined(sent, gated(came, gate), bit, sizes.pop())
    other = swap(part, "ctx", 1)
    gate = yield part
    yield part, gated(other, gate)


def sum_all(value):
    got = swap(value, "ctx", 1)
    gate = yield value
    value = value + gated(got, gate)
    groups = [("dp", (1, 2, 3)), ("ctx", (2, 4, 6))]
    mask = 8
    while mask < lax.axis_size("ctx"):
        groups.append(("ctx", (mask,)))
        mask *= 2
    for axis, masks in groups:
        got = [value] + [swap(value, axis, m) for m in masks]
        gate = yield value
        if len(got) == 4:
            a, b = got[0] + got[1], got[2] + got[3]
            value = gated(a, gate) + b
        else:
            value = gated(got[0], gate) + got[1]
    yield value


class Stages:
    def __init__(self, stages):
        self.stages, self.value, self.left = stages, next(stages), True

    def step(self, gate):
        try:
            self.value = self.stages.send(gate)
        except StopIteration:
            self.left = False
        return self.value

    def result(self):
        while self.left:
            self.step(None)
        return self.value


def mm(left, right, dims=NN):
    return lax.dot_general(left, right, dims, preferred_element_type=F32)


def silu_of_half(y):
    return y * (1.0 + jnp.tanh(y))


def loop(count, body, unroll):
    lax.fori_loop(0, count, lambda i, _: (body(i), 0)[1], 0, unroll=unroll)


def full(shape):
    return pl.BlockSpec(shape, lambda s: (0,) * len(shape), pipeline_mode=pl.Buffered(1))


def seq(shape):
    return pl.BlockSpec((None,) + shape, lambda s: (s,) + (0,) * len(shape))


ANY = pl.BlockSpec(memory_space=pl.ANY)


def sds(shape, dtype):
    return jax.ShapeDtypeStruct(shape, dtype)


def rows_at(i, base=0):
    return pl.ds(pl.multiple_of(i * ROWS + base, ROWS), ROWS)


def lanes(tile, width):
    return jnp.concatenate([tile] * (width // 128), axis=1)


def col(ref, j, r, width):
    return lanes(ref[j, r, :], width)


def fold(v):
    t = v[:, 0:128]
    for j in range(1, v.shape[1] // 128):
        t = t + v[:, j * 128 : (j + 1) * 128]
    return t


def eight(v):
    return v[0:8] + v[8:16]


def spread(packs, out_ref, j, row, scale=1.0):
    own, near, far = packs
    me, core = lax.axis_index("dp"), lax.rem(lax.axis_index("ctx"), 2)
    part = out_ref.shape[1] // 4
    for mask, ref in ((0, own), (1 + core, near), (2 - core, far.at[0]), (3, far.at[1])):
        start = pl.multiple_of(jnp.bitwise_xor(me, mask) * part, 8)
        v = ref[...].astype(F32)[row : row + 1, 0:part] * scale
        out_ref[j, pl.ds(start, part), :] = jnp.broadcast_to(v, (128, part)).T


def gathered_row(sums):
    return jnp.sum(sums.T, axis=0, keepdims=True)


def row_stats(count, load, width, length):
    def total(i, a):
        return a + eight(load(i))

    zero = jnp.zeros((8, length), F32)
    a = lax.fori_loop(0, count, total, zero, unroll=5)
    mean = jnp.sum(a, axis=0, keepdims=True) * (1.0 / width)

    def squares(i, a):
        c = load(i) - mean
        return a + eight(c * c)

    a = lax.fori_loop(0, count, squares, zero, unroll=5)
    var = jnp.sum(a, axis=0, keepdims=True) * (1.0 / width)
    return mean, var


def start_load(pieces, dst, sems):
    shard, first, second, other_first, other_second = pieces
    rows = shard.shape[0]
    off, size = half_of(rows)
    me, core = lax.axis_index("dp"), lax.rem(lax.axis_index("ctx"), 2)
    near = jnp.bitwise_xor(me, 1 + core)
    far = jnp.bitwise_xor(me, 2 - core)
    both = jnp.bitwise_xor(me, 3)

    def at(device, half, count):
        return dst.at[pl.ds(pl.multiple_of(device * rows + half * off, 16), count), :]

    batch_one = [
        (shard, at(me, 0, rows)),
        (first.at[0:size], at(near, core, size)),
        (second.at[0, 0:size], at(far, core, size)),
        (second.at[1, 0:size], at(both, core, size)),
    ]
    batch_two = [
        (other_first.at[0:size], at(far, 1 - core, size)),
        (other_second.at[0, 0:size], at(near, 1 - core, size)),
        (other_second.at[1, 0:size], at(both, 1 - core, size)),
    ]
    copies = [
        pltpu.make_async_copy(src, to, sems.at[i])
        for i, (src, to) in enumerate(batch_one + batch_two)
    ]
    for c in copies[:4]:
        c.start()
    return copies


def finish_load(copies):
    for c in copies[:4]:
        c.wait()
    for c in copies[4:]:
        c.start()
    for c in copies[4:]:
        c.wait()


def assemble(shard, pieces, k, wide_s):
    first, second, other_first, other_second = pieces
    rows = shard.shape[0]
    off, _ = half_of(rows)
    me, core = lax.axis_index("dp"), lax.rem(lax.axis_index("ctx"), 2)
    near = jnp.bitwise_xor(me, 1 + core)
    far = jnp.bitwise_xor(me, 2 - core)
    both = jnp.bitwise_xor(me, 3)

    def put(device, half, piece):
        start = pl.ds(pl.multiple_of(device * rows + half * off, 8), piece.shape[0])
        wide_s[start, :] = piece.astype(F32)

    put(me, 0, shard)
    put(near, core, first[k])
    put(far, core, second[0, k])
    put(both, core, second[1, k])
    put(far, 1 - core, other_first[k])
    put(near, 1 - core, other_second[0, k])
    put(both, 1 - core, other_second[1, k])
    return wide_s[...].astype(BF)


def params(mib=60):
    return pltpu.CompilerParams(vmem_limit_bytes=mib * MIB)


def cost(products, entries):
    return pl.CostEstimate(
        flops=40 * products + 800 * entries, bytes_accessed=1, transcendentals=0
    )


def split_grad(acc_ref, keep_ref, send_ref, taps, first_block=None):
    me, core = lax.axis_index("dp"), lax.rem(lax.axis_index("ctx"), 2)
    block = acc_ref.shape[0] // taps
    width = keep_ref.shape[-1]
    rows = block // 4
    off, size = half_of(rows)
    mine = (0, 2 - core, 1 + core, 3)
    theirs = (0, 1 + core, 2 - core, 3)
    for j in range(4):
        for k in range(taps):
            a = jnp.bitwise_xor(me, mine[j]) * rows + core * off + k * block
            b = jnp.bitwise_xor(me, theirs[j]) * rows + (1 - core) * off + k * block
            for ref, begin in ((keep_ref, a), (send_ref, b)):
                v = acc_ref[pl.ds(pl.multiple_of(begin, 8), size), :].astype(BF)
                if taps > 1:
                    ref[j, k] = v
                elif first_block is None:
                    ref[j] = v
                else:
                    for h in range(v.shape[1] // width):
                        ref[j, first_block + h] = v[:, h * width : (h + 1) * width]


def prepare_in_body(*refs):
    w_ref, out_ref, rows_s = refs[0], refs[-2], refs[-1]
    off, size = half_of(w_ref.shape[0])
    core = lax.rem(lax.axis_index("ctx"), 2)
    out_ref[0:size, :] = w_ref[pl.ds(pl.multiple_of(core * off, 16), size), :]
    rows_s[...] = jnp.zeros_like(rows_s)
    for j, ref in enumerate(refs[1:-2]):
        n = ref.shape[0]
        rows_s[j : j + 1, 0:n] = ref[...].astype(F32).reshape(1, n)
    out_ref[size:, :] = rows_s[...].astype(BF)


def prepare_in(weight, vectors):
    rows, inner = weight.shape
    size = half_of(rows)[1]
    assert size % 16 == 0 and max(v.shape[0] for v in vectors) <= inner and len(vectors) <= 16
    vmem = pl.BlockSpec(memory_space=pltpu.VMEM)
    return pl.pallas_call(
        prepare_in_body,
        in_specs=[vmem] * (1 + len(vectors)),
        out_specs=vmem,
        out_shape=sds((size + 16, inner), BF),
        scratch_shapes=[pltpu.VMEM((16, inner), F32)],
        compiler_params=params(),
        name="prepare_in",
    )(weight, *vectors)


def prepare_rest_body(wc_ref, wo_ref, out_ref):
    inner = wc_ref.shape[2]
    off, size = half_of(wc_ref.shape[1])
    core = lax.rem(lax.axis_index("ctx"), 2)
    r = pl.ds(pl.multiple_of(core * off, 16), size)
    for k in range(3):
        out_ref[k] = wc_ref[k, r, :]
    half = wo_ref[r, :]
    out_ref[3] = half[:, 0:inner]
    out_ref[4] = half[:, inner:]


def prepare_rest(weight_conv, weight_out):
    inner = weight_conv.shape[2]
    vmem = pl.BlockSpec(memory_space=pltpu.VMEM)
    return pl.pallas_call(
        prepare_rest_body,
        in_specs=[vmem] * 2,
        out_specs=vmem,
        out_shape=sds((5, half_of(weight_conv.shape[1])[1], inner), BF),
        compiler_params=params(),
        name="prepare_rest",
    )(weight_conv, weight_out)


def vec_specs(packs):
    own, first, second = packs
    inner = own.shape[1]
    at = own.shape[0] // 16 - 1
    row = pl.BlockSpec((16, inner), lambda s: (at, 0))
    return [row, row, pl.BlockSpec((2, 16, inner), lambda s: (0, at, 0))]


def stats_body(x_ref, st_ref, sq_ref):
    wide, length = x_ref.shape

    @pl.when(pl.program_id(0) == 0)
    def _():
        sq_ref[...] = jnp.zeros_like(sq_ref)

    mean, var = row_stats(wide // ROWS, lambda i: x_ref[rows_at(i), :].astype(F32), wide, length)
    st_ref[0:1, :] = mean
    st_ref[1:2, :] = lax.rsqrt(var + EPS)
    sq_ref[0:1, :] += (var + mean * mean) * float(wide)


def input_stats(x):
    seqs, wide, length = x.shape
    return pl.pallas_call(
        stats_body,
        grid=(seqs,),
        in_specs=[seq((wide, length))],
        out_specs=[seq((8, length)), full((8, length))],
        out_shape=[sds((seqs, 8, length), F32), sds((8, length), F32)],
        compiler_params=params(),
        cost_estimate=cost(0, x.size // 4),
        name="input_stats",
    )(x)


def act_body(x_ref, st_ref, v0, v1, v2, a0_ref, vw_s):
    wide, length = x_ref.shape

    @pl.when(pl.program_id(0) == 0)
    def _():
        for j in range(2):
            spread((v0, v1, v2), vw_s, j, j, 0.5)

    mean = st_ref[0:1, :]
    inv = st_ref[1:2, :]

    def act0(i):
        r = rows_at(i)
        y = (x_ref[r, :].astype(F32) - mean) * inv * col(vw_s, 0, r, length)
        a0_ref[r, :] = silu_of_half(y + col(vw_s, 1, r, length)).astype(BF)

    loop(wide // ROWS, act0, 5)


def first_act(x, stats, packs):
    seqs, wide, length = x.shape
    return pl.pallas_call(
        act_body,
        grid=(seqs,),
        in_specs=[seq((wide, length)), seq((8, length))] + vec_specs(packs),
        out_specs=seq((wide, length)),
        out_shape=sds((seqs, wide, length), BF),
        scratch_shapes=[pltpu.VMEM((2, wide, 128), F32)],
        compiler_params=params(),
        cost_estimate=cost(0, x.size // 2),
        name="first_act",
    )(x, stats, *packs)


def first_body(
    a0_ref, p0, p1, p2, p3, p4, v0, v1, v2,
    h1_ref, a1_ref, edge_ref, sq_ref, st_ref, w_ref,
    w_s, wt_s, vi_s, sems, out_sem,
):
    s = pl.program_id(0)
    inner, length = h1_ref.shape

    @pl.when(s == 0)
    def _():
        copies = start_load((p0, p1, p2, p3, p4), w_s, sems)
        sq_ref[...] = jnp.zeros_like(sq_ref)
        for j in range(3):
            spread((v0, v1, v2), vi_s, j, j + 3, (1.0, 0.5, 0.5)[j])
        finish_load(copies)
        pltpu.make_async_copy(w_s, w_ref, out_sem).start()
        wt_s[...] = w_s[...].T

    h1_ref[...] = mm(wt_s[...], a0_ref[...]) + lanes(vi_s[0], length)
    mean1, var1 = row_stats(inner // ROWS, lambda i: h1_ref[rows_at(i), :], inner, length)
    inv1 = lax.rsqrt(var1 + EPS)
    st_ref[0:1, :] = mean1
    st_ref[1:2, :] = inv1
    sq_ref[0:1, :] += (var1 + mean1 * mean1) * float(inner)

    def act1(i):
        r = rows_at(i)
        y = (h1_ref[r, :] - mean1) * inv1 * col(vi_s, 1, r, length) + col(vi_s, 2, r, length)
        a1_ref[r, :] = silu_of_half(y).astype(BF)

    loop(inner // ROWS, act1, 5)
    edge_ref[...] = a1_ref[:, length - 128 :].astype(F32).T[120:128, :].astype(BF)

    @pl.when(s == pl.num_programs(0) - 1)
    def _():
        pltpu.make_async_copy(w_s, w_ref, out_sem).wait()


def first(a0, pieces, packs):
    seqs, wide, length = a0.shape
    inner = pieces[0].shape[1]
    return pl.pallas_call(
        first_body,
        grid=(seqs,),
        in_specs=[seq((wide, length))] + [ANY] * 5 + vec_specs(packs),
        out_specs=[
            seq((inner, length)),
            seq((inner, length)),
            seq((8, inner)),
            full((8, length)),
            seq((8, length)),
            ANY,
        ],
        out_shape=[
            sds((seqs, inner, length), F32),
            sds((seqs, inner, length), BF),
            sds((seqs, 8, inner), BF),
            sds((8, length), F32),
            sds((seqs, 8, length), F32),
            sds((wide, inner), BF),
        ],
        scratch_shapes=[
            pltpu.VMEM((wide, inner), BF),
            pltpu.VMEM((inner, wide), BF),
            pltpu.VMEM((3, inner, 128), F32),
            pltpu.SemaphoreType.DMA((7,)),
            pltpu.SemaphoreType.DMA,
        ],
        compiler_params=params(),
        cost_estimate=cost(a0.size * inner, a0.size),
        name="first_product",
    )(a0, *pieces, *packs)


def assemble_body(wc_own, wo_own, f, g, of, og, wc_ref, wct_ref, wo_ref, tap_s):
    inner = wc_ref.shape[1]
    pieces = (f, g, of, og)
    for k in range(3):
        wc_ref[k] = assemble(wc_own[k], pieces, k, tap_s)
    wct_ref[...] = wc_ref[...].reshape(3 * inner, inner).T
    for k in range(2):
        wo_ref[k] = assemble(wo_own[:, k * inner : (k + 1) * inner], pieces, 3 + k, tap_s)


def assemble_weights(own_conv, own_out, pieces):
    inner = own_conv.shape[2]
    vmem = pl.BlockSpec(memory_space=pltpu.VMEM)
    return pl.pallas_call(
        assemble_body,
        in_specs=[vmem] * 6,
        out_specs=[vmem] * 3,
        out_shape=[
            sds((3, inner, inner), BF),
            sds((inner, 3 * inner), BF),
            sds((2, inner, inner), BF),
        ],
        scratch_shapes=[pltpu.VMEM((inner, inner), F32)],
        compiler_params=params(),
        cost_estimate=cost(0, 4 * inner * inner),
        name="assemble_weights",
    )(own_conv, own_out, *pieces)


def transpose_body(w_ref, wt_ref):
    inner = w_ref.shape[1]
    for k in range(2):
        wt_ref[k * inner : (k + 1) * inner, :] = w_ref[k].T


def transposed(w):
    inner = w.shape[1]
    vmem = pl.BlockSpec(memory_space=pltpu.VMEM)
    return pl.pallas_call(
        transpose_body,
        in_specs=[vmem],
        out_specs=vmem,
        out_shape=sds((2 * inner, inner), BF),
        compiler_params=params(),
        name="transpose_out",
    )(w)


def conv_body(
    a1_ref, halo_ref, dy_ref, dyp_ref, mk_ref, wct_ref, wo_ref, v0, v1, v2,
    a2_ref, dh2_ref, edge_ref, sums_ref, bo_ref, sq_ref, keep_ref, send_ref,
    st_s, a2_s, dh_s, h_s, d_s, hl_s, vi_s, sums_s, bo_s, acc_s, out_s, mi_s,
):
    s = pl.program_id(0)
    seqs = pl.num_programs(0) - 1
    inner, length = a1_ref.shape
    wide = dy_ref.shape[0]
    steps = inner // ROWS
    now, then = lax.rem(s, 2), lax.rem(s + 1, 2)

    @pl.when(s == 0)
    def _():
        sq_ref[...] = jnp.zeros_like(sq_ref)
        sums_s[...] = jnp.zeros_like(sums_s)
        bo_s[...] = jnp.zeros_like(bo_s)
        acc_s[...] = jnp.zeros_like(acc_s)
        out_s[...] = jnp.zeros_like(out_s)
        for j in range(3):
            spread((v0, v1, v2), vi_s, j, j + 6, (1.0, 0.5, 0.5)[j])

    @pl.when(s < seqs)
    def _():
        hl_s[...] = jnp.concatenate(
            [jnp.zeros((120, inner), F32), halo_ref[...].astype(F32)], axis=0
        ).T
        m1 = mk_ref[1:2, :]
        m2 = mk_ref[2:3, :]

        def build(i):
            r = rows_at(i)
            b = a1_ref[r, :]
            v = jnp.concatenate([b.astype(F32), hl_s[r, :]], axis=1)
            st_s[now, r, :] = b
            st_s[now, rows_at(i, inner), :] = (pltpu.roll(v, 2, 1)[:, 0:length] * m1).astype(BF)
            st_s[now, rows_at(i, 2 * inner), :] = (pltpu.roll(v, 4, 1)[:, 0:length] * m2).astype(BF)

        loop(steps, build, 10)
        h_s[...] = mm(wct_ref[...], st_s[now]) + lanes(vi_s[0], length)
        d_s[...] = mm(wo_ref[0], dy_ref[0:inner, :]) + mm(wo_ref[1], dy_ref[inner:, :])

        mean, var = row_stats(steps, lambda i: h_s[rows_at(i), :], inner, length)
        mi_s[0:1, :] = mean
        mi_s[1:2, :] = lax.rsqrt(var + EPS)
        sq_ref[0:1, :] += (var + mean * mean) * float(inner)

    mean = mi_s[0:1, :]
    inv = mi_s[1:2, :]
    zero = jnp.zeros((8, length), F32)

    def back(i, acc):
        r = rows_at(i)
        n = (h_s[r, :] - mean) * inv
        g = col(vi_s, 1, r, length)
        y = n * g + col(vi_s, 2, r, length)
        t = jnp.tanh(y)
        up = 1.0 + t
        a2 = (y * up).astype(BF)
        a2_ref[r, :] = a2
        a2_s[now, r, :] = a2
        e = d_s[r, :] * (up * (1.0 + y * (1.0 - t)))
        q = e * g
        d_s[r, :] = q
        h_s[r, :] = n
        sums_s[0, r, :] += fold(e * n)
        sums_s[1, r, :] += fold(e)
        return acc[0] + eight(q), acc[1] + eight(q * n)

    def means(acc):
        return [jnp.sum(a, axis=0, keepdims=True) * (1.0 / inner) for a in acc]

    def last(i, mq, mqn):
        r = rows_at(i)
        dh = ((d_s[r, :] - mq - h_s[r, :] * mqn) * inv).astype(BF)
        dh2_ref[r, :] = dh
        dh_s[now, r, :] = dh
        sums_s[2, r, :] += fold(dh.astype(F32))

    def block(j):
        return pl.ds(pl.multiple_of(j * inner, 16), inner)

    def grad_tap(j):
        acc_s[block(j), :] += mm(st_s[then, block(j), :], dh_s[then], NT)

    def grad_out(k):
        r = pl.ds(pl.multiple_of(k * (inner // 2), 16), inner // 2)
        out_s[r, :] += mm(a2_s[then, r, :], dyp_ref[...], NT)

    def bias(i):
        r = rows_at(i)
        bo_s[r, :] += fold(dyp_ref[r, :].astype(F32))

    @pl.when(s == 0)
    def _():
        acc = lax.fori_loop(0, steps, back, (zero, zero), unroll=5)
        mq, mqn = means(acc)
        loop(steps, lambda i: last(i, mq, mqn), 5)

    @pl.when(jnp.logical_and(s > 0, s < seqs))
    def _():
        each, some = steps // 3, wide // ROWS // 3
        acc = lax.fori_loop(3 * each, steps, back, (zero, zero), unroll=True)
        for i in range(3 * some, wide // ROWS):
            bias(i)

        def tap(j, acc):
            grad_tap(j)
            for c in range(each):
                acc = back(j * each + c, acc)
            for c in range(some):
                bias(j * some + c)
            return acc

        mq, mqn = means(lax.fori_loop(0, 3, tap, acc))

        def out(k):
            grad_out(k)
            for c in range(steps // 2):
                last(k * (steps // 2) + c, mq, mqn)

        loop(2, out, 1)

    @pl.when(s < seqs)
    def _():
        edge_ref[...] = dh2_ref[:, 0:128].astype(F32).T[0:8, :].astype(BF)

    @pl.when(s == seqs)
    def _():
        loop(3, grad_tap, 1)
        loop(2, grad_out, 1)
        loop(wide // ROWS, bias, 5)
        for j in range(3):
            sums_ref[j : j + 1, :] = gathered_row(sums_s[j]) * (0.5, 0.5, 1.0)[j]
        bo_ref[0:1, :] = gathered_row(bo_s[...])
        split_grad(acc_s, keep_ref, send_ref, 3)
        split_grad(out_s, keep_ref, send_ref, 1, 3)


def conv(a1, halo, dy, mk, wct, wo, packs):
    seqs, inner, length = a1.shape
    wide = dy.shape[1]
    assert inner % (2 * ROWS) == 0
    size = half_of(inner // 4)[1]

    this, previous = functools.partial(this_seq, seqs), previous_seq

    return pl.pallas_call(
        conv_body,
        grid=(seqs + 1,),
        in_specs=[
            this((inner, length)),
            this((8, inner)),
            this((wide, length)),
            previous((wide, length)),
            this((8, length)),
        ]
        + [full(p.shape) for p in (wct, wo)]
        + vec_specs(packs),
        out_specs=[
            this((inner, length)),
            this((inner, length)),
            this((8, inner)),
            full((8, inner)),
            full((8, wide)),
            full((8, length)),
            full((4, 5, size, inner)),
            full((4, 5, size, inner)),
        ],
        out_shape=[
            sds((seqs, inner, length), BF),
            sds((seqs, inner, length), BF),
            sds((seqs, 8, inner), BF),
            sds((8, inner), F32),
            sds((8, wide), F32),
            sds((8, length), F32),
            sds((4, 5, size, inner), BF),
            sds((4, 5, size, inner), BF),
        ],
        scratch_shapes=[
            pltpu.VMEM((2, 3 * inner, length), BF),
            pltpu.VMEM((2, inner, length), BF),
            pltpu.VMEM((2, inner, length), BF),
            pltpu.VMEM((inner, length), F32),
            pltpu.VMEM((inner, length), F32),
            pltpu.VMEM((inner, 128), F32),
            pltpu.VMEM((3, inner, 128), F32),
            pltpu.VMEM((3, inner, 128), F32),
            pltpu.VMEM((wide, 128), F32),
            pltpu.VMEM((3 * inner, inner), F32),
            pltpu.VMEM((inner, wide), F32),
            pltpu.VMEM((8, length), F32),
        ],
        compiler_params=params(),
        cost_estimate=cost(a1.size * (6 * inner + 2 * wide), 2 * a1.size),
        name="conv_and_third_norm",
    )(a1, halo, dy, dy, mk, wct, wo, *packs)


def grad_body(a_ref, b_ref, keep_ref, send_ref, acc_s):
    s = pl.program_id(0)

    @pl.when(s == 0)
    def _():
        acc_s[...] = mm(a_ref[...], b_ref[...], NT)

    @pl.when(s > 0)
    def _():
        acc_s[...] += mm(a_ref[...], b_ref[...], NT)

    @pl.when(s == pl.num_programs(0) - 1)
    def _():
        split_grad(acc_s, keep_ref, send_ref, 1)


def grad(a, b, name):
    seqs, m, length = a.shape
    n = b.shape[1]
    size = half_of(m // 4)[1]
    return pl.pallas_call(
        grad_body,
        grid=(seqs,),
        in_specs=[seq((m, length)), seq((n, length))],
        out_specs=[full((4, size, n)), full((4, size, n))],
        out_shape=[sds((4, size, n), BF), sds((4, size, n), BF)],
        scratch_shapes=[pltpu.VMEM((m, n), F32)],
        compiler_params=params(),
        cost_estimate=cost(a.size * n, 0),
        name=name,
    )(a, b)


def shift_back(dh2_ref, halo_ref, mk_ref, hl_s, t_s):
    inner, length = dh2_ref.shape
    hl_s[...] = jnp.concatenate(
        [halo_ref[...].astype(F32), jnp.zeros((120, inner), F32)], axis=0
    ).T
    f1 = mk_ref[3:4, :]
    f2 = mk_ref[4:5, :]

    def build(i):
        r = rows_at(i)
        b = dh2_ref[r, :]
        v = jnp.concatenate([b.astype(F32), hl_s[r, :]], axis=1)
        t_s[0, r, :] = b
        t_s[1, r, :] = (pltpu.roll(v, length + 126, 1)[:, 0:length] * f1).astype(BF)
        t_s[2, r, :] = (pltpu.roll(v, length + 124, 1)[:, 0:length] * f2).astype(BF)

    loop(inner // ROWS, build, 10)


def conv_back_body(
    dh2_ref, halo_ref, h1_ref, st_ref, mk_ref, wc_ref, v0, v1, v2,
    dh1_ref, sums_ref,
    t_s, d_s, n_s, hl_s, vi_s, sums_s,
):
    s = pl.program_id(0)
    seqs = pl.num_programs(0) - 1
    inner, length = dh2_ref.shape
    steps = inner // ROWS
    now, then = lax.rem(s, 2), lax.rem(s + 1, 2)

    @pl.when(s == 0)
    def _():
        sums_s[...] = jnp.zeros_like(sums_s)
        for j in range(2):
            spread((v0, v1, v2), vi_s, j, j + 4, 0.5)

    @pl.when(s < seqs)
    def _():
        shift_back(dh2_ref, halo_ref, mk_ref, hl_s, t_s)

    def back_of(mean, inv):
        def back(i, acc):
            r = rows_at(i)
            n = (h1_ref[r, :] - mean) * inv
            g = col(vi_s, 0, r, length)
            y = n * g + col(vi_s, 1, r, length)
            t = jnp.tanh(y)
            e = d_s[then, r, :] * ((1.0 + t) * (1.0 + y * (1.0 - t)))
            q = e * g
            d_s[then, r, :] = q
            n_s[r, :] = n
            sums_s[0, r, :] += fold(e * n)
            sums_s[1, r, :] += fold(e)
            return acc[0] + eight(q), acc[1] + eight(q * n)

        return back

    def close(acc, inv):
        mq, mqn = [jnp.sum(a, axis=0, keepdims=True) * (1.0 / inner) for a in acc]

        def last(i):
            r = rows_at(i)
            dh = ((d_s[then, r, :] - mq - n_s[r, :] * mqn) * inv).astype(BF)
            dh1_ref[r, :] = dh
            sums_s[2, r, :] += fold(dh.astype(F32))

        loop(steps, last, 5)

    def stats():
        return st_ref[0:1, :], st_ref[1:2, :]

    zero = jnp.zeros((8, length), F32)

    @pl.when(s == 0)
    def _():
        d_s[now] = mm(wc_ref[0], t_s[0]) + mm(wc_ref[1], t_s[1]) + mm(wc_ref[2], t_s[2])

    @pl.when(jnp.logical_and(s > 0, s < seqs))
    def _():
        mean, inv = stats()
        back = back_of(mean, inv)
        each = steps // 3
        acc = lax.fori_loop(3 * each, steps, back, (zero, zero), unroll=True)
        for k in range(3):
            part = mm(wc_ref[k], t_s[k])
            d_s[now] = part if k == 0 else d_s[now] + part
            for c in range(each):
                acc = back(k * each + c, acc)
        close(acc, inv)

    @pl.when(s == seqs)
    def _():
        mean, inv = stats()
        close(lax.fori_loop(0, steps, back_of(mean, inv), (zero, zero), unroll=5), inv)
        for j in range(3):
            sums_ref[j : j + 1, :] = gathered_row(sums_s[j]) * (0.5, 0.5, 1.0)[j]


def seq_from(begin, shape):
    return pl.BlockSpec((None,) + shape, lambda s: (s + begin,) + (0,) * len(shape))


def this_seq(seqs, shape):
    return pl.BlockSpec((None,) + shape, lambda s: (jnp.minimum(s, seqs - 1),) + (0,) * len(shape))


def previous_seq(shape):
    return pl.BlockSpec((None,) + shape, lambda s: (jnp.maximum(s - 1, 0),) + (0,) * len(shape))


def conv_back(dh2, halo, h1, stats, mk, wc, packs):
    seqs, inner, length = dh2.shape
    return pl.pallas_call(
        conv_back_body,
        grid=(seqs + 1,),
        in_specs=[
            this_seq(seqs, (inner, length)),
            this_seq(seqs, (8, inner)),
            previous_seq((inner, length)),
            previous_seq((8, length)),
            this_seq(seqs, (8, length)),
            full(wc.shape),
        ]
        + vec_specs(packs),
        out_specs=[previous_seq((inner, length)), full((8, inner))],
        out_shape=[sds((seqs, inner, length), BF), sds((8, inner), F32)],
        scratch_shapes=[
            pltpu.VMEM((3, inner, length), BF),
            pltpu.VMEM((2, inner, length), F32),
            pltpu.VMEM((inner, length), F32),
            pltpu.VMEM((inner, 128), F32),
            pltpu.VMEM((2, inner, 128), F32),
            pltpu.VMEM((3, inner, 128), F32),
        ],
        compiler_params=params(),
        cost_estimate=cost(dh2.size * 3 * inner, 2 * dh2.size),
        name="conv_backward",
    )(dh2, halo, h1, stats, mk, wc, *packs)


def stream_body(
    x_ref, st_ref, dy_ref, dh1_ref, w_ref, v0, v1, v2, before_ref,
    gs_ref, sums_ref,
    d_s, n_s, vw_s, sums_s,
):
    s = pl.program_id(0)
    wide, length = x_ref.shape
    steps = wide // ROWS

    @pl.when(s == 0)
    def _():
        sums_s[...] = jnp.zeros_like(sums_s)
        for j in range(2):
            spread((v0, v1, v2), vw_s, j, j, 0.5)

    d_s[...] = mm(w_ref[...], dh1_ref[...])
    mean = st_ref[0:1, :]
    inv = st_ref[1:2, :]

    def back(i, acc):
        r = rows_at(i)
        n = (x_ref[r, :].astype(F32) - mean) * inv
        g = col(vw_s, 0, r, length)
        y = n * g + col(vw_s, 1, r, length)
        t = jnp.tanh(y)
        e = d_s[r, :] * ((1.0 + t) * (1.0 + y * (1.0 - t)))
        q = e * g
        d_s[r, :] = q
        n_s[r, :] = n
        sums_s[0, r, :] += fold(e * n)
        sums_s[1, r, :] += fold(e)
        return acc[0] + eight(q), acc[1] + eight(q * n)

    zero = jnp.zeros((8, length), F32)
    qa, qn = lax.fori_loop(0, steps, back, (zero, zero), unroll=5)
    mq = jnp.sum(qa, axis=0, keepdims=True) * (1.0 / wide)
    mqn = jnp.sum(qn, axis=0, keepdims=True) * (1.0 / wide)

    def last(i):
        r = rows_at(i)
        gs = dy_ref[r, :].astype(F32) + (d_s[r, :] - mq - n_s[r, :] * mqn) * inv
        gs_ref[r, :] = gs.astype(BF)

    loop(steps, last, 5)

    @pl.when(s == pl.num_programs(0) - 1)
    def _():
        for j in range(2):
            sums_ref[j : j + 1, :] = gathered_row(sums_s[j]) * 0.5


def stream_back(x, stats, dy, dh1, w, packs, begin, count, before):
    seqs, wide, length = x.shape
    inner = dh1.shape[1]
    aliases = {8: 0} if begin else {}
    return pl.pallas_call(
        stream_body,
        grid=(count,),
        in_specs=[
            seq_from(begin, (wide, length)),
            seq_from(begin, (8, length)),
            seq_from(begin, (wide, length)),
            seq_from(begin, (inner, length)),
            full(w.shape),
        ]
        + vec_specs(packs)
        + [ANY],
        out_specs=[seq_from(begin, (wide, length)), full((8, wide))],
        out_shape=[sds((seqs, wide, length), BF), sds((8, wide), F32)],
        input_output_aliases=aliases,
        scratch_shapes=[
            pltpu.VMEM((wide, length), F32),
            pltpu.VMEM((wide, length), F32),
            pltpu.VMEM((2, wide, 128), F32),
            pltpu.VMEM((2, wide, 128), F32),
        ],
        compiler_params=params(),
        cost_estimate=cost(dh1.size * wide * count // seqs, x.size * count // seqs),
        name="grad_stream",
    )(x, stats, dy, dh1, w, *packs, before)


def output_body(x_ref, a2_ref, wt_ref, v0, v1, v2, before_ref, out_ref, sq_ref, o_s, vw_s):
    s = pl.program_id(0)
    wide, length = x_ref.shape

    @pl.when(s == 0)
    def _():
        sq_ref[...] = jnp.zeros_like(sq_ref)
        spread((v0, v1, v2), vw_s, 0, 2)

    o_s[...] = mm(wt_ref[...], a2_ref[...])

    def close(i, acc):
        r = rows_at(i)
        branch = o_s[r, :] + col(vw_s, 0, r, length)
        result = x_ref[r, :].astype(F32) + branch
        out_ref[r, :] = result.astype(BF)
        return acc[0] + eight(branch * branch), acc[1] + eight(result * result)

    zero = jnp.zeros((8, length), F32)
    b2, r2 = lax.fori_loop(0, wide // ROWS, close, (zero, zero), unroll=5)
    sq_ref[0:1, :] += jnp.sum(b2, axis=0, keepdims=True)
    sq_ref[1:2, :] += jnp.sum(r2, axis=0, keepdims=True)


def output_of(x, a2, wt, packs, begin, count, before):
    seqs, wide, length = x.shape
    inner = a2.shape[1]
    aliases = {6: 0} if begin else {}
    return pl.pallas_call(
        output_body,
        grid=(count,),
        in_specs=[seq_from(begin, (wide, length)), seq_from(begin, (inner, length))]
        + [full(wt.shape)]
        + vec_specs(packs)
        + [ANY],
        out_specs=[seq_from(begin, (wide, length)), full((8, length))],
        out_shape=[sds((seqs, wide, length), BF), sds((8, length), F32)],
        input_output_aliases=aliases,
        scratch_shapes=[
            pltpu.VMEM((wide, length), F32),
            pltpu.VMEM((1, wide, 128), F32),
        ],
        compiler_params=params(),
        cost_estimate=cost(a2.size * wide * count // seqs, x.size * count // (4 * seqs)),
        name="block_output",
    )(x, a2, wt, *packs, before)


def pack_sums_body(n_one, n_zero, n_out, *refs):
    refs, out_ref = list(refs[:-1]), refs[-1]
    bo, two, q_in, q_one, q_two = (refs.pop(0) for _ in range(5))
    one = sum(refs.pop(0)[0:3, :] for _ in range(n_one))
    zero = sum(refs.pop(0)[0:2, :] for _ in range(n_zero))
    out = sum(refs.pop(0)[0:2, :] for _ in range(n_out))
    inner = two.shape[1]
    out_ref[...] = jnp.zeros_like(out_ref)
    out_ref[0:2, :] = zero
    out_ref[2:3, :] = bo[0:1, :]
    out_ref[3:6, 0:inner] = one
    out_ref[3:6, inner : 2 * inner] = two[0:3, :]
    rows = (q_in[0:1, :], out[1:2, :], q_one[0:1, :], q_two[0:1, :], out[0:1, :])
    for j, row in enumerate(rows):
        total = jnp.sum(row, axis=1, keepdims=True)
        out_ref[6:7, j * 128 : (j + 1) * 128] = jnp.broadcast_to(total, (1, 128))


def pack_sums(bo, two, q_in, q_one, q_two, ones, zeros, outs):
    vmem = pl.BlockSpec(memory_space=pltpu.VMEM)
    args = (bo, two, q_in, q_one, q_two, *ones, *zeros, *outs)
    return pl.pallas_call(
        functools.partial(pack_sums_body, len(ones), len(zeros), len(outs)),
        in_specs=[vmem] * len(args),
        out_specs=vmem,
        out_shape=sds((8, bo.shape[1]), F32),
        compiler_params=params(16),
        name="pack_sums",
    )(*args)


def join_body(mine_ref, other_ref, mine_in, other_in, conv_ref, out_ref, in_ref):
    core = lax.rem(lax.axis_index("ctx"), 2)
    rows, inner = conv_ref.shape[1:]

    def halves(a, b, total):
        off, size = half_of(total)
        low = jnp.where(core == 0, a, b).astype(F32)
        high = jnp.where(core == 0, b, a).astype(F32)
        return size, low, high[size - off :]

    for k in range(5):
        size, low, high = halves(mine_ref[k], other_ref[k], rows)
        if k < 3:
            conv_ref[k, 0:size, :] = low
            conv_ref[k, size:rows, :] = high
        else:
            out_ref[0:size, (k - 3) * inner : (k - 2) * inner] = low
            out_ref[size:rows, (k - 3) * inner : (k - 2) * inner] = high
    size, low, high = halves(mine_in[...], other_in[...], in_ref.shape[0])
    in_ref[0:size, :] = low
    in_ref[size:, :] = high


def join_grads(rest, rows, of_in, rows_in):
    inner = of_in[0].shape[1]
    vmem = pl.BlockSpec(memory_space=pltpu.VMEM)
    return pl.pallas_call(
        join_body,
        in_specs=[vmem] * 4,
        out_specs=[vmem] * 3,
        out_shape=[
            sds((3, rows, inner), F32),
            sds((rows, 2 * inner), F32),
            sds((rows_in, inner), F32),
        ],
        compiler_params=params(32),
        name="join_grads",
    )(*rest, *of_in)


def unpack_body(counts, s_ref, *outs):
    me = lax.axis_index("dp")
    wide = s_ref.shape[1]
    inner = wide // 2

    def part(row, begin, size):
        v = s_ref[row : row + 1, begin : begin + size]
        for d in range(1, 4):
            at = begin + d * size
            v = jnp.where(me == d, s_ref[row : row + 1, at : at + size], v)
        return v.reshape(size)

    for j in range(3):
        outs[j][...] = part(j, 0, wide // 4)
    for j in range(6):
        outs[3 + j][...] = part(3 + j % 3, (j // 3) * inner, inner // 4)
    for j, count in enumerate(counts):
        outs[9 + j][...] = jnp.sqrt(s_ref[6:7, j * 128 : (j + 1) * 128] / count)


def unpack_sums(sums, counts):
    wide = sums.shape[1]
    vmem = pl.BlockSpec(memory_space=pltpu.VMEM)
    return pl.pallas_call(
        functools.partial(unpack_body, counts),
        in_specs=[vmem],
        out_specs=[vmem] * 14,
        out_shape=[sds((wide // 4,), F32)] * 3
        + [sds((wide // 8,), F32)] * 6
        + [sds((1, 128), F32)] * 5,
        compiler_params=params(16),
        name="unpack_sums",
    )(sums)


def local(
    stream, segments, cotangent, gain_zero, shift_zero, weight_in, bias_in, gain_one, shift_one,
    weight_conv, bias_conv, gain_two, shift_two, weight_out, bias_out,
):
    n_dp, n_ctx = lax.axis_size("dp"), lax.axis_size("ctx")
    assert n_dp == 4 and n_ctx & (n_ctx - 1) == 0
    me, place = lax.axis_index("dp"), lax.axis_index("ctx")
    seqs, length, wide = stream.shape
    inner = weight_conv.shape[2]
    part_w, part_i = gain_zero.shape[0], bias_in.shape[0]

    x = jnp.swapaxes(stream, 1, 2)
    dy = jnp.swapaxes(cotangent, 1, 2)

    half_in = prepare_in(
        weight_in,
        [gain_zero, shift_zero, bias_out, bias_in, gain_one, shift_one, bias_conv, gain_two, shift_two],
    )
    part_in = gather_halves(half_in)
    sent = next(part_in)
    rest_half = prepare_rest(after(weight_conv, sent), weight_out)
    sent = part_in.send(rest_half)
    stats, sq_in = input_stats(after(x, sent))
    came = part_in.send(sq_in)
    part_rest = gather_halves(after(rest_half, came))
    sent = next(part_rest)
    piece_in = (weight_in, *next(part_in))
    packs = (half_in, *piece_in[1:3])
    act_zero = first_act(x, after(stats, sent), packs)
    sent = part_rest.send(act_zero)

    padded = jnp.pad(segments, ((0, 0), (4, 4)), constant_values=-1)
    near_segs = lax.dynamic_slice_in_dim(padded, place * length, length + 8, 1)
    here = near_segs[:, 4 : 4 + length]
    same = [(near_segs[:, 4 + j : 4 + j + length] == here).astype(F32) for j in (0, -2, -4, 2, 4)]
    masks = jnp.stack(same + same[:3], axis=1)

    hidden_one, act_one, edge, sq_one, stats_one, full_in = first(
        act_zero, piece_in, (after(half_in, sent, masks), *packs[1:])
    )
    halo = shifted(edge, 1)
    part_rest.send(sq_one)
    full_conv, full_conv_t, full_out = assemble_weights(
        weight_conv, weight_out, next(part_rest)
    )
    act_two, d_hidden_two, edge_back, sums_two, sum_bo, sq_two, keep, send = conv(
        act_one, halo, dy, masks, full_conv_t, full_out, packs
    )
    halo_back = shifted(edge_back, -1)
    sum_rest = Stages(sum_shards(keep, send, True))
    own = after(half_in, sum_rest.value)
    full_out_t = transposed(after(full_out, edge_back))
    ones, zeros, outs = [], [], []
    output = grad_x = stats

    def run(what, begin, end):
        nonlocal output, grad_x
        vecs = (own, *packs[1:])
        if what == "out":
            output, sums = output_of(x, act_two, full_out_t, vecs, begin, end - begin, output)
            outs.append(sums)
        else:
            grad_x, sums = stream_back(
                x, stats, dy, d_hidden_one, full_in, vecs, begin, end - begin, grad_x
            )
            zeros.append(sums)
        return sums

    sums = run("out", 0, 1)
    own = after(own, sum_rest.step(sums))
    d_hidden_one, sums = conv_back(
        d_hidden_two, halo_back, hidden_one, stats_one, masks, full_conv, (own, *packs[1:])
    )
    ones.append(sums)
    own = after(own, sum_rest.step(sums))
    keep_in, send_in = grad(act_zero, after(d_hidden_one, own), "grad_weight_in")
    sum_in = Stages(sum_shards(keep_in, send_in, False))
    own = after(own, sum_in.value, sum_rest.step(send_in))
    sums = run("out", 1, 2)
    own = after(own, sum_in.step(sums))
    sums = run("stream", 0, 1)
    own = after(own, sum_in.step(sums), sum_rest.step(sums))
    sums = run("out", 2, seqs)
    own = after(own, sum_in.step(sums), sum_rest.step(sums))
    sums = run("stream", 1, 2)
    own = after(own, sum_in.step(sums), sum_rest.step(sums))
    sums = run("stream", 2, seqs)
    sum_rest.step(sums)
    sums = pack_sums(after(sum_bo, sum_in.step(sums)), sums_two, sq_in, sq_one, sq_two, ones, zeros, outs)
    count = float(seqs * length * n_dp * n_ctx)
    total = Stages(sum_all(sums))
    grad_weight_conv, grad_weight_out, grad_weight_in = join_grads(
        sum_rest.result(), part_i, sum_in.result(), part_w
    )
    total.step(None)
    total.step((grad_weight_out, grad_weight_in))
    sums = total.result()
    totals = unpack_sums(
        sums, (count * wide, count * wide, count * inner, count * inner, count * wide)
    )
    grad_gain_zero, grad_shift_zero, grad_bias_out = totals[0:3]
    grad_gain_one, grad_shift_one, grad_bias_in = totals[3:6]
    grad_gain_two, grad_shift_two, grad_bias_conv = totals[6:9]
    rms_in, rms_out, rms_hidden_one, rms_hidden_two, rms_branch = (v[0, 0] for v in totals[9:])
    return (
        jnp.swapaxes(output, 1, 2),
        jnp.swapaxes(grad_x, 1, 2),
        grad_gain_zero,
        grad_shift_zero,
        grad_weight_in,
        grad_bias_in,
        grad_gain_one,
        grad_shift_one,
        grad_weight_conv,
        grad_bias_conv,
        grad_gain_two,
        grad_shift_two,
        grad_weight_out,
        grad_bias_out,
        rms_in,
        rms_out,
        rms_hidden_one,
        rms_hidden_two,
        rms_branch,
    )


def solution(mesh):
    placed = (
        P("dp", "ctx", None),
        P("dp", None),
        P("dp", "ctx", None),
        P("dp"),
        P("dp"),
        P("dp", None),
        P("dp"),
        P("dp"),
        P("dp"),
        P(None, "dp", None),
        P("dp"),
        P("dp"),
        P("dp"),
        P("dp", None),
        P("dp"),
    )
    return jax.shard_map(
        local,
        mesh=mesh,
        in_specs=placed,
        out_specs=(
            P("dp", "ctx", None),
            P("dp", "ctx", None),
            P("dp"),
            P("dp"),
            P("dp", None),
            P("dp"),
            P("dp"),
            P("dp"),
            P(None, "dp", None),
            P("dp"),
            P("dp"),
            P("dp"),
            P("dp", None),
            P("dp"),
            P(),
            P(),
            P(),
            P(),
            P(),
        ),
        check_vma=False,
    )
```

```python
import functools

import jax
import jax.numpy as jnp
from jax import lax
from jax.experimental import pallas as pl
from jax.experimental.pallas import tpu as pltpu
from jax.sharding import PartitionSpec as P

F32 = jnp.float32
BF = jnp.bfloat16
EPS = 1e-05
ROWS = 16
NN = (((1,), (0,)), ((), ()))
NT = (((1,), (1,)), ((), ()))
MIB = 1024 * 1024


def by_core(value, even_mask, odd_mask):
    n_dp, n_ctx = lax.axis_size("dp"), lax.axis_size("ctx")
    masks = (even_mask, odd_mask)
    pairs = [
        (d * n_ctx + t, (d ^ masks[t % 2]) * n_ctx + t) for d in range(n_dp) for t in range(n_ctx)
    ]
    return lax.ppermute(value, ("dp", "ctx"), pairs)


def swap(value, axis, mask):
    return lax.ppermute(value, axis, [(i, i ^ mask) for i in range(lax.axis_size(axis))])


def shifted(value, by):
    size = lax.axis_size("ctx")
    return lax.ppermute(value, "ctx", [(i, i + by) for i in range(size) if 0 <= i + by < size])


def half_of(rows):
    off = rows // 2 // 16 * 16
    return off, rows - off


def gated(value, gate):
    return value if gate is None else lax.optimization_barrier((value, gate))[0]


def after(value, *others):
    return lax.optimization_barrier((value, *others))[0]


def gather_halves(half):
    first = by_core(half, 1, 2)
    gate = yield half
    sent = jnp.stack([half, gated(first, gate)])
    second = by_core(sent, 2, 1)
    gate = yield sent
    second = gated(second, gate)
    other_first = swap(first, "ctx", 1)
    other_second = swap(second, "ctx", 1)
    yield second
    yield first, second, other_first, other_second


def halved(value, bit):
    rows = value.shape[1]
    off, size = parts_of(rows)
    keep = lax.dynamic_slice_in_dim(value, bit * off, size, 1)
    return keep, lax.dynamic_slice_in_dim(value, (1 - bit) * off, size, 1)


def parts_of(rows):
    off = rows // 2 // 8 * 8
    return off, rows - off


def joined(mine, other, bit, rows):
    off, size = parts_of(rows)
    low = jnp.where(bit == 0, mine, other)
    high = jnp.where(bit == 0, other, mine)
    return jnp.concatenate([low, high[:, size - off :]], axis=1)


def sum_shards(keep, send, halving):
    got = swap(send, "ctx", 1)
    gate = yield send
    got = gated(got, gate)
    sent = (keep[2:4].astype(F32) + got[2:4].astype(F32)).astype(BF)
    one = by_core(sent, 1, 2)
    gate = yield sent
    one = gated(one, gate)
    sent = (keep[1].astype(F32) + got[1].astype(F32) + one[1].astype(F32)).astype(BF)
    two = by_core(sent, 2, 1)
    gate = yield sent
    two = gated(two, gate)
    part = keep[0].astype(F32) + got[0].astype(F32) + one[0].astype(F32) + two.astype(F32)
    place = lax.axis_index("ctx")
    masks = [1 << b for b in range(1, (lax.axis_size("ctx") - 1).bit_length())]
    split = [(mask, (place // mask) % 2) for mask in masks[: 2 if halving else 0]]
    sizes = []
    for mask, bit in split:
        sizes.append(part.shape[1])
        part, sent = halved(part, bit)
        sent = sent.astype(BF)
        came = swap(sent, "ctx", mask)
        gate = yield sent
        part = part + gated(came, gate).astype(F32)
    for mask in masks[len(split) :]:
        sent = part.astype(BF)
        came = swap(sent, "ctx", mask)
        gate = yield sent
        part = sent.astype(F32) + gated(came, gate).astype(F32)
    for mask, bit in split[::-1]:
        sent = part.astype(BF)
        came = swap(sent, "ctx", mask)
        gate = yield sent
        part = joined(sent, gated(came, gate), bit, sizes.pop())
    other = swap(part, "ctx", 1)
    gate = yield part
    yield part, gated(other, gate)


def sum_all(value):
    got = swap(value, "ctx", 1)
    gate = yield value
    value = value + gated(got, gate)
    groups = [("dp", (1, 2, 3)), ("ctx", (2, 4, 6))]
    mask = 8
    while mask < lax.axis_size("ctx"):
        groups.append(("ctx", (mask,)))
        mask *= 2
    for axis, masks in groups:
        got = [value] + [swap(value, axis, m) for m in masks]
        gate = yield value
        if len(got) == 4:
            a, b = got[0] + got[1], got[2] + got[3]
            value = gated(a, gate) + b
        else:
            value = gated(got[0], gate) + got[1]
    yield value


class Stages:
    def __init__(self, stages):
        self.stages, self.value, self.left = stages, next(stages), True

    def step(self, gate):
        try:
            self.value = self.stages.send(gate)
        except StopIteration:
            self.left = False
        return self.value

    def result(self):
        while self.left:
            self.step(None)
        return self.value


def mm(left, right, dims=NN):
    return lax.dot_general(left, right, dims, preferred_element_type=F32)


def silu_of_half(y):
    return y * (1.0 + jnp.tanh(y))


def loop(count, body, unroll):
    lax.fori_loop(0, count, lambda i, _: (body(i), 0)[1], 0, unroll=unroll)


def full(shape):
    return pl.BlockSpec(shape, lambda s: (0,) * len(shape), pipeline_mode=pl.Buffered(1))


def seq(shape):
    return pl.BlockSpec((None,) + shape, lambda s: (s,) + (0,) * len(shape))


ANY = pl.BlockSpec(memory_space=pl.ANY)


def sds(shape, dtype):
    return jax.ShapeDtypeStruct(shape, dtype)


def rows_at(i, base=0):
    return pl.ds(pl.multiple_of(i * ROWS + base, ROWS), ROWS)


def lanes(tile, width):
    return jnp.concatenate([tile] * (width // 128), axis=1)


def col(ref, j, r, width):
    return lanes(ref[j, r, :], width)


def fold(v):
    t = v[:, 0:128]
    for j in range(1, v.shape[1] // 128):
        t = t + v[:, j * 128 : (j + 1) * 128]
    return t


def eight(v):
    return v[0:8] + v[8:16]


def spread(packs, out_ref, j, row, scale=1.0):
    own, near, far = packs
    me, core = lax.axis_index("dp"), lax.rem(lax.axis_index("ctx"), 2)
    part = out_ref.shape[1] // 4
    for mask, ref in ((0, own), (1 + core, near), (2 - core, far.at[0]), (3, far.at[1])):
        start = pl.multiple_of(jnp.bitwise_xor(me, mask) * part, 8)
        v = ref[...].astype(F32)[row : row + 1, 0:part] * scale
        out_ref[j, pl.ds(start, part), :] = jnp.broadcast_to(v, (128, part)).T


def gathered_row(sums):
    return jnp.sum(sums.T, axis=0, keepdims=True)


def row_stats(count, load, width, length):
    def total(i, a):
        return a + eight(load(i))

    zero = jnp.zeros((8, length), F32)
    a = lax.fori_loop(0, count, total, zero, unroll=10)
    mean = jnp.sum(a, axis=0, keepdims=True) * (1.0 / width)

    def squares(i, a):
        c = load(i) - mean
        return a + eight(c * c)

    a = lax.fori_loop(0, count, squares, zero, unroll=10)
    var = jnp.sum(a, axis=0, keepdims=True) * (1.0 / width)
    return mean, var


def start_load(pieces, dst, sems):
    shard, first, second, other_first, other_second = pieces
    rows = shard.shape[0]
    off, size = half_of(rows)
    me, core = lax.axis_index("dp"), lax.rem(lax.axis_index("ctx"), 2)
    near = jnp.bitwise_xor(me, 1 + core)
    far = jnp.bitwise_xor(me, 2 - core)
    both = jnp.bitwise_xor(me, 3)

    def at(device, half, count):
        return dst.at[pl.ds(pl.multiple_of(device * rows + half * off, 16), count), :]

    batch_one = [
        (shard, at(me, 0, rows)),
        (first.at[0:size], at(near, core, size)),
        (second.at[0, 0:size], at(far, core, size)),
        (second.at[1, 0:size], at(both, core, size)),
    ]
    batch_two = [
        (other_first.at[0:size], at(far, 1 - core, size)),
        (other_second.at[0, 0:size], at(near, 1 - core, size)),
        (other_second.at[1, 0:size], at(both, 1 - core, size)),
    ]
    copies = [
        pltpu.make_async_copy(src, to, sems.at[i])
        for i, (src, to) in enumerate(batch_one + batch_two)
    ]
    for c in copies[:4]:
        c.start()
    return copies


def finish_load(copies):
    for c in copies[:4]:
        c.wait()
    for c in copies[4:]:
        c.start()
    for c in copies[4:]:
        c.wait()


def assemble(shard, pieces, k, wide_s):
    first, second, other_first, other_second = pieces
    rows = shard.shape[0]
    off, _ = half_of(rows)
    me, core = lax.axis_index("dp"), lax.rem(lax.axis_index("ctx"), 2)
    near = jnp.bitwise_xor(me, 1 + core)
    far = jnp.bitwise_xor(me, 2 - core)
    both = jnp.bitwise_xor(me, 3)

    def put(device, half, piece):
        start = pl.ds(pl.multiple_of(device * rows + half * off, 8), piece.shape[0])
        wide_s[start, :] = piece.astype(F32)

    put(me, 0, shard)
    put(near, core, first[k])
    put(far, core, second[0, k])
    put(both, core, second[1, k])
    put(far, 1 - core, other_first[k])
    put(near, 1 - core, other_second[0, k])
    put(both, 1 - core, other_second[1, k])
    return wide_s[...].astype(BF)


def params(mib=60):
    return pltpu.CompilerParams(vmem_limit_bytes=mib * MIB)


def cost(products, entries):
    return pl.CostEstimate(
        flops=40 * products + 800 * entries, bytes_accessed=1, transcendentals=0
    )


def split_grad(acc_ref, keep_ref, send_ref, taps, first_block=None):
    me, core = lax.axis_index("dp"), lax.rem(lax.axis_index("ctx"), 2)
    block = acc_ref.shape[0] // taps
    width = keep_ref.shape[-1]
    rows = block // 4
    off, size = half_of(rows)
    mine = (0, 2 - core, 1 + core, 3)
    theirs = (0, 1 + core, 2 - core, 3)
    for j in range(4):
        for k in range(taps):
            a = jnp.bitwise_xor(me, mine[j]) * rows + core * off + k * block
            b = jnp.bitwise_xor(me, theirs[j]) * rows + (1 - core) * off + k * block
            for ref, begin in ((keep_ref, a), (send_ref, b)):
                v = acc_ref[pl.ds(pl.multiple_of(begin, 8), size), :].astype(BF)
                if taps > 1:
                    ref[j, k] = v
                elif first_block is None:
                    ref[j] = v
                else:
                    for h in range(v.shape[1] // width):
                        ref[j, first_block + h] = v[:, h * width : (h + 1) * width]


def prepare_in_body(*refs):
    w_ref, out_ref, rows_s = refs[0], refs[-2], refs[-1]
    off, size = half_of(w_ref.shape[0])
    core = lax.rem(lax.axis_index("ctx"), 2)
    out_ref[0:size, :] = w_ref[pl.ds(pl.multiple_of(core * off, 16), size), :]
    rows_s[...] = jnp.zeros_like(rows_s)
    for j, ref in enumerate(refs[1:-2]):
        n = ref.shape[0]
        rows_s[j : j + 1, 0:n] = ref[...].astype(F32).reshape(1, n)
    out_ref[size:, :] = rows_s[...].astype(BF)


def prepare_in(weight, vectors):
    rows, inner = weight.shape
    size = half_of(rows)[1]
    assert size % 16 == 0 and max(v.shape[0] for v in vectors) <= inner and len(vectors) <= 16
    vmem = pl.BlockSpec(memory_space=pltpu.VMEM)
    return pl.pallas_call(
        prepare_in_body,
        in_specs=[vmem] * (1 + len(vectors)),
        out_specs=vmem,
        out_shape=sds((size + 16, inner), BF),
        scratch_shapes=[pltpu.VMEM((16, inner), F32)],
        compiler_params=params(),
        name="prepare_in",
    )(weight, *vectors)


def prepare_rest_body(wc_ref, wo_ref, out_ref):
    inner = wc_ref.shape[2]
    off, size = half_of(wc_ref.shape[1])
    core = lax.rem(lax.axis_index("ctx"), 2)
    r = pl.ds(pl.multiple_of(core * off, 16), size)
    for k in range(3):
        out_ref[k] = wc_ref[k, r, :]
    half = wo_ref[r, :]
    out_ref[3] = half[:, 0:inner]
    out_ref[4] = half[:, inner:]


def prepare_rest(weight_conv, weight_out):
    inner = weight_conv.shape[2]
    vmem = pl.BlockSpec(memory_space=pltpu.VMEM)
    return pl.pallas_call(
        prepare_rest_body,
        in_specs=[vmem] * 2,
        out_specs=vmem,
        out_shape=sds((5, half_of(weight_conv.shape[1])[1], inner), BF),
        compiler_params=params(),
        name="prepare_rest",
    )(weight_conv, weight_out)


def vec_specs(packs):
    own, first, second = packs
    inner = own.shape[1]
    at = own.shape[0] // 16 - 1
    row = pl.BlockSpec((16, inner), lambda s: (at, 0))
    return [row, row, pl.BlockSpec((2, 16, inner), lambda s: (0, at, 0))]


def stats_body(x_ref, st_ref, sq_ref):
    wide, length = x_ref.shape

    @pl.when(pl.program_id(0) == 0)
    def _():
        sq_ref[...] = jnp.zeros_like(sq_ref)

    mean, var = row_stats(wide // ROWS, lambda i: x_ref[rows_at(i), :].astype(F32), wide, length)
    st_ref[0:1, :] = mean
    st_ref[1:2, :] = lax.rsqrt(var + EPS)
    sq_ref[0:1, :] += (var + mean * mean) * float(wide)


def input_stats(x):
    seqs, wide, length = x.shape
    return pl.pallas_call(
        stats_body,
        grid=(seqs,),
        in_specs=[seq((wide, length))],
        out_specs=[seq((8, length)), full((8, length))],
        out_shape=[sds((seqs, 8, length), F32), sds((8, length), F32)],
        compiler_params=params(),
        cost_estimate=cost(0, x.size // 4),
        name="input_stats",
    )(x)


def act_body(x_ref, st_ref, v0, v1, v2, a0_ref, vw_s):
    wide, length = x_ref.shape

    @pl.when(pl.program_id(0) == 0)
    def _():
        for j in range(2):
            spread((v0, v1, v2), vw_s, j, j, 0.5)

    mean = st_ref[0:1, :]
    inv = st_ref[1:2, :]

    def act0(i):
        r = rows_at(i)
        y = (x_ref[r, :].astype(F32) - mean) * inv * col(vw_s, 0, r, length)
        a0_ref[r, :] = silu_of_half(y + col(vw_s, 1, r, length)).astype(BF)

    loop(wide // ROWS, act0, 10)


def first_act(x, stats, packs):
    seqs, wide, length = x.shape
    return pl.pallas_call(
        act_body,
        grid=(seqs,),
        in_specs=[seq((wide, length)), seq((8, length))] + vec_specs(packs),
        out_specs=seq((wide, length)),
        out_shape=sds((seqs, wide, length), BF),
        scratch_shapes=[pltpu.VMEM((2, wide, 128), F32)],
        compiler_params=params(),
        cost_estimate=cost(0, x.size // 2),
        name="first_act",
    )(x, stats, *packs)


def first_body(
    a0_ref, p0, p1, p2, p3, p4, v0, v1, v2,
    h1_ref, a1_ref, edge_ref, sq_ref, st_ref, w_ref,
    w_s, wt_s, vi_s, sems, out_sem,
):
    s = pl.program_id(0)
    inner, length = h1_ref.shape

    @pl.when(s == 0)
    def _():
        copies = start_load((p0, p1, p2, p3, p4), w_s, sems)
        sq_ref[...] = jnp.zeros_like(sq_ref)
        for j in range(3):
            spread((v0, v1, v2), vi_s, j, j + 3, (1.0, 0.5, 0.5)[j])
        finish_load(copies)
        pltpu.make_async_copy(w_s, w_ref, out_sem).start()
        wt_s[...] = w_s[...].T

    h1_ref[...] = mm(wt_s[...], a0_ref[...]) + lanes(vi_s[0], length)
    mean1, var1 = row_stats(inner // ROWS, lambda i: h1_ref[rows_at(i), :], inner, length)
    inv1 = lax.rsqrt(var1 + EPS)
    st_ref[0:1, :] = mean1
    st_ref[1:2, :] = inv1
    sq_ref[0:1, :] += (var1 + mean1 * mean1) * float(inner)

    def act1(i):
        r = rows_at(i)
        y = (h1_ref[r, :] - mean1) * inv1 * col(vi_s, 1, r, length) + col(vi_s, 2, r, length)
        a1_ref[r, :] = silu_of_half(y).astype(BF)

    loop(inner // ROWS, act1, 10)
    edge_ref[...] = a1_ref[:, length - 128 :].astype(F32).T[120:128, :].astype(BF)

    @pl.when(s == pl.num_programs(0) - 1)
    def _():
        pltpu.make_async_copy(w_s, w_ref, out_sem).wait()


def first(a0, pieces, packs):
    seqs, wide, length = a0.shape
    inner = pieces[0].shape[1]
    return pl.pallas_call(
        first_body,
        grid=(seqs,),
        in_specs=[seq((wide, length))] + [ANY] * 5 + vec_specs(packs),
        out_specs=[
            seq((inner, length)),
            seq((inner, length)),
            seq((8, inner)),
            full((8, length)),
            seq((8, length)),
            ANY,
        ],
        out_shape=[
            sds((seqs, inner, length), F32),
            sds((seqs, inner, length), BF),
            sds((seqs, 8, inner), BF),
            sds((8, length), F32),
            sds((seqs, 8, length), F32),
            sds((wide, inner), BF),
        ],
        scratch_shapes=[
            pltpu.VMEM((wide, inner), BF),
            pltpu.VMEM((inner, wide), BF),
            pltpu.VMEM((3, inner, 128), F32),
            pltpu.SemaphoreType.DMA((7,)),
            pltpu.SemaphoreType.DMA,
        ],
        compiler_params=params(),
        cost_estimate=cost(a0.size * inner, a0.size),
        name="first_product",
    )(a0, *pieces, *packs)


def assemble_body(wc_own, wo_own, f, g, of, og, wc_ref, wct_ref, wo_ref, tap_s):
    inner = wc_ref.shape[1]
    pieces = (f, g, of, og)
    for k in range(3):
        wc_ref[k] = assemble(wc_own[k], pieces, k, tap_s)
    wct_ref[...] = wc_ref[...].reshape(3 * inner, inner).T
    for k in range(2):
        wo_ref[k] = assemble(wo_own[:, k * inner : (k + 1) * inner], pieces, 3 + k, tap_s)


def assemble_weights(own_conv, own_out, pieces):
    inner = own_conv.shape[2]
    vmem = pl.BlockSpec(memory_space=pltpu.VMEM)
    return pl.pallas_call(
        assemble_body,
        in_specs=[vmem] * 6,
        out_specs=[vmem] * 3,
        out_shape=[
            sds((3, inner, inner), BF),
            sds((inner, 3 * inner), BF),
            sds((2, inner, inner), BF),
        ],
        scratch_shapes=[pltpu.VMEM((inner, inner), F32)],
        compiler_params=params(),
        cost_estimate=cost(0, 4 * inner * inner),
        name="assemble_weights",
    )(own_conv, own_out, *pieces)


def transpose_body(w_ref, wt_ref):
    inner = w_ref.shape[1]
    for k in range(2):
        wt_ref[k * inner : (k + 1) * inner, :] = w_ref[k].T


def transposed(w):
    inner = w.shape[1]
    vmem = pl.BlockSpec(memory_space=pltpu.VMEM)
    return pl.pallas_call(
        transpose_body,
        in_specs=[vmem],
        out_specs=vmem,
        out_shape=sds((2 * inner, inner), BF),
        compiler_params=params(),
        name="transpose_out",
    )(w)


def conv_body(
    a1_ref, halo_ref, dy_ref, dyp_ref, mk_ref, wct_ref, wo_ref, v0, v1, v2,
    a2_ref, dh2_ref, edge_ref, sums_ref, bo_ref, sq_ref, keep_ref, send_ref,
    st_s, a2_s, dh_s, h_s, d_s, hl_s, vi_s, sums_s, bo_s, acc_s, out_s, mi_s,
):
    s = pl.program_id(0)
    seqs = pl.num_programs(0) - 1
    inner, length = a1_ref.shape
    wide = dy_ref.shape[0]
    steps = inner // ROWS
    now, then = lax.rem(s, 2), lax.rem(s + 1, 2)

    @pl.when(s == 0)
    def _():
        sq_ref[...] = jnp.zeros_like(sq_ref)
        sums_s[...] = jnp.zeros_like(sums_s)
        bo_s[...] = jnp.zeros_like(bo_s)
        acc_s[...] = jnp.zeros_like(acc_s)
        out_s[...] = jnp.zeros_like(out_s)
        for j in range(3):
            spread((v0, v1, v2), vi_s, j, j + 6, (1.0, 0.5, 0.5)[j])

    @pl.when(s < seqs)
    def _():
        hl_s[...] = jnp.concatenate(
            [jnp.zeros((120, inner), F32), halo_ref[...].astype(F32)], axis=0
        ).T
        m1 = mk_ref[1:2, :]
        m2 = mk_ref[2:3, :]

        def build(i):
            r = rows_at(i)
            b = a1_ref[r, :]
            v = jnp.concatenate([b.astype(F32), hl_s[r, :]], axis=1)
            st_s[now, r, :] = b
            st_s[now, rows_at(i, inner), :] = (pltpu.roll(v, 2, 1)[:, 0:length] * m1).astype(BF)
            st_s[now, rows_at(i, 2 * inner), :] = (pltpu.roll(v, 4, 1)[:, 0:length] * m2).astype(BF)

        loop(steps, build, 25)
        h_s[...] = mm(wct_ref[...], st_s[now]) + lanes(vi_s[0], length)
        d_s[...] = mm(wo_ref[0], dy_ref[0:inner, :]) + mm(wo_ref[1], dy_ref[inner:, :])

        mean, var = row_stats(steps, lambda i: h_s[rows_at(i), :], inner, length)
        mi_s[0:1, :] = mean
        mi_s[1:2, :] = lax.rsqrt(var + EPS)
        sq_ref[0:1, :] += (var + mean * mean) * float(inner)

    mean = mi_s[0:1, :]
    inv = mi_s[1:2, :]
    zero = jnp.zeros((8, length), F32)

    def back(i, acc):
        r = rows_at(i)
        n = (h_s[r, :] - mean) * inv
        g = col(vi_s, 1, r, length)
        y = n * g + col(vi_s, 2, r, length)
        t = jnp.tanh(y)
        up = 1.0 + t
        a2 = (y * up).astype(BF)
        a2_ref[r, :] = a2
        a2_s[now, r, :] = a2
        e = d_s[r, :] * (up * (1.0 + y * (1.0 - t)))
        q = e * g
        d_s[r, :] = q
        h_s[r, :] = n
        sums_s[0, r, :] += fold(e * n)
        sums_s[1, r, :] += fold(e)
        return acc[0] + eight(q), acc[1] + eight(q * n)

    def means(acc):
        return [jnp.sum(a, axis=0, keepdims=True) * (1.0 / inner) for a in acc]

    def last(i, mq, mqn):
        r = rows_at(i)
        dh = ((d_s[r, :] - mq - h_s[r, :] * mqn) * inv).astype(BF)
        dh2_ref[r, :] = dh
        dh_s[now, r, :] = dh
        sums_s[2, r, :] += fold(dh.astype(F32))

    def block(j):
        return pl.ds(pl.multiple_of(j * inner, 16), inner)

    def grad_tap(j):
        acc_s[block(j), :] += mm(st_s[then, block(j), :], dh_s[then], NT)

    def grad_out(k):
        r = pl.ds(pl.multiple_of(k * (inner // 2), 16), inner // 2)
        out_s[r, :] += mm(a2_s[then, r, :], dyp_ref[...], NT)

    def bias(i):
        r = rows_at(i)
        bo_s[r, :] += fold(dyp_ref[r, :].astype(F32))

    @pl.when(s == 0)
    def _():
        acc = lax.fori_loop(0, steps, back, (zero, zero), unroll=10)
        mq, mqn = means(acc)
        loop(steps, lambda i: last(i, mq, mqn), 5)

    @pl.when(jnp.logical_and(s > 0, s < seqs))
    def _():
        each, some = steps // 3, wide // ROWS // 3
        acc = lax.fori_loop(3 * each, steps, back, (zero, zero), unroll=True)
        for i in range(3 * some, wide // ROWS):
            bias(i)

        def tap(j, acc):
            grad_tap(j)
            for c in range(each):
                acc = back(j * each + c, acc)
            for c in range(some):
                bias(j * some + c)
            return acc

        mq, mqn = means(lax.fori_loop(0, 3, tap, acc))

        def out(k):
            grad_out(k)
            for c in range(steps // 2):
                last(k * (steps // 2) + c, mq, mqn)

        loop(2, out, 1)

    @pl.when(s < seqs)
    def _():
        edge_ref[...] = dh2_ref[:, 0:128].astype(F32).T[0:8, :].astype(BF)

    @pl.when(s == seqs)
    def _():
        loop(3, grad_tap, 1)
        loop(2, grad_out, 1)
        loop(wide // ROWS, bias, 5)
        for j in range(3):
            sums_ref[j : j + 1, :] = gathered_row(sums_s[j]) * (0.5, 0.5, 1.0)[j]
        bo_ref[0:1, :] = gathered_row(bo_s[...])
        split_grad(acc_s, keep_ref, send_ref, 3)
        split_grad(out_s, keep_ref, send_ref, 1, 3)


def conv(a1, halo, dy, mk, wct, wo, packs):
    seqs, inner, length = a1.shape
    wide = dy.shape[1]
    assert inner % (2 * ROWS) == 0
    size = half_of(inner // 4)[1]

    this, previous = functools.partial(this_seq, seqs), previous_seq

    return pl.pallas_call(
        conv_body,
        grid=(seqs + 1,),
        in_specs=[
            this((inner, length)),
            this((8, inner)),
            this((wide, length)),
            previous((wide, length)),
            this((8, length)),
        ]
        + [full(p.shape) for p in (wct, wo)]
        + vec_specs(packs),
        out_specs=[
            this((inner, length)),
            this((inner, length)),
            this((8, inner)),
            full((8, inner)),
            full((8, wide)),
            full((8, length)),
            full((4, 5, size, inner)),
            full((4, 5, size, inner)),
        ],
        out_shape=[
            sds((seqs, inner, length), BF),
            sds((seqs, inner, length), BF),
            sds((seqs, 8, inner), BF),
            sds((8, inner), F32),
            sds((8, wide), F32),
            sds((8, length), F32),
            sds((4, 5, size, inner), BF),
            sds((4, 5, size, inner), BF),
        ],
        scratch_shapes=[
            pltpu.VMEM((2, 3 * inner, length), BF),
            pltpu.VMEM((2, inner, length), BF),
            pltpu.VMEM((2, inner, length), BF),
            pltpu.VMEM((inner, length), F32),
            pltpu.VMEM((inner, length), F32),
            pltpu.VMEM((inner, 128), F32),
            pltpu.VMEM((3, inner, 128), F32),
            pltpu.VMEM((3, inner, 128), F32),
            pltpu.VMEM((wide, 128), F32),
            pltpu.VMEM((3 * inner, inner), F32),
            pltpu.VMEM((inner, wide), F32),
            pltpu.VMEM((8, length), F32),
        ],
        compiler_params=params(),
        cost_estimate=cost(a1.size * (6 * inner + 2 * wide), 2 * a1.size),
        name="conv_and_third_norm",
    )(a1, halo, dy, dy, mk, wct, wo, *packs)


def grad_body(a_ref, b_ref, keep_ref, send_ref, acc_s):
    s = pl.program_id(0)

    @pl.when(s == 0)
    def _():
        acc_s[...] = mm(a_ref[...], b_ref[...], NT)

    @pl.when(s > 0)
    def _():
        acc_s[...] += mm(a_ref[...], b_ref[...], NT)

    @pl.when(s == pl.num_programs(0) - 1)
    def _():
        split_grad(acc_s, keep_ref, send_ref, 1)


def grad(a, b, name):
    seqs, m, length = a.shape
    n = b.shape[1]
    size = half_of(m // 4)[1]
    return pl.pallas_call(
        grad_body,
        grid=(seqs,),
        in_specs=[seq((m, length)), seq((n, length))],
        out_specs=[full((4, size, n)), full((4, size, n))],
        out_shape=[sds((4, size, n), BF), sds((4, size, n), BF)],
        scratch_shapes=[pltpu.VMEM((m, n), F32)],
        compiler_params=params(),
        cost_estimate=cost(a.size * n, 0),
        name=name,
    )(a, b)


def shift_back(dh2_ref, halo_ref, mk_ref, hl_s, t_s):
    inner, length = dh2_ref.shape
    hl_s[...] = jnp.concatenate(
        [halo_ref[...].astype(F32), jnp.zeros((120, inner), F32)], axis=0
    ).T
    f1 = mk_ref[3:4, :]
    f2 = mk_ref[4:5, :]

    def build(i):
        r = rows_at(i)
        b = dh2_ref[r, :]
        v = jnp.concatenate([b.astype(F32), hl_s[r, :]], axis=1)
        t_s[0, r, :] = b
        t_s[1, r, :] = (pltpu.roll(v, length + 126, 1)[:, 0:length] * f1).astype(BF)
        t_s[2, r, :] = (pltpu.roll(v, length + 124, 1)[:, 0:length] * f2).astype(BF)

    loop(inner // ROWS, build, 25)


def conv_back_body(
    dh2_ref, halo_ref, h1_ref, st_ref, mk_ref, wc_ref, v0, v1, v2,
    dh1_ref, sums_ref,
    t_s, d_s, n_s, hl_s, vi_s, sums_s,
):
    s = pl.program_id(0)
    seqs = pl.num_programs(0) - 1
    inner, length = dh2_ref.shape
    steps = inner // ROWS
    now, then = lax.rem(s, 2), lax.rem(s + 1, 2)

    @pl.when(s == 0)
    def _():
        sums_s[...] = jnp.zeros_like(sums_s)
        for j in range(2):
            spread((v0, v1, v2), vi_s, j, j + 4, 0.5)

    @pl.when(s < seqs)
    def _():
        shift_back(dh2_ref, halo_ref, mk_ref, hl_s, t_s)

    def back_of(mean, inv):
        def back(i, acc):
            r = rows_at(i)
            n = (h1_ref[r, :] - mean) * inv
            g = col(vi_s, 0, r, length)
            y = n * g + col(vi_s, 1, r, length)
            t = jnp.tanh(y)
            e = d_s[then, r, :] * ((1.0 + t) * (1.0 + y * (1.0 - t)))
            q = e * g
            d_s[then, r, :] = q
            n_s[r, :] = n
            sums_s[0, r, :] += fold(e * n)
            sums_s[1, r, :] += fold(e)
            return acc[0] + eight(q), acc[1] + eight(q * n)

        return back

    def close(acc, inv):
        mq, mqn = [jnp.sum(a, axis=0, keepdims=True) * (1.0 / inner) for a in acc]

        def last(i):
            r = rows_at(i)
            dh = ((d_s[then, r, :] - mq - n_s[r, :] * mqn) * inv).astype(BF)
            dh1_ref[r, :] = dh
            sums_s[2, r, :] += fold(dh.astype(F32))

        loop(steps, last, 10)

    def stats():
        return st_ref[0:1, :], st_ref[1:2, :]

    zero = jnp.zeros((8, length), F32)

    @pl.when(s == 0)
    def _():
        d_s[now] = mm(wc_ref[0], t_s[0]) + mm(wc_ref[1], t_s[1]) + mm(wc_ref[2], t_s[2])

    @pl.when(jnp.logical_and(s > 0, s < seqs))
    def _():
        mean, inv = stats()
        back = back_of(mean, inv)
        each = steps // 3
        acc = lax.fori_loop(3 * each, steps, back, (zero, zero), unroll=True)
        for k in range(3):
            part = mm(wc_ref[k], t_s[k])
            d_s[now] = part if k == 0 else d_s[now] + part
            for c in range(each):
                acc = back(k * each + c, acc)
        close(acc, inv)

    @pl.when(s == seqs)
    def _():
        mean, inv = stats()
        close(lax.fori_loop(0, steps, back_of(mean, inv), (zero, zero), unroll=5), inv)
        for j in range(3):
            sums_ref[j : j + 1, :] = gathered_row(sums_s[j]) * (0.5, 0.5, 1.0)[j]


def seq_from(begin, shape):
    return pl.BlockSpec((None,) + shape, lambda s: (s + begin,) + (0,) * len(shape))


def this_seq(seqs, shape):
    return pl.BlockSpec((None,) + shape, lambda s: (jnp.minimum(s, seqs - 1),) + (0,) * len(shape))


def previous_seq(shape):
    return pl.BlockSpec((None,) + shape, lambda s: (jnp.maximum(s - 1, 0),) + (0,) * len(shape))


def conv_back(dh2, halo, h1, stats, mk, wc, packs):
    seqs, inner, length = dh2.shape
    return pl.pallas_call(
        conv_back_body,
        grid=(seqs + 1,),
        in_specs=[
            this_seq(seqs, (inner, length)),
            this_seq(seqs, (8, inner)),
            previous_seq((inner, length)),
            previous_seq((8, length)),
            this_seq(seqs, (8, length)),
            full(wc.shape),
        ]
        + vec_specs(packs),
        out_specs=[previous_seq((inner, length)), full((8, inner))],
        out_shape=[sds((seqs, inner, length), BF), sds((8, inner), F32)],
        scratch_shapes=[
            pltpu.VMEM((3, inner, length), BF),
            pltpu.VMEM((2, inner, length), F32),
            pltpu.VMEM((inner, length), F32),
            pltpu.VMEM((inner, 128), F32),
            pltpu.VMEM((2, inner, 128), F32),
            pltpu.VMEM((3, inner, 128), F32),
        ],
        compiler_params=params(),
        cost_estimate=cost(dh2.size * 3 * inner, 2 * dh2.size),
        name="conv_backward",
    )(dh2, halo, h1, stats, mk, wc, *packs)


def stream_body(
    x_ref, st_ref, dy_ref, dh1_ref, w_ref, v0, v1, v2, before_ref,
    gs_ref, sums_ref,
    d_s, n_s, vw_s, sums_s,
):
    s = pl.program_id(0)
    wide, length = x_ref.shape
    steps = wide // ROWS

    @pl.when(s == 0)
    def _():
        sums_s[...] = jnp.zeros_like(sums_s)
        for j in range(2):
            spread((v0, v1, v2), vw_s, j, j, 0.5)

    d_s[...] = mm(w_ref[...], dh1_ref[...])
    mean = st_ref[0:1, :]
    inv = st_ref[1:2, :]

    def back(i, acc):
        r = rows_at(i)
        n = (x_ref[r, :].astype(F32) - mean) * inv
        g = col(vw_s, 0, r, length)
        y = n * g + col(vw_s, 1, r, length)
        t = jnp.tanh(y)
        e = d_s[r, :] * ((1.0 + t) * (1.0 + y * (1.0 - t)))
        q = e * g
        d_s[r, :] = q
        n_s[r, :] = n
        sums_s[0, r, :] += fold(e * n)
        sums_s[1, r, :] += fold(e)
        return acc[0] + eight(q), acc[1] + eight(q * n)

    zero = jnp.zeros((8, length), F32)
    qa, qn = lax.fori_loop(0, steps, back, (zero, zero), unroll=10)
    mq = jnp.sum(qa, axis=0, keepdims=True) * (1.0 / wide)
    mqn = jnp.sum(qn, axis=0, keepdims=True) * (1.0 / wide)

    def last(i):
        r = rows_at(i)
        gs = dy_ref[r, :].astype(F32) + (d_s[r, :] - mq - n_s[r, :] * mqn) * inv
        gs_ref[r, :] = gs.astype(BF)

    loop(steps, last, 10)

    @pl.when(s == pl.num_programs(0) - 1)
    def _():
        for j in range(2):
            sums_ref[j : j + 1, :] = gathered_row(sums_s[j]) * 0.5


def stream_back(x, stats, dy, dh1, w, packs, begin, count, before):
    seqs, wide, length = x.shape
    inner = dh1.shape[1]
    aliases = {8: 0} if begin else {}
    return pl.pallas_call(
        stream_body,
        grid=(count,),
        in_specs=[
            seq_from(begin, (wide, length)),
            seq_from(begin, (8, length)),
            seq_from(begin, (wide, length)),
            seq_from(begin, (inner, length)),
            full(w.shape),
        ]
        + vec_specs(packs)
        + [ANY],
        out_specs=[seq_from(begin, (wide, length)), full((8, wide))],
        out_shape=[sds((seqs, wide, length), BF), sds((8, wide), F32)],
        input_output_aliases=aliases,
        scratch_shapes=[
            pltpu.VMEM((wide, length), F32),
            pltpu.VMEM((wide, length), F32),
            pltpu.VMEM((2, wide, 128), F32),
            pltpu.VMEM((2, wide, 128), F32),
        ],
        compiler_params=params(),
        cost_estimate=cost(dh1.size * wide * count // seqs, x.size * count // seqs),
        name="grad_stream",
    )(x, stats, dy, dh1, w, *packs, before)


def output_body(x_ref, a2_ref, wt_ref, v0, v1, v2, before_ref, out_ref, sq_ref, o_s, vw_s):
    s = pl.program_id(0)
    wide, length = x_ref.shape

    @pl.when(s == 0)
    def _():
        sq_ref[...] = jnp.zeros_like(sq_ref)
        spread((v0, v1, v2), vw_s, 0, 2)

    o_s[...] = mm(wt_ref[...], a2_ref[...])

    def close(i, acc):
        r = rows_at(i)
        branch = o_s[r, :] + col(vw_s, 0, r, length)
        result = x_ref[r, :].astype(F32) + branch
        out_ref[r, :] = result.astype(BF)
        return acc[0] + eight(branch * branch), acc[1] + eight(result * result)

    zero = jnp.zeros((8, length), F32)
    b2, r2 = lax.fori_loop(0, wide // ROWS, close, (zero, zero), unroll=10)
    sq_ref[0:1, :] += jnp.sum(b2, axis=0, keepdims=True)
    sq_ref[1:2, :] += jnp.sum(r2, axis=0, keepdims=True)


def output_of(x, a2, wt, packs, begin, count, before):
    seqs, wide, length = x.shape
    inner = a2.shape[1]
    aliases = {6: 0} if begin else {}
    return pl.pallas_call(
        output_body,
        grid=(count,),
        in_specs=[seq_from(begin, (wide, length)), seq_from(begin, (inner, length))]
        + [full(wt.shape)]
        + vec_specs(packs)
        + [ANY],
        out_specs=[seq_from(begin, (wide, length)), full((8, length))],
        out_shape=[sds((seqs, wide, length), BF), sds((8, length), F32)],
        input_output_aliases=aliases,
        scratch_shapes=[
            pltpu.VMEM((wide, length), F32),
            pltpu.VMEM((1, wide, 128), F32),
        ],
        compiler_params=params(),
        cost_estimate=cost(a2.size * wide * count // seqs, x.size * count // (4 * seqs)),
        name="block_output",
    )(x, a2, wt, *packs, before)


def pack_sums_body(n_one, n_zero, n_out, *refs):
    refs, out_ref = list(refs[:-1]), refs[-1]
    bo, two, q_in, q_one, q_two = (refs.pop(0) for _ in range(5))
    one = sum(refs.pop(0)[0:3, :] for _ in range(n_one))
    zero = sum(refs.pop(0)[0:2, :] for _ in range(n_zero))
    out = sum(refs.pop(0)[0:2, :] for _ in range(n_out))
    inner = two.shape[1]
    out_ref[...] = jnp.zeros_like(out_ref)
    out_ref[0:2, :] = zero
    out_ref[2:3, :] = bo[0:1, :]
    out_ref[3:6, 0:inner] = one
    out_ref[3:6, inner : 2 * inner] = two[0:3, :]
    rows = (q_in[0:1, :], out[1:2, :], q_one[0:1, :], q_two[0:1, :], out[0:1, :])
    for j, row in enumerate(rows):
        total = jnp.sum(row, axis=1, keepdims=True)
        out_ref[6:7, j * 128 : (j + 1) * 128] = jnp.broadcast_to(total, (1, 128))


def pack_sums(bo, two, q_in, q_one, q_two, ones, zeros, outs):
    vmem = pl.BlockSpec(memory_space=pltpu.VMEM)
    args = (bo, two, q_in, q_one, q_two, *ones, *zeros, *outs)
    return pl.pallas_call(
        functools.partial(pack_sums_body, len(ones), len(zeros), len(outs)),
        in_specs=[vmem] * len(args),
        out_specs=vmem,
        out_shape=sds((8, bo.shape[1]), F32),
        compiler_params=params(16),
        name="pack_sums",
    )(*args)


def join_body(mine_ref, other_ref, mine_in, other_in, conv_ref, out_ref, in_ref):
    core = lax.rem(lax.axis_index("ctx"), 2)
    rows, inner = conv_ref.shape[1:]

    def halves(a, b, total):
        off, size = half_of(total)
        low = jnp.where(core == 0, a, b).astype(F32)
        high = jnp.where(core == 0, b, a).astype(F32)
        return size, low, high[size - off :]

    for k in range(5):
        size, low, high = halves(mine_ref[k], other_ref[k], rows)
        if k < 3:
            conv_ref[k, 0:size, :] = low
            conv_ref[k, size:rows, :] = high
        else:
            out_ref[0:size, (k - 3) * inner : (k - 2) * inner] = low
            out_ref[size:rows, (k - 3) * inner : (k - 2) * inner] = high
    size, low, high = halves(mine_in[...], other_in[...], in_ref.shape[0])
    in_ref[0:size, :] = low
    in_ref[size:, :] = high


def join_grads(rest, rows, of_in, rows_in):
    inner = of_in[0].shape[1]
    vmem = pl.BlockSpec(memory_space=pltpu.VMEM)
    return pl.pallas_call(
        join_body,
        in_specs=[vmem] * 4,
        out_specs=[vmem] * 3,
        out_shape=[
            sds((3, rows, inner), F32),
            sds((rows, 2 * inner), F32),
            sds((rows_in, inner), F32),
        ],
        compiler_params=params(32),
        name="join_grads",
    )(*rest, *of_in)


def unpack_body(counts, s_ref, *outs):
    me = lax.axis_index("dp")
    wide = s_ref.shape[1]
    inner = wide // 2

    def part(row, begin, size):
        v = s_ref[row : row + 1, begin : begin + size]
        for d in range(1, 4):
            at = begin + d * size
            v = jnp.where(me == d, s_ref[row : row + 1, at : at + size], v)
        return v.reshape(size)

    for j in range(3):
        outs[j][...] = part(j, 0, wide // 4)
    for j in range(6):
        outs[3 + j][...] = part(3 + j % 3, (j // 3) * inner, inner // 4)
    for j, count in enumerate(counts):
        outs[9 + j][...] = jnp.sqrt(s_ref[6:7, j * 128 : (j + 1) * 128] / count)


def unpack_sums(sums, counts):
    wide = sums.shape[1]
    vmem = pl.BlockSpec(memory_space=pltpu.VMEM)
    return pl.pallas_call(
        functools.partial(unpack_body, counts),
        in_specs=[vmem],
        out_specs=[vmem] * 14,
        out_shape=[sds((wide // 4,), F32)] * 3
        + [sds((wide // 8,), F32)] * 6
        + [sds((1, 128), F32)] * 5,
        compiler_params=params(16),
        name="unpack_sums",
    )(sums)


def local(
    stream, segments, cotangent, gain_zero, shift_zero, weight_in, bias_in, gain_one, shift_one,
    weight_conv, bias_conv, gain_two, shift_two, weight_out, bias_out,
):
    n_dp, n_ctx = lax.axis_size("dp"), lax.axis_size("ctx")
    assert n_dp == 4 and n_ctx & (n_ctx - 1) == 0
    me, place = lax.axis_index("dp"), lax.axis_index("ctx")
    seqs, length, wide = stream.shape
    inner = weight_conv.shape[2]
    part_w, part_i = gain_zero.shape[0], bias_in.shape[0]

    x = jnp.swapaxes(stream, 1, 2)
    dy = jnp.swapaxes(cotangent, 1, 2)

    half_in = prepare_in(
        weight_in,
        [gain_zero, shift_zero, bias_out, bias_in, gain_one, shift_one, bias_conv, gain_two, shift_two],
    )
    part_in = gather_halves(half_in)
    sent = next(part_in)
    rest_half = prepare_rest(after(weight_conv, sent), weight_out)
    sent = part_in.send(rest_half)
    stats, sq_in = input_stats(after(x, sent))
    came = part_in.send(sq_in)
    part_rest = gather_halves(after(rest_half, came))
    sent = next(part_rest)
    piece_in = (weight_in, *next(part_in))
    packs = (half_in, *piece_in[1:3])
    act_zero = first_act(x, after(stats, sent), packs)
    sent = part_rest.send(act_zero)

    padded = jnp.pad(segments, ((0, 0), (4, 4)), constant_values=-1)
    near_segs = lax.dynamic_slice_in_dim(padded, place * length, length + 8, 1)
    here = near_segs[:, 4 : 4 + length]
    same = [(near_segs[:, 4 + j : 4 + j + length] == here).astype(F32) for j in (0, -2, -4, 2, 4)]
    masks = jnp.stack(same + same[:3], axis=1)

    hidden_one, act_one, edge, sq_one, stats_one, full_in = first(
        act_zero, piece_in, (after(half_in, sent, masks), *packs[1:])
    )
    halo = shifted(edge, 1)
    part_rest.send(sq_one)
    full_conv, full_conv_t, full_out = assemble_weights(
        weight_conv, weight_out, next(part_rest)
    )
    act_two, d_hidden_two, edge_back, sums_two, sum_bo, sq_two, keep, send = conv(
        act_one, halo, dy, masks, full_conv_t, full_out, packs
    )
    halo_back = shifted(edge_back, -1)
    sum_rest = Stages(sum_shards(keep, send, True))
    own = after(half_in, sum_rest.value)
    full_out_t = transposed(after(full_out, edge_back))
    ones, zeros, outs = [], [], []
    output = grad_x = stats

    def run(what, begin, end):
        nonlocal output, grad_x
        vecs = (own, *packs[1:])
        if what == "out":
            output, sums = output_of(x, act_two, full_out_t, vecs, begin, end - begin, output)
            outs.append(sums)
        else:
            grad_x, sums = stream_back(
                x, stats, dy, d_hidden_one, full_in, vecs, begin, end - begin, grad_x
            )
            zeros.append(sums)
        return sums

    sums = run("out", 0, 1)
    own = after(own, sum_rest.step(sums))
    d_hidden_one, sums = conv_back(
        d_hidden_two, halo_back, hidden_one, stats_one, masks, full_conv, (own, *packs[1:])
    )
    ones.append(sums)
    own = after(own, sum_rest.step(sums))
    keep_in, send_in = grad(act_zero, after(d_hidden_one, own), "grad_weight_in")
    sum_in = Stages(sum_shards(keep_in, send_in, False))
    own = after(own, sum_in.value, sum_rest.step(send_in))
    sums = run("out", 1, 2)
    own = after(own, sum_in.step(sums))
    sums = run("stream", 0, 1)
    own = after(own, sum_in.step(sums), sum_rest.step(sums))
    sums = run("out", 2, seqs)
    own = after(own, sum_in.step(sums), sum_rest.step(sums))
    sums = run("stream", 1, 2)
    own = after(own, sum_in.step(sums), sum_rest.step(sums))
    sums = run("stream", 2, seqs)
    sum_rest.step(sums)
    sums = pack_sums(after(sum_bo, sum_in.step(sums)), sums_two, sq_in, sq_one, sq_two, ones, zeros, outs)
    count = float(seqs * length * n_dp * n_ctx)
    total = Stages(sum_all(sums))
    grad_weight_conv, grad_weight_out, grad_weight_in = join_grads(
        sum_rest.result(), part_i, sum_in.result(), part_w
    )
    total.step(None)
    total.step((grad_weight_out, grad_weight_in))
    sums = total.result()
    totals = unpack_sums(
        sums, (count * wide, count * wide, count * inner, count * inner, count * wide)
    )
    grad_gain_zero, grad_shift_zero, grad_bias_out = totals[0:3]
    grad_gain_one, grad_shift_one, grad_bias_in = totals[3:6]
    grad_gain_two, grad_shift_two, grad_bias_conv = totals[6:9]
    rms_in, rms_out, rms_hidden_one, rms_hidden_two, rms_branch = (v[0, 0] for v in totals[9:])
    return (
        jnp.swapaxes(output, 1, 2),
        jnp.swapaxes(grad_x, 1, 2),
        grad_gain_zero,
        grad_shift_zero,
        grad_weight_in,
        grad_bias_in,
        grad_gain_one,
        grad_shift_one,
        grad_weight_conv,
        grad_bias_conv,
        grad_gain_two,
        grad_shift_two,
        grad_weight_out,
        grad_bias_out,
        rms_in,
        rms_out,
        rms_hidden_one,
        rms_hidden_two,
        rms_branch,
    )


def solution(mesh):
    placed = (
        P("dp", "ctx", None),
        P("dp", None),
        P("dp", "ctx", None),
        P("dp"),
        P("dp"),
        P("dp", None),
        P("dp"),
        P("dp"),
        P("dp"),
        P(None, "dp", None),
        P("dp"),
        P("dp"),
        P("dp"),
        P("dp", None),
        P("dp"),
    )
    return jax.shard_map(
        local,
        mesh=mesh,
        in_specs=placed,
        out_specs=(
            P("dp", "ctx", None),
            P("dp", "ctx", None),
            P("dp"),
            P("dp"),
            P("dp", None),
            P("dp"),
            P("dp"),
            P("dp"),
            P(None, "dp", None),
            P("dp"),
            P("dp"),
            P("dp"),
            P("dp", None),
            P("dp"),
            P(),
            P(),
            P(),
            P(),
            P(),
        ),
        check_vma=False,
    )
```

```python
import functools

import jax
import jax.numpy as jnp
from jax import lax
from jax.experimental import pallas as pl
from jax.experimental.pallas import tpu as pltpu
from jax.sharding import PartitionSpec as P

F32 = jnp.float32
BF = jnp.bfloat16
EPS = 1e-05
ROWS = 16
NN = (((1,), (0,)), ((), ()))
NT = (((1,), (1,)), ((), ()))
MIB = 1024 * 1024


def by_core(value, even_mask, odd_mask):
    n_dp, n_ctx = lax.axis_size("dp"), lax.axis_size("ctx")
    masks = (even_mask, odd_mask)
    pairs = [
        (d * n_ctx + t, (d ^ masks[t % 2]) * n_ctx + t) for d in range(n_dp) for t in range(n_ctx)
    ]
    return lax.ppermute(value, ("dp", "ctx"), pairs)


def swap(value, axis, mask):
    return lax.ppermute(value, axis, [(i, i ^ mask) for i in range(lax.axis_size(axis))])


def shifted(value, by):
    size = lax.axis_size("ctx")
    return lax.ppermute(value, "ctx", [(i, i + by) for i in range(size) if 0 <= i + by < size])


def half_of(rows):
    off = rows // 2 // 16 * 16
    return off, rows - off


def gated(value, gate):
    return value if gate is None else lax.optimization_barrier((value, gate))[0]


def after(value, *others):
    return lax.optimization_barrier((value, *others))[0]


def gather_halves(half):
    first = by_core(half, 1, 2)
    gate = yield half
    sent = jnp.stack([half, gated(first, gate)])
    second = by_core(sent, 2, 1)
    gate = yield sent
    second = gated(second, gate)
    other_first = swap(first, "ctx", 1)
    other_second = swap(second, "ctx", 1)
    yield second
    yield first, second, other_first, other_second


def halved(value, bit):
    rows = value.shape[1]
    off, size = parts_of(rows)
    keep = lax.dynamic_slice_in_dim(value, bit * off, size, 1)
    return keep, lax.dynamic_slice_in_dim(value, (1 - bit) * off, size, 1)


def parts_of(rows):
    off = rows // 2 // 8 * 8
    return off, rows - off


def joined(mine, other, bit, rows):
    off, size = parts_of(rows)
    low = jnp.where(bit == 0, mine, other)
    high = jnp.where(bit == 0, other, mine)
    return jnp.concatenate([low, high[:, size - off :]], axis=1)


def sum_shards(keep, send, halving):
    got = swap(send, "ctx", 1)
    gate = yield send
    got = gated(got, gate)
    sent = (keep[2:4].astype(F32) + got[2:4].astype(F32)).astype(BF)
    one = by_core(sent, 1, 2)
    gate = yield sent
    one = gated(one, gate)
    sent = (keep[1].astype(F32) + got[1].astype(F32) + one[1].astype(F32)).astype(BF)
    two = by_core(sent, 2, 1)
    gate = yield sent
    two = gated(two, gate)
    part = keep[0].astype(F32) + got[0].astype(F32) + one[0].astype(F32) + two.astype(F32)
    place = lax.axis_index("ctx")
    masks = [1 << b for b in range(1, (lax.axis_size("ctx") - 1).bit_length())]
    split = [(mask, (place // mask) % 2) for mask in masks[: 2 if halving else 0]]
    sizes = []
    for mask, bit in split:
        sizes.append(part.shape[1])
        part, sent = halved(part, bit)
        sent = sent.astype(BF)
        came = swap(sent, "ctx", mask)
        gate = yield sent
        part = part + gated(came, gate).astype(F32)
    for mask in masks[len(split) :]:
        sent = part.astype(BF)
        came = swap(sent, "ctx", mask)
        gate = yield sent
        part = sent.astype(F32) + gated(came, gate).astype(F32)
    for mask, bit in split[::-1]:
        sent = part.astype(BF)
        came = swap(sent, "ctx", mask)
        gate = yield sent
        part = joined(sent, gated(came, gate), bit, sizes.pop())
    other = swap(part, "ctx", 1)
    gate = yield part
    yield part, gated(other, gate)


def sum_all(value):
    got = swap(value, "ctx", 1)
    gate = yield value
    value = value + gated(got, gate)
    groups = [("dp", (1, 2, 3)), ("ctx", (2, 4, 6))]
    mask = 8
    while mask < lax.axis_size("ctx"):
        groups.append(("ctx", (mask,)))
        mask *= 2
    for axis, masks in groups:
        got = [value] + [swap(value, axis, m) for m in masks]
        gate = yield value
        if len(got) == 4:
            a, b = got[0] + got[1], got[2] + got[3]
            value = gated(a, gate) + b
        else:
            value = gated(got[0], gate) + got[1]
    yield value


class Stages:
    def __init__(self, stages):
        self.stages, self.value, self.left = stages, next(stages), True

    def step(self, gate):
        try:
            self.value = self.stages.send(gate)
        except StopIteration:
            self.left = False
        return self.value

    def result(self):
        while self.left:
            self.step(None)
        return self.value


def mm(left, right, dims=NN):
    return lax.dot_general(left, right, dims, preferred_element_type=F32)


def silu_of_half(y):
    return y * (1.0 + jnp.tanh(y))


def loop(count, body, unroll):
    lax.fori_loop(0, count, lambda i, _: (body(i), 0)[1], 0, unroll=unroll)


def full(shape):
    return pl.BlockSpec(shape, lambda s: (0,) * len(shape), pipeline_mode=pl.Buffered(1))


def seq(shape):
    return pl.BlockSpec((None,) + shape, lambda s: (s,) + (0,) * len(shape))


ANY = pl.BlockSpec(memory_space=pl.ANY)


def sds(shape, dtype):
    return jax.ShapeDtypeStruct(shape, dtype)


def rows_at(i, base=0):
    return pl.ds(pl.multiple_of(i * ROWS + base, ROWS), ROWS)


def lanes(tile, width):
    return jnp.concatenate([tile] * (width // 128), axis=1)


def col(ref, j, r, width):
    return lanes(ref[j, r, :], width)


def fold(v):
    t = v[:, 0:128]
    for j in range(1, v.shape[1] // 128):
        t = t + v[:, j * 128 : (j + 1) * 128]
    return t


def eight(v):
    return v[0:8] + v[8:16]


def spread(packs, out_ref, j, row, scale=1.0):
    own, near, far = packs
    me, core = lax.axis_index("dp"), lax.rem(lax.axis_index("ctx"), 2)
    part = out_ref.shape[1] // 4
    for mask, ref in ((0, own), (1 + core, near), (2 - core, far.at[0]), (3, far.at[1])):
        start = pl.multiple_of(jnp.bitwise_xor(me, mask) * part, 8)
        v = ref[...].astype(F32)[row : row + 1, 0:part] * scale
        out_ref[j, pl.ds(start, part), :] = jnp.broadcast_to(v, (128, part)).T


def gathered_row(sums):
    return jnp.sum(sums.T, axis=0, keepdims=True)


def row_stats(count, load, width, length):
    def total(i, a):
        return a + eight(load(i))

    zero = jnp.zeros((8, length), F32)
    a = lax.fori_loop(0, count, total, zero, unroll=10)
    mean = jnp.sum(a, axis=0, keepdims=True) * (1.0 / width)

    def squares(i, a):
        c = load(i) - mean
        return a + eight(c * c)

    a = lax.fori_loop(0, count, squares, zero, unroll=10)
    var = jnp.sum(a, axis=0, keepdims=True) * (1.0 / width)
    return mean, var


def start_load(pieces, dst, sems):
    shard, first, second, other_first, other_second = pieces
    rows = shard.shape[0]
    off, size = half_of(rows)
    me, core = lax.axis_index("dp"), lax.rem(lax.axis_index("ctx"), 2)
    near = jnp.bitwise_xor(me, 1 + core)
    far = jnp.bitwise_xor(me, 2 - core)
    both = jnp.bitwise_xor(me, 3)

    def at(device, half, count):
        return dst.at[pl.ds(pl.multiple_of(device * rows + half * off, 16), count), :]

    batch_one = [
        (shard, at(me, 0, rows)),
        (first.at[0:size], at(near, core, size)),
        (second.at[0, 0:size], at(far, core, size)),
        (second.at[1, 0:size], at(both, core, size)),
    ]
    batch_two = [
        (other_first.at[0:size], at(far, 1 - core, size)),
        (other_second.at[0, 0:size], at(near, 1 - core, size)),
        (other_second.at[1, 0:size], at(both, 1 - core, size)),
    ]
    copies = [
        pltpu.make_async_copy(src, to, sems.at[i])
        for i, (src, to) in enumerate(batch_one + batch_two)
    ]
    for c in copies[:4]:
        c.start()
    return copies


def finish_load(copies):
    for c in copies[:4]:
        c.wait()
    for c in copies[4:]:
        c.start()
    for c in copies[4:]:
        c.wait()


def assemble(shard, pieces, wide_s):
    first, second, other_first, other_second = pieces
    rows = shard.shape[0]
    off, _ = half_of(rows)
    me, core = lax.axis_index("dp"), lax.rem(lax.axis_index("ctx"), 2)
    near = jnp.bitwise_xor(me, 1 + core)
    far = jnp.bitwise_xor(me, 2 - core)
    both = jnp.bitwise_xor(me, 3)

    def put(device, half, piece):
        start = pl.ds(pl.multiple_of(device * rows + half * off, 8), piece.shape[0])
        wide_s[start, :] = piece.astype(F32)

    put(me, 0, shard)
    put(near, core, first[...])
    put(far, core, second[0])
    put(both, core, second[1])
    put(far, 1 - core, other_first[...])
    put(near, 1 - core, other_second[0])
    put(both, 1 - core, other_second[1])
    return wide_s[...].astype(BF)


def params(mib=60):
    return pltpu.CompilerParams(vmem_limit_bytes=mib * MIB)


def cost(products, entries):
    return pl.CostEstimate(
        flops=40 * products + 800 * entries, bytes_accessed=1, transcendentals=0
    )


def split_grad(acc_ref, keep_ref, send_ref, taps, first_block=None, slots=(0, 1, 2, 3)):
    me, core = lax.axis_index("dp"), lax.rem(lax.axis_index("ctx"), 2)
    block = acc_ref.shape[0] // taps
    width = keep_ref.shape[-1]
    rows = block // 4
    off, size = half_of(rows)
    mine = (0, 2 - core, 1 + core, 3)
    theirs = (0, 1 + core, 2 - core, 3)
    for j in slots:
        for k in range(taps):
            a = jnp.bitwise_xor(me, mine[j]) * rows + core * off + k * block
            b = jnp.bitwise_xor(me, theirs[j]) * rows + (1 - core) * off + k * block
            for ref, begin in ((keep_ref, a), (send_ref, b)):
                v = acc_ref[pl.ds(pl.multiple_of(begin, 8), size), :].astype(BF)
                if taps > 1:
                    ref[j, k] = v
                elif first_block is None:
                    ref[j] = v
                else:
                    for h in range(v.shape[1] // width):
                        ref[j, first_block + h] = v[:, h * width : (h + 1) * width]


def prepare_in_body(*refs):
    w_ref, out_ref, rows_s = refs[0], refs[-2], refs[-1]
    off, size = half_of(w_ref.shape[0])
    core = lax.rem(lax.axis_index("ctx"), 2)
    out_ref[0:size, :] = w_ref[pl.ds(pl.multiple_of(core * off, 16), size), :]
    rows_s[...] = jnp.zeros_like(rows_s)
    for j, ref in enumerate(refs[1:-2]):
        n = ref.shape[0]
        rows_s[j : j + 1, 0:n] = ref[...].astype(F32).reshape(1, n)
    out_ref[size:, :] = rows_s[...].astype(BF)


def prepare_in(weight, vectors):
    rows, inner = weight.shape
    size = half_of(rows)[1]
    assert size % 16 == 0 and max(v.shape[0] for v in vectors) <= inner and len(vectors) <= 16
    vmem = pl.BlockSpec(memory_space=pltpu.VMEM)
    return pl.pallas_call(
        prepare_in_body,
        in_specs=[vmem] * (1 + len(vectors)),
        out_specs=vmem,
        out_shape=sds((size + 16, inner), BF),
        scratch_shapes=[pltpu.VMEM((16, inner), F32)],
        compiler_params=params(),
        name="prepare_in",
    )(weight, *vectors)


def prepare_rest_body(wc_ref, wo_ref, out_ref):
    inner = wc_ref.shape[2]
    off, size = half_of(wc_ref.shape[1])
    core = lax.rem(lax.axis_index("ctx"), 2)
    r = pl.ds(pl.multiple_of(core * off, 16), size)
    for k in range(3):
        out_ref[k] = wc_ref[k, r, :]
    half = wo_ref[r, :]
    out_ref[3] = half[:, 0:inner]
    out_ref[4] = half[:, inner:]


def prepare_rest(weight_conv, weight_out):
    inner = weight_conv.shape[2]
    vmem = pl.BlockSpec(memory_space=pltpu.VMEM)
    return pl.pallas_call(
        prepare_rest_body,
        in_specs=[vmem] * 2,
        out_specs=vmem,
        out_shape=sds((5, half_of(weight_conv.shape[1])[1], inner), BF),
        compiler_params=params(),
        name="prepare_rest",
    )(weight_conv, weight_out)


def vec_specs(packs):
    own, first, second = packs
    inner = own.shape[1]
    at = own.shape[0] // 16 - 1
    row = pl.BlockSpec((16, inner), lambda s: (at, 0))
    return [row, row, pl.BlockSpec((2, 16, inner), lambda s: (0, at, 0))]


def stats_body(x_ref, st_ref, sq_ref):
    wide, length = x_ref.shape

    @pl.when(pl.program_id(0) == 0)
    def _():
        sq_ref[...] = jnp.zeros_like(sq_ref)

    mean, var = row_stats(wide // ROWS, lambda i: x_ref[rows_at(i), :].astype(F32), wide, length)
    st_ref[0:1, :] = mean
    st_ref[1:2, :] = lax.rsqrt(var + EPS)
    sq_ref[0:1, :] += (var + mean * mean) * float(wide)


def input_stats(x):
    seqs, wide, length = x.shape
    return pl.pallas_call(
        stats_body,
        grid=(seqs,),
        in_specs=[seq((wide, length))],
        out_specs=[seq((8, length)), full((8, length))],
        out_shape=[sds((seqs, 8, length), F32), sds((8, length), F32)],
        compiler_params=params(),
        cost_estimate=cost(0, x.size // 4),
        name="input_stats",
    )(x)


def act_body(x_ref, st_ref, v0, v1, v2, a0_ref, vw_s):
    wide, length = x_ref.shape

    @pl.when(pl.program_id(0) == 0)
    def _():
        for j in range(2):
            spread((v0, v1, v2), vw_s, j, j, 0.5)

    mean = st_ref[0:1, :]
    inv = st_ref[1:2, :]

    def act0(i):
        r = rows_at(i)
        y = (x_ref[r, :].astype(F32) - mean) * inv * col(vw_s, 0, r, length)
        a0_ref[r, :] = silu_of_half(y + col(vw_s, 1, r, length)).astype(BF)

    loop(wide // ROWS, act0, 10)


def first_act(x, stats, packs):
    seqs, wide, length = x.shape
    return pl.pallas_call(
        act_body,
        grid=(seqs,),
        in_specs=[seq((wide, length)), seq((8, length))] + vec_specs(packs),
        out_specs=seq((wide, length)),
        out_shape=sds((seqs, wide, length), BF),
        scratch_shapes=[pltpu.VMEM((2, wide, 128), F32)],
        compiler_params=params(),
        cost_estimate=cost(0, x.size // 2),
        name="first_act",
    )(x, stats, *packs)


def first_body(
    a0_ref, p0, p1, p2, p3, p4, v0, v1, v2,
    h1_ref, a1_ref, edge_ref, sq_ref, st_ref, w_ref,
    w_s, wt_s, vi_s, sems, out_sem,
):
    s = pl.program_id(0)
    inner, length = h1_ref.shape

    @pl.when(s == 0)
    def _():
        copies = start_load((p0, p1, p2, p3, p4), w_s, sems)
        sq_ref[...] = jnp.zeros_like(sq_ref)
        for j in range(3):
            spread((v0, v1, v2), vi_s, j, j + 3, (1.0, 0.5, 0.5)[j])
        finish_load(copies)
        pltpu.make_async_copy(w_s, w_ref, out_sem).start()
        wt_s[...] = w_s[...].T

    h1_ref[...] = mm(wt_s[...], a0_ref[...]) + lanes(vi_s[0], length)
    mean1, var1 = row_stats(inner // ROWS, lambda i: h1_ref[rows_at(i), :], inner, length)
    inv1 = lax.rsqrt(var1 + EPS)
    st_ref[0:1, :] = mean1
    st_ref[1:2, :] = inv1
    sq_ref[0:1, :] += (var1 + mean1 * mean1) * float(inner)

    def act1(i):
        r = rows_at(i)
        y = (h1_ref[r, :] - mean1) * inv1 * col(vi_s, 1, r, length) + col(vi_s, 2, r, length)
        a1_ref[r, :] = silu_of_half(y).astype(BF)

    loop(inner // ROWS, act1, 10)
    edge_ref[...] = a1_ref[:, length - 128 :].astype(F32).T[120:128, :].astype(BF)

    @pl.when(s == pl.num_programs(0) - 1)
    def _():
        pltpu.make_async_copy(w_s, w_ref, out_sem).wait()


def first(a0, pieces, packs):
    seqs, wide, length = a0.shape
    inner = pieces[0].shape[1]
    return pl.pallas_call(
        first_body,
        grid=(seqs,),
        in_specs=[seq((wide, length))] + [ANY] * 5 + vec_specs(packs),
        out_specs=[
            seq((inner, length)),
            seq((inner, length)),
            seq((8, inner)),
            full((8, length)),
            seq((8, length)),
            ANY,
        ],
        out_shape=[
            sds((seqs, inner, length), F32),
            sds((seqs, inner, length), BF),
            sds((seqs, 8, inner), BF),
            sds((8, length), F32),
            sds((seqs, 8, length), F32),
            sds((wide, inner), BF),
        ],
        scratch_shapes=[
            pltpu.VMEM((wide, inner), BF),
            pltpu.VMEM((inner, wide), BF),
            pltpu.VMEM((3, inner, 128), F32),
            pltpu.SemaphoreType.DMA((7,)),
            pltpu.SemaphoreType.DMA,
        ],
        compiler_params=params(),
        cost_estimate=cost(a0.size * inner, a0.size),
        name="first_product",
    )(a0, *pieces, *packs)


def assemble_body(wc_own, wo_own, f, g, of, og, wc_ref, wct_ref, wo_ref, tap_s):
    step = pl.program_id(0)
    inner = wc_ref.shape[0]

    @pl.when(step < 3)
    def _():
        w = assemble(wc_own[...], (f, g, of, og), tap_s)
        wc_ref[...] = w
        t = w.T
        for k in range(3):

            @pl.when(step == k)
            def _():
                wct_ref[:, k * inner : (k + 1) * inner] = t

    for k in range(2):

        @pl.when(step == 3 + k)
        def _():
            own = wo_own[:, k * inner : (k + 1) * inner]
            wo_ref[...] = assemble(own, (f, g, of, og), tap_s)


def assemble_weights(own_conv, own_out, pieces):
    inner = own_conv.shape[2]
    rows, size = own_conv.shape[1], pieces[0].shape[1]
    one = pl.BlockSpec((None, size, inner), lambda k: (k, 0, 0))
    two = pl.BlockSpec((2, None, size, inner), lambda k: (0, k, 0, 0))
    return pl.pallas_call(
        assemble_body,
        grid=(5,),
        in_specs=[
            pl.BlockSpec((None, rows, inner), lambda k: (jnp.minimum(k, 2), 0, 0)),
            full(own_out.shape),
            one,
            two,
            one,
            two,
        ],
        out_specs=[
            pl.BlockSpec((None, inner, inner), lambda k: (jnp.minimum(k, 2), 0, 0)),
            full((inner, 3 * inner)),
            pl.BlockSpec((None, inner, inner), lambda k: (jnp.maximum(k - 3, 0), 0, 0)),
        ],
        out_shape=[
            sds((3, inner, inner), BF),
            sds((inner, 3 * inner), BF),
            sds((2, inner, inner), BF),
        ],
        scratch_shapes=[pltpu.VMEM((inner, inner), F32)],
        compiler_params=params(30),
        cost_estimate=cost(0, 4 * inner * inner),
        name="assemble_weights",
    )(own_conv, own_out, *pieces)


def transpose_body(w_ref, wt_ref):
    inner = w_ref.shape[1]
    for k in range(2):
        wt_ref[k * inner : (k + 1) * inner, :] = w_ref[k].T


def transposed(w):
    inner = w.shape[1]
    vmem = pl.BlockSpec(memory_space=pltpu.VMEM)
    return pl.pallas_call(
        transpose_body,
        in_specs=[vmem],
        out_specs=vmem,
        out_shape=sds((2 * inner, inner), BF),
        compiler_params=params(),
        name="transpose_out",
    )(w)


def conv_body(
    a1_ref, halo_ref, dy_ref, dyp_ref, mk_ref, wct_ref, wo_ref, v0, v1, v2,
    a2_ref, dh2_ref, edge_ref, sums_ref, bo_ref, sq_ref, keep_ref, send_ref,
    st_s, a2_s, dh_s, h_s, d_s, hl_s, vi_s, sums_s, bo_s, acc_s, out_s, mi_s, keep_s, send_s, gsem,
):
    s = pl.program_id(0)
    seqs = pl.num_programs(0) - 1
    inner, length = a1_ref.shape
    wide = dy_ref.shape[0]
    steps = inner // ROWS
    now, then = lax.rem(s, 2), lax.rem(s + 1, 2)

    @pl.when(s == 0)
    def _():
        sq_ref[...] = jnp.zeros_like(sq_ref)
        sums_s[...] = jnp.zeros_like(sums_s)
        bo_s[...] = jnp.zeros_like(bo_s)
        acc_s[...] = jnp.zeros_like(acc_s)
        out_s[...] = jnp.zeros_like(out_s)
        for j in range(3):
            spread((v0, v1, v2), vi_s, j, j + 6, (1.0, 0.5, 0.5)[j])

    @pl.when(s < seqs)
    def _():
        hl_s[...] = jnp.concatenate(
            [jnp.zeros((120, inner), F32), halo_ref[...].astype(F32)], axis=0
        ).T
        m1 = mk_ref[1:2, :]
        m2 = mk_ref[2:3, :]

        def build(i):
            r = rows_at(i)
            b = a1_ref[r, :]
            v = jnp.concatenate([b.astype(F32), hl_s[r, :]], axis=1)
            st_s[now, r, :] = b
            st_s[now, rows_at(i, inner), :] = (pltpu.roll(v, 2, 1)[:, 0:length] * m1).astype(BF)
            st_s[now, rows_at(i, 2 * inner), :] = (pltpu.roll(v, 4, 1)[:, 0:length] * m2).astype(BF)

        loop(steps, build, 25)
        h_s[...] = mm(wct_ref[...], st_s[now]) + lanes(vi_s[0], length)
        d_s[...] = mm(wo_ref[0], dy_ref[0:inner, :]) + mm(wo_ref[1], dy_ref[inner:, :])

        mean, var = row_stats(steps, lambda i: h_s[rows_at(i), :], inner, length)
        mi_s[0:1, :] = mean
        mi_s[1:2, :] = lax.rsqrt(var + EPS)
        sq_ref[0:1, :] += (var + mean * mean) * float(inner)

    mean = mi_s[0:1, :]
    inv = mi_s[1:2, :]
    zero = jnp.zeros((8, length), F32)

    def back(i, acc):
        r = rows_at(i)
        n = (h_s[r, :] - mean) * inv
        g = col(vi_s, 1, r, length)
        y = n * g + col(vi_s, 2, r, length)
        t = jnp.tanh(y)
        up = 1.0 + t
        a2 = (y * up).astype(BF)
        a2_ref[r, :] = a2
        a2_s[now, r, :] = a2
        e = d_s[r, :] * (up * (1.0 + y * (1.0 - t)))
        q = e * g
        d_s[r, :] = q
        h_s[r, :] = n
        sums_s[0, r, :] += fold(e * n)
        sums_s[1, r, :] += fold(e)
        return acc[0] + eight(q), acc[1] + eight(q * n)

    def means(acc):
        return [jnp.sum(a, axis=0, keepdims=True) * (1.0 / inner) for a in acc]

    def last(i, mq, mqn):
        r = rows_at(i)
        dh = ((d_s[r, :] - mq - h_s[r, :] * mqn) * inv).astype(BF)
        dh2_ref[r, :] = dh
        dh_s[now, r, :] = dh
        sums_s[2, r, :] += fold(dh.astype(F32))

    def block(j):
        return pl.ds(pl.multiple_of(j * inner, 16), inner)

    def grad_tap(j):
        acc_s[block(j), :] += mm(st_s[then, block(j), :], dh_s[then], NT)

    def grad_out(k):
        r = pl.ds(pl.multiple_of(k * (inner // 2), 16), inner // 2)
        out_s[r, :] += mm(a2_s[then, r, :], dyp_ref[...], NT)

    def bias(i):
        r = rows_at(i)
        bo_s[r, :] += fold(dyp_ref[r, :].astype(F32))

    @pl.when(s == 0)
    def _():
        acc = lax.fori_loop(0, steps, back, (zero, zero), unroll=10)
        mq, mqn = means(acc)
        loop(steps, lambda i: last(i, mq, mqn), 5)

    @pl.when(jnp.logical_and(s > 0, s < seqs))
    def _():
        each, some = steps // 3, wide // ROWS // 3
        acc = lax.fori_loop(3 * each, steps, back, (zero, zero), unroll=True)
        for i in range(3 * some, wide // ROWS):
            bias(i)

        def tap(j, acc):
            grad_tap(j)
            for c in range(each):
                acc = back(j * each + c, acc)
            for c in range(some):
                bias(j * some + c)
            return acc

        mq, mqn = means(lax.fori_loop(0, 3, tap, acc))

        def out(k):
            grad_out(k)
            for c in range(steps // 2):
                last(k * (steps // 2) + c, mq, mqn)

        loop(2, out, 1)

    @pl.when(s < seqs)
    def _():
        edge_ref[...] = dh2_ref[:, 0:128].astype(F32).T[0:8, :].astype(BF)

    @pl.when(s == seqs)
    def _():
        loop(3, grad_tap, 1)
        loop(2, grad_out, 1)
        loop(wide // ROWS, bias, 5)
        for j in range(3):
            sums_ref[j : j + 1, :] = gathered_row(sums_s[j]) * (0.5, 0.5, 1.0)[j]
        bo_ref[0:1, :] = gathered_row(bo_s[...])
        copies = []
        for j in range(4):
            split_grad(acc_s, keep_s, send_s, 3, slots=(j,))
            split_grad(out_s, keep_s, send_s, 1, 3, slots=(j,))
            for i, (src, dst) in enumerate(((send_s, send_ref), (keep_s, keep_ref))):
                copies.append(pltpu.make_async_copy(src.at[j], dst.at[j], gsem.at[2 * j + i]))
                copies[-1].start()
        for c in copies:
            c.wait()


def conv(a1, halo, dy, mk, wct, wo, packs):
    seqs, inner, length = a1.shape
    wide = dy.shape[1]
    assert inner % (2 * ROWS) == 0
    size = half_of(inner // 4)[1]

    this, previous = functools.partial(this_seq, seqs), previous_seq

    return pl.pallas_call(
        conv_body,
        grid=(seqs + 1,),
        in_specs=[
            this((inner, length)),
            this((8, inner)),
            this((wide, length)),
            previous((wide, length)),
            this((8, length)),
        ]
        + [full(p.shape) for p in (wct, wo)]
        + vec_specs(packs),
        out_specs=[
            this((inner, length)),
            this((inner, length)),
            this((8, inner)),
            full((8, inner)),
            full((8, wide)),
            full((8, length)),
            ANY,
            ANY,
        ],
        out_shape=[
            sds((seqs, inner, length), BF),
            sds((seqs, inner, length), BF),
            sds((seqs, 8, inner), BF),
            sds((8, inner), F32),
            sds((8, wide), F32),
            sds((8, length), F32),
            sds((4, 5, size, inner), BF),
            sds((4, 5, size, inner), BF),
        ],
        scratch_shapes=[
            pltpu.VMEM((2, 3 * inner, length), BF),
            pltpu.VMEM((2, inner, length), BF),
            pltpu.VMEM((2, inner, length), BF),
            pltpu.VMEM((inner, length), F32),
            pltpu.VMEM((inner, length), F32),
            pltpu.VMEM((inner, 128), F32),
            pltpu.VMEM((3, inner, 128), F32),
            pltpu.VMEM((3, inner, 128), F32),
            pltpu.VMEM((wide, 128), F32),
            pltpu.VMEM((3 * inner, inner), F32),
            pltpu.VMEM((inner, wide), F32),
            pltpu.VMEM((8, length), F32),
            pltpu.VMEM((4, 5, size, inner), BF),
            pltpu.VMEM((4, 5, size, inner), BF),
            pltpu.SemaphoreType.DMA((8,)),
        ],
        compiler_params=params(),
        cost_estimate=cost(a1.size * (6 * inner + 2 * wide), 2 * a1.size),
        name="conv_and_third_norm",
    )(a1, halo, dy, dy, mk, wct, wo, *packs)


def grad_body(a_ref, b_ref, keep_ref, send_ref, acc_s):
    s = pl.program_id(0)

    @pl.when(s == 0)
    def _():
        acc_s[...] = mm(a_ref[...], b_ref[...], NT)

    @pl.when(s > 0)
    def _():
        acc_s[...] += mm(a_ref[...], b_ref[...], NT)

    @pl.when(s == pl.num_programs(0) - 1)
    def _():
        split_grad(acc_s, keep_ref, send_ref, 1)


def grad(a, b, name):
    seqs, m, length = a.shape
    n = b.shape[1]
    size = half_of(m // 4)[1]
    return pl.pallas_call(
        grad_body,
        grid=(seqs,),
        in_specs=[seq((m, length)), seq((n, length))],
        out_specs=[full((4, size, n)), full((4, size, n))],
        out_shape=[sds((4, size, n), BF), sds((4, size, n), BF)],
        scratch_shapes=[pltpu.VMEM((m, n), F32)],
        compiler_params=params(),
        cost_estimate=cost(a.size * n, 0),
        name=name,
    )(a, b)


def shift_back(dh2_ref, halo_ref, mk_ref, hl_s, t_s):
    inner, length = dh2_ref.shape
    hl_s[...] = jnp.concatenate(
        [halo_ref[...].astype(F32), jnp.zeros((120, inner), F32)], axis=0
    ).T
    f1 = mk_ref[3:4, :]
    f2 = mk_ref[4:5, :]

    def build(i):
        r = rows_at(i)
        b = dh2_ref[r, :]
        v = jnp.concatenate([b.astype(F32), hl_s[r, :]], axis=1)
        t_s[0, r, :] = b
        t_s[1, r, :] = (pltpu.roll(v, length + 126, 1)[:, 0:length] * f1).astype(BF)
        t_s[2, r, :] = (pltpu.roll(v, length + 124, 1)[:, 0:length] * f2).astype(BF)

    loop(inner // ROWS, build, 25)


def conv_back_body(
    dh2_ref, halo_ref, h1_ref, st_ref, mk_ref, wc_ref, v0, v1, v2,
    dh1_ref, sums_ref,
    t_s, d_s, n_s, hl_s, vi_s, sums_s,
):
    s = pl.program_id(0)
    seqs = pl.num_programs(0) - 1
    inner, length = dh2_ref.shape
    steps = inner // ROWS
    now, then = lax.rem(s, 2), lax.rem(s + 1, 2)

    @pl.when(s == 0)
    def _():
        sums_s[...] = jnp.zeros_like(sums_s)
        for j in range(2):
            spread((v0, v1, v2), vi_s, j, j + 4, 0.5)

    @pl.when(s < seqs)
    def _():
        shift_back(dh2_ref, halo_ref, mk_ref, hl_s, t_s)

    def back_of(mean, inv):
        def back(i, acc):
            r = rows_at(i)
            n = (h1_ref[r, :] - mean) * inv
            g = col(vi_s, 0, r, length)
            y = n * g + col(vi_s, 1, r, length)
            t = jnp.tanh(y)
            e = d_s[then, r, :] * ((1.0 + t) * (1.0 + y * (1.0 - t)))
            q = e * g
            d_s[then, r, :] = q
            n_s[r, :] = n
            sums_s[0, r, :] += fold(e * n)
            sums_s[1, r, :] += fold(e)
            return acc[0] + eight(q), acc[1] + eight(q * n)

        return back

    def close(acc, inv):
        mq, mqn = [jnp.sum(a, axis=0, keepdims=True) * (1.0 / inner) for a in acc]

        def last(i):
            r = rows_at(i)
            dh = ((d_s[then, r, :] - mq - n_s[r, :] * mqn) * inv).astype(BF)
            dh1_ref[r, :] = dh
            sums_s[2, r, :] += fold(dh.astype(F32))

        loop(steps, last, 10)

    def stats():
        return st_ref[0:1, :], st_ref[1:2, :]

    zero = jnp.zeros((8, length), F32)

    @pl.when(s == 0)
    def _():
        d_s[now] = mm(wc_ref[0], t_s[0]) + mm(wc_ref[1], t_s[1]) + mm(wc_ref[2], t_s[2])

    @pl.when(jnp.logical_and(s > 0, s < seqs))
    def _():
        mean, inv = stats()
        back = back_of(mean, inv)
        each = steps // 3
        acc = lax.fori_loop(3 * each, steps, back, (zero, zero), unroll=True)
        for k in range(3):
            part = mm(wc_ref[k], t_s[k])
            d_s[now] = part if k == 0 else d_s[now] + part
            for c in range(each):
                acc = back(k * each + c, acc)
        close(acc, inv)

    @pl.when(s == seqs)
    def _():
        mean, inv = stats()
        close(lax.fori_loop(0, steps, back_of(mean, inv), (zero, zero), unroll=5), inv)
        for j in range(3):
            sums_ref[j : j + 1, :] = gathered_row(sums_s[j]) * (0.5, 0.5, 1.0)[j]


def seq_from(begin, shape):
    return pl.BlockSpec((None,) + shape, lambda s: (s + begin,) + (0,) * len(shape))


def this_seq(seqs, shape):
    return pl.BlockSpec((None,) + shape, lambda s: (jnp.minimum(s, seqs - 1),) + (0,) * len(shape))


def previous_seq(shape):
    return pl.BlockSpec((None,) + shape, lambda s: (jnp.maximum(s - 1, 0),) + (0,) * len(shape))


def conv_back(dh2, halo, h1, stats, mk, wc, packs):
    seqs, inner, length = dh2.shape
    return pl.pallas_call(
        conv_back_body,
        grid=(seqs + 1,),
        in_specs=[
            this_seq(seqs, (inner, length)),
            this_seq(seqs, (8, inner)),
            previous_seq((inner, length)),
            previous_seq((8, length)),
            this_seq(seqs, (8, length)),
            full(wc.shape),
        ]
        + vec_specs(packs),
        out_specs=[previous_seq((inner, length)), full((8, inner))],
        out_shape=[sds((seqs, inner, length), BF), sds((8, inner), F32)],
        scratch_shapes=[
            pltpu.VMEM((3, inner, length), BF),
            pltpu.VMEM((2, inner, length), F32),
            pltpu.VMEM((inner, length), F32),
            pltpu.VMEM((inner, 128), F32),
            pltpu.VMEM((2, inner, 128), F32),
            pltpu.VMEM((3, inner, 128), F32),
        ],
        compiler_params=params(),
        cost_estimate=cost(dh2.size * 3 * inner, 2 * dh2.size),
        name="conv_backward",
    )(dh2, halo, h1, stats, mk, wc, *packs)


def stream_body(
    x_ref, st_ref, dy_ref, dh1_ref, w_ref, v0, v1, v2, before_ref,
    gs_ref, sums_ref,
    d_s, n_s, vw_s, sums_s,
):
    s = pl.program_id(0)
    wide, length = x_ref.shape
    steps = wide // ROWS

    @pl.when(s == 0)
    def _():
        sums_s[...] = jnp.zeros_like(sums_s)
        for j in range(2):
            spread((v0, v1, v2), vw_s, j, j, 0.5)

    d_s[...] = mm(w_ref[...], dh1_ref[...])
    mean = st_ref[0:1, :]
    inv = st_ref[1:2, :]

    def back(i, acc):
        r = rows_at(i)
        n = (x_ref[r, :].astype(F32) - mean) * inv
        g = col(vw_s, 0, r, length)
        y = n * g + col(vw_s, 1, r, length)
        t = jnp.tanh(y)
        e = d_s[r, :] * ((1.0 + t) * (1.0 + y * (1.0 - t)))
        q = e * g
        d_s[r, :] = q
        n_s[r, :] = n
        sums_s[0, r, :] += fold(e * n)
        sums_s[1, r, :] += fold(e)
        return acc[0] + eight(q), acc[1] + eight(q * n)

    zero = jnp.zeros((8, length), F32)
    qa, qn = lax.fori_loop(0, steps, back, (zero, zero), unroll=10)
    mq = jnp.sum(qa, axis=0, keepdims=True) * (1.0 / wide)
    mqn = jnp.sum(qn, axis=0, keepdims=True) * (1.0 / wide)

    def last(i):
        r = rows_at(i)
        gs = dy_ref[r, :].astype(F32) + (d_s[r, :] - mq - n_s[r, :] * mqn) * inv
        gs_ref[r, :] = gs.astype(BF)

    loop(steps, last, 10)

    @pl.when(s == pl.num_programs(0) - 1)
    def _():
        for j in range(2):
            sums_ref[j : j + 1, :] = gathered_row(sums_s[j]) * 0.5


def stream_back(x, stats, dy, dh1, w, packs, begin, count, before):
    seqs, wide, length = x.shape
    inner = dh1.shape[1]
    aliases = {8: 0} if begin else {}
    return pl.pallas_call(
        stream_body,
        grid=(count,),
        in_specs=[
            seq_from(begin, (wide, length)),
            seq_from(begin, (8, length)),
            seq_from(begin, (wide, length)),
            seq_from(begin, (inner, length)),
            full(w.shape),
        ]
        + vec_specs(packs)
        + [ANY],
        out_specs=[seq_from(begin, (wide, length)), full((8, wide))],
        out_shape=[sds((seqs, wide, length), BF), sds((8, wide), F32)],
        input_output_aliases=aliases,
        scratch_shapes=[
            pltpu.VMEM((wide, length), F32),
            pltpu.VMEM((wide, length), F32),
            pltpu.VMEM((2, wide, 128), F32),
            pltpu.VMEM((2, wide, 128), F32),
        ],
        compiler_params=params(),
        cost_estimate=cost(dh1.size * wide * count // seqs, x.size * count // seqs),
        name="grad_stream",
    )(x, stats, dy, dh1, w, *packs, before)


def output_body(x_ref, a2_ref, wt_ref, v0, v1, v2, before_ref, out_ref, sq_ref, o_s, vw_s):
    s = pl.program_id(0)
    wide, length = x_ref.shape

    @pl.when(s == 0)
    def _():
        sq_ref[...] = jnp.zeros_like(sq_ref)
        spread((v0, v1, v2), vw_s, 0, 2)

    o_s[...] = mm(wt_ref[...], a2_ref[...])

    def close(i, acc):
        r = rows_at(i)
        branch = o_s[r, :] + col(vw_s, 0, r, length)
        result = x_ref[r, :].astype(F32) + branch
        out_ref[r, :] = result.astype(BF)
        return acc[0] + eight(branch * branch), acc[1] + eight(result * result)

    zero = jnp.zeros((8, length), F32)
    b2, r2 = lax.fori_loop(0, wide // ROWS, close, (zero, zero), unroll=10)
    sq_ref[0:1, :] += jnp.sum(b2, axis=0, keepdims=True)
    sq_ref[1:2, :] += jnp.sum(r2, axis=0, keepdims=True)


def output_of(x, a2, wt, packs, begin, count, before):
    seqs, wide, length = x.shape
    inner = a2.shape[1]
    aliases = {6: 0} if begin else {}
    return pl.pallas_call(
        output_body,
        grid=(count,),
        in_specs=[seq_from(begin, (wide, length)), seq_from(begin, (inner, length))]
        + [full(wt.shape)]
        + vec_specs(packs)
        + [ANY],
        out_specs=[seq_from(begin, (wide, length)), full((8, length))],
        out_shape=[sds((seqs, wide, length), BF), sds((8, length), F32)],
        input_output_aliases=aliases,
        scratch_shapes=[
            pltpu.VMEM((wide, length), F32),
            pltpu.VMEM((1, wide, 128), F32),
        ],
        compiler_params=params(),
        cost_estimate=cost(a2.size * wide * count // seqs, x.size * count // (4 * seqs)),
        name="block_output",
    )(x, a2, wt, *packs, before)


def pack_sums_body(n_one, n_zero, n_out, *refs):
    refs, out_ref = list(refs[:-1]), refs[-1]
    bo, two, q_in, q_one, q_two = (refs.pop(0) for _ in range(5))
    one = sum(refs.pop(0)[0:3, :] for _ in range(n_one))
    zero = sum(refs.pop(0)[0:2, :] for _ in range(n_zero))
    out = sum(refs.pop(0)[0:2, :] for _ in range(n_out))
    inner = two.shape[1]
    out_ref[...] = jnp.zeros_like(out_ref)
    out_ref[0:2, :] = zero
    out_ref[2:3, :] = bo[0:1, :]
    out_ref[3:6, 0:inner] = one
    out_ref[3:6, inner : 2 * inner] = two[0:3, :]
    rows = (q_in[0:1, :], out[1:2, :], q_one[0:1, :], q_two[0:1, :], out[0:1, :])
    for j, row in enumerate(rows):
        total = jnp.sum(row, axis=1, keepdims=True)
        out_ref[6:7, j * 128 : (j + 1) * 128] = jnp.broadcast_to(total, (1, 128))


def pack_sums(bo, two, q_in, q_one, q_two, ones, zeros, outs):
    vmem = pl.BlockSpec(memory_space=pltpu.VMEM)
    args = (bo, two, q_in, q_one, q_two, *ones, *zeros, *outs)
    return pl.pallas_call(
        functools.partial(pack_sums_body, len(ones), len(zeros), len(outs)),
        in_specs=[vmem] * len(args),
        out_specs=vmem,
        out_shape=sds((8, bo.shape[1]), F32),
        compiler_params=params(16),
        name="pack_sums",
    )(*args)


def join_body(mine_ref, other_ref, mine_in, other_in, conv_ref, out_ref, in_ref):
    core = lax.rem(lax.axis_index("ctx"), 2)
    rows, inner = conv_ref.shape[1:]

    def halves(a, b, total):
        off, size = half_of(total)
        low = jnp.where(core == 0, a, b).astype(F32)
        high = jnp.where(core == 0, b, a).astype(F32)
        return size, low, high[size - off :]

    for k in range(5):
        size, low, high = halves(mine_ref[k], other_ref[k], rows)
        if k < 3:
            conv_ref[k, 0:size, :] = low
            conv_ref[k, size:rows, :] = high
        else:
            out_ref[0:size, (k - 3) * inner : (k - 2) * inner] = low
            out_ref[size:rows, (k - 3) * inner : (k - 2) * inner] = high
    size, low, high = halves(mine_in[...], other_in[...], in_ref.shape[0])
    in_ref[0:size, :] = low
    in_ref[size:, :] = high


def join_grads(rest, rows, of_in, rows_in):
    inner = of_in[0].shape[1]
    vmem = pl.BlockSpec(memory_space=pltpu.VMEM)
    return pl.pallas_call(
        join_body,
        in_specs=[vmem] * 4,
        out_specs=[vmem] * 3,
        out_shape=[
            sds((3, rows, inner), F32),
            sds((rows, 2 * inner), F32),
            sds((rows_in, inner), F32),
        ],
        compiler_params=params(32),
        name="join_grads",
    )(*rest, *of_in)


def unpack_body(counts, s_ref, *outs):
    me = lax.axis_index("dp")
    wide = s_ref.shape[1]
    inner = wide // 2

    def part(row, begin, size):
        v = s_ref[row : row + 1, begin : begin + size]
        for d in range(1, 4):
            at = begin + d * size
            v = jnp.where(me == d, s_ref[row : row + 1, at : at + size], v)
        return v.reshape(size)

    for j in range(3):
        outs[j][...] = part(j, 0, wide // 4)
    for j in range(6):
        outs[3 + j][...] = part(3 + j % 3, (j // 3) * inner, inner // 4)
    for j, count in enumerate(counts):
        outs[9 + j][...] = jnp.sqrt(s_ref[6:7, j * 128 : (j + 1) * 128] / count)


def unpack_sums(sums, counts):
    wide = sums.shape[1]
    vmem = pl.BlockSpec(memory_space=pltpu.VMEM)
    return pl.pallas_call(
        functools.partial(unpack_body, counts),
        in_specs=[vmem],
        out_specs=[vmem] * 14,
        out_shape=[sds((wide // 4,), F32)] * 3
        + [sds((wide // 8,), F32)] * 6
        + [sds((1, 128), F32)] * 5,
        compiler_params=params(16),
        name="unpack_sums",
    )(sums)


def local(
    stream, segments, cotangent, gain_zero, shift_zero, weight_in, bias_in, gain_one, shift_one,
    weight_conv, bias_conv, gain_two, shift_two, weight_out, bias_out,
):
    n_dp, n_ctx = lax.axis_size("dp"), lax.axis_size("ctx")
    assert n_dp == 4 and n_ctx & (n_ctx - 1) == 0
    me, place = lax.axis_index("dp"), lax.axis_index("ctx")
    seqs, length, wide = stream.shape
    inner = weight_conv.shape[2]
    part_w, part_i = gain_zero.shape[0], bias_in.shape[0]

    x = jnp.swapaxes(stream, 1, 2)
    dy = jnp.swapaxes(cotangent, 1, 2)

    half_in = prepare_in(
        weight_in,
        [gain_zero, shift_zero, bias_out, bias_in, gain_one, shift_one, bias_conv, gain_two, shift_two],
    )
    part_in = gather_halves(half_in)
    sent = next(part_in)
    rest_half = prepare_rest(after(weight_conv, sent), weight_out)
    sent = part_in.send(rest_half)
    stats, sq_in = input_stats(after(x, sent))
    came = part_in.send(sq_in)
    part_rest = gather_halves(after(rest_half, came))
    sent = next(part_rest)
    piece_in = (weight_in, *next(part_in))
    packs = (half_in, *piece_in[1:3])
    act_zero = first_act(x, after(stats, sent), packs)
    sent = part_rest.send(act_zero)

    padded = jnp.pad(segments, ((0, 0), (4, 4)), constant_values=-1)
    near_segs = lax.dynamic_slice_in_dim(padded, place * length, length + 8, 1)
    here = near_segs[:, 4 : 4 + length]
    same = [(near_segs[:, 4 + j : 4 + j + length] == here).astype(F32) for j in (0, -2, -4, 2, 4)]
    masks = jnp.stack(same + same[:3], axis=1)

    hidden_one, act_one, edge, sq_one, stats_one, full_in = first(
        act_zero, piece_in, (after(half_in, sent, masks), *packs[1:])
    )
    halo = shifted(edge, 1)
    part_rest.send(sq_one)
    full_conv, full_conv_t, full_out = assemble_weights(
        weight_conv, weight_out, next(part_rest)
    )
    act_two, d_hidden_two, edge_back, sums_two, sum_bo, sq_two, keep, send = conv(
        act_one, halo, dy, masks, full_conv_t, full_out, packs
    )
    halo_back = shifted(edge_back, -1)
    sum_rest = Stages(sum_shards(keep, send, True))
    own = after(half_in, sum_rest.value)
    full_out_t = transposed(after(full_out, edge_back))
    ones, zeros, outs = [], [], []
    output = grad_x = stats

    def run(what, begin, end):
        nonlocal output, grad_x
        vecs = (own, *packs[1:])
        if what == "out":
            output, sums = output_of(x, act_two, full_out_t, vecs, begin, end - begin, output)
            outs.append(sums)
        else:
            grad_x, sums = stream_back(
                x, stats, dy, d_hidden_one, full_in, vecs, begin, end - begin, grad_x
            )
            zeros.append(sums)
        return sums

    sums = run("out", 0, 1)
    own = after(own, sum_rest.step(sums))
    d_hidden_one, sums = conv_back(
        d_hidden_two, halo_back, hidden_one, stats_one, masks, full_conv, (own, *packs[1:])
    )
    ones.append(sums)
    own = after(own, sum_rest.step(sums))
    keep_in, send_in = grad(act_zero, after(d_hidden_one, own), "grad_weight_in")
    sum_in = Stages(sum_shards(keep_in, send_in, False))
    own = after(own, sum_in.value, sum_rest.step(send_in))
    sums = run("out", 1, 2)
    own = after(own, sum_in.step(sums))
    sums = run("stream", 0, 1)
    own = after(own, sum_in.step(sums), sum_rest.step(sums))
    sums = run("out", 2, seqs)
    own = after(own, sum_in.step(sums), sum_rest.step(sums))
    sums = run("stream", 1, 2)
    own = after(own, sum_in.step(sums), sum_rest.step(sums))
    sums = run("stream", 2, seqs)
    sum_rest.step(sums)
    sums = pack_sums(after(sum_bo, sum_in.step(sums)), sums_two, sq_in, sq_one, sq_two, ones, zeros, outs)
    count = float(seqs * length * n_dp * n_ctx)
    total = Stages(sum_all(sums))
    grad_weight_conv, grad_weight_out, grad_weight_in = join_grads(
        sum_rest.result(), part_i, sum_in.result(), part_w
    )
    total.step(None)
    total.step((grad_weight_out, grad_weight_in))
    sums = total.result()
    totals = unpack_sums(
        sums, (count * wide, count * wide, count * inner, count * inner, count * wide)
    )
    grad_gain_zero, grad_shift_zero, grad_bias_out = totals[0:3]
    grad_gain_one, grad_shift_one, grad_bias_in = totals[3:6]
    grad_gain_two, grad_shift_two, grad_bias_conv = totals[6:9]
    rms_in, rms_out, rms_hidden_one, rms_hidden_two, rms_branch = (v[0, 0] for v in totals[9:])
    return (
        jnp.swapaxes(output, 1, 2),
        jnp.swapaxes(grad_x, 1, 2),
        grad_gain_zero,
        grad_shift_zero,
        grad_weight_in,
        grad_bias_in,
        grad_gain_one,
        grad_shift_one,
        grad_weight_conv,
        grad_bias_conv,
        grad_gain_two,
        grad_shift_two,
        grad_weight_out,
        grad_bias_out,
        rms_in,
        rms_out,
        rms_hidden_one,
        rms_hidden_two,
        rms_branch,
    )


def solution(mesh):
    placed = (
        P("dp", "ctx", None),
        P("dp", None),
        P("dp", "ctx", None),
        P("dp"),
        P("dp"),
        P("dp", None),
        P("dp"),
        P("dp"),
        P("dp"),
        P(None, "dp", None),
        P("dp"),
        P("dp"),
        P("dp"),
        P("dp", None),
        P("dp"),
    )
    return jax.shard_map(
        local,
        mesh=mesh,
        in_specs=placed,
        out_specs=(
            P("dp", "ctx", None),
            P("dp", "ctx", None),
            P("dp"),
            P("dp"),
            P("dp", None),
            P("dp"),
            P("dp"),
            P("dp"),
            P(None, "dp", None),
            P("dp"),
            P("dp"),
            P("dp"),
            P("dp", None),
            P("dp"),
            P(),
            P(),
            P(),
            P(),
            P(),
        ),
        check_vma=False,
    )
```
